32 devices in a mesh: wide: 4 (over y, core), blk: 8 (over z, x).
Axes of the slice: x: 2, y: 2, z: 4, core: 2. Of those that a mesh axis runs over, the one named last changes fastest.
Arguments:
- flux_rows: float32 [32768, 1024], P(('wide', 'blk')), may hold values from -36 to 36
- row_signs: int32 [32768], P(('wide', 'blk')), may hold values from -1 to 1, as said below
- sample_rows: int32 [65536], P(('wide', 'blk')), may hold values from 0 to 1023
- sample_owner: int32 [65536, 1], P(('wide', 'blk')), may hold values from 0 to 7; in each aligned block of 2048 rows (0 to 2047, 2048 to 4095, ...) at most 640 rows name the same one
Outputs:
- transformed: bfloat16 [32768, 1024], P(('wide', 'blk'))
- sketch_factors: float32 [8192, 1024], P(('wide', 'blk'))
The draws below stay inside these ranges and needn't reach their ends.
Inputs may be any that keep to these rules, and one draw needn't show every extreme that they name: `row_signs`: every entry is -1 or 1. `sample_owner`: among the 2048 sampled rows of one device, no owner is named by more than 640 rows, a bound that some block reaches.
All inputs are finite; a program needn't handle non-finite values.
Results may differ from the reference program's by a relative error of at most 0.0058.
Values may be sent and summed in bfloat16 or wider, within the bound.
No kernel may reach another device: no remote copies, remote signals or barrier semaphores. Data moves between devices by JAX's collectives and lax.ppermute only.
A program may use at most 128 MiB of HBM per device.

```python
import math
import jax
import jax.numpy as jnp
import numpy as np
from jax import lax

D = 1024
PANEL = 256
HB = 128
ROWS_DEV = 1024
SEL_DEV = 2048
CAP = 640
ROWS = 32768
SAMPLES = 65536
OWNER_ROWS = 8192
N_WIDE = 4
N_BLK = 8


def draw_flux_rows(key, part):
    subkeys = jax.random.split(key, 3)
    row_total = N_WIDE * N_BLK * ROWS_DEV
    row_scale = jnp.exp(jax.random.uniform(subkeys[1], (row_total, 1), jnp.float32, math.log(0.3), math.log(3.0)))
    column_scale = jnp.exp(jax.random.uniform(subkeys[2], (1, D), jnp.float32, math.log(0.3), math.log(3.0)))
    base_values = jnp.clip(jax.random.normal(subkeys[0], (row_total, D), jnp.float32), -4.0, 4.0)
    return base_values * row_scale * column_scale


def draw_row_signs(key, part):
    row_total = N_WIDE * N_BLK * ROWS_DEV
    return (2 * jax.random.randint(key, (row_total,), 0, 2) - 1).astype(jnp.int32)


def touch_ends(array, stream_key, smallest, high):
    shape = array.shape
    place = [jax.random.randint(jax.random.fold_in(stream_key, axis), (), 0, shape[axis]) for axis in range(len(shape))]
    array = array.at[tuple(place)].set(smallest)
    longest = shape.index(max(shape))
    place[longest] = (place[longest] + 1) % shape[longest]
    return array.at[tuple(place)].set(high)


def shared_out(own_key, own, number, rows, count, top, limit, skew):
    ranking = jax.random.permutation(own_key, count)
    packed, ordinary = portions_of(count, rows * top, limit, skew, True), portions_of(count, rows * top, limit, skew, False)
    places = jnp.arange(count)

    def named(tallies, turn):
        used = int((tallies > 0).sum())
        fixed = max(1, used // 4)
        shifted = fixed + (places - fixed + turn * (used - fixed)) % max(1, count - fixed)
        return jnp.zeros((count,), jnp.int32).at[ranking[jnp.where(places < fixed, places, shifted)]].set(jnp.asarray(tallies, jnp.int32))

    tallies = jnp.where(number % 4 == 0, named(packed, number // 4), named(ordinary, number - number // 4 - 1))
    mixed = jax.random.permutation(jax.random.fold_in(own, 3), count)
    giver, sink = mixed[0:count // 2 * 2:2], mixed[1:count // 2 * 2:2]
    slack = jnp.minimum(tallies[giver] - 1, limit - tallies[sink]) // 2
    slack = jnp.where((giver == ranking[0]) | (sink == ranking[0]) | (tallies[sink] == 0), 0, jnp.maximum(slack, 0))
    shifted = jax.random.randint(jax.random.fold_in(own, 4), (count // 2,), 0, 1 << 20) % (slack + 1)
    tallies = tallies.at[giver].add(-shifted).at[sink].add(shifted)
    items = jnp.searchsorted(jnp.cumsum(tallies), jnp.arange(rows * top), side="right").astype(jnp.int32)
    grid = items.reshape(top, rows).T
    grid = grid[jax.random.permutation(jax.random.fold_in(own, 1), rows)]
    turn = jax.random.randint(jax.random.fold_in(own, 2), (rows, 1), 0, top)
    return jnp.take_along_axis(grid, (jnp.arange(top)[None, :] + turn) % top, axis=1)


def portions_of(count, total, bound, lean, full):
    portions = [(1 << 20) // math.isqrt(grade ** lean) + 1 for grade in range(1, count + 1)]
    largest = bound if full else min(bound, max(-(-total // count), total * portions[0] // sum(portions)))
    least = 1 if total - largest >= count - 1 else 0
    given, surplus = [largest] + [least] * (count - 1), total - largest - least * (count - 1)
    while surplus > 0:
        free = [i for i in range(1, count) if given[i] < largest] or [i for i in range(1, count) if given[i] < bound]
        mass, left = sum([portions[i] for i in free]), surplus
        for i in free:
            more = min(bound - given[i], max(1, left * portions[i] // mass), surplus)
            given[i] = given[i] + more
            surplus = surplus - more
    return np.array(given)


def setup_inputs(seed: int = 0) -> dict:
    key_list = jax.random.split(jax.random.key(seed), 5)
    flux_rows = draw_flux_rows(jax.random.fold_in(key_list[4], 71), 0)
    row_signs = draw_row_signs(jax.random.fold_in(key_list[4], 71), 0)
    sample_rows = touch_ends(jax.random.randint(key_list[2], (SAMPLES,), 0, ROWS_DEV), jax.random.fold_in(key_list[2], 1), 0, ROWS_DEV - 1).astype(jnp.int32)
    sample_owner_keys = jax.random.split(jax.random.fold_in(key_list[3], 1), SAMPLES // SEL_DEV)
    sample_owner_turns = jax.random.permutation(jax.random.fold_in(key_list[3], 3), SAMPLES // SEL_DEV)
    sample_owner = jax.vmap(lambda own, number: shared_out(jax.random.fold_in(key_list[3], 2), own, number, SEL_DEV, N_BLK, 1, CAP, 1))(sample_owner_keys, sample_owner_turns).reshape((SAMPLES, 1))
    return dict(flux_rows=flux_rows, row_signs=row_signs, sample_rows=sample_rows, sample_owner=sample_owner)


SQRT_HALF = 0.7071067811865476

def sylvester(length):
    indices = jnp.arange(length, dtype=jnp.int32)
    common = jnp.bitwise_and(indices[:, None], indices[None, :])
    parity = jnp.zeros((length, length), jnp.int32)
    for section_index in range(length.bit_length() - 1):
        parity = parity + jnp.bitwise_and(jnp.right_shift(common, section_index), 1)
    return (1 - 2 * jnp.bitwise_and(parity, 1)).astype(jnp.float32) * length ** (-0.5)

def block_mix(flux_rows, row_signs, length):
    row_total, columns = flux_rows.shape
    signed = flux_rows * row_signs.astype(jnp.float32)[:, None]
    blocks = signed.reshape(row_total // length, length, columns)
    mixed = jnp.einsum('ij,bjd->bid', sylvester(length), blocks, precision=lax.Precision.HIGHEST)
    return mixed.reshape(row_total, columns).astype(jnp.bfloat16)

def column_sections(pieces):
    members = pieces.shape[0]
    for section_index in range(members.bit_length() - 1):
        stride = 2 ** section_index
        grouped = pieces.reshape(members // (2 * stride), 2, stride, pieces.shape[1], pieces.shape[2]).astype(jnp.float32)
        low_part = grouped[:, 0]
        high_part = grouped[:, 1]
        joined = jnp.stack([(low_part + high_part) * SQRT_HALF, (low_part - high_part) * SQRT_HALF], axis=1)
        pieces = joined.astype(jnp.bfloat16).reshape(pieces.shape)
    return pieces

def make_bucket(block_rows, indices, owner_column, owners, capacity):
    picked = jnp.take(block_rows, indices, axis=0)
    owner_ids = owner_column[:, 0]
    onehot = (owner_ids[:, None] == jnp.arange(owners, dtype=jnp.int32)[None, :]).astype(jnp.int32)
    before = jnp.cumsum(onehot, axis=0) - onehot
    position = jnp.sum(before * onehot, axis=1)
    slot_index = (owner_ids * capacity + position).astype(jnp.int32)
    bucket = jnp.zeros((owners * capacity, block_rows.shape[1]), block_rows.dtype)
    return bucket.at[slot_index].set(picked)

def factor_panel(gram_block):
    lead = gram_block[:, :PANEL] + 0.5 * jnp.eye(PANEL, dtype=gram_block.dtype)
    lower_factor = jnp.linalg.cholesky(lead)
    coupling = lax.linalg.triangular_solve(lower_factor, gram_block[:, PANEL:], left_side=True, lower=True)
    return jnp.concatenate([lower_factor.T, coupling], axis=1)

def reference(flux_rows, row_signs, sample_rows, sample_owner):
    mixed = block_mix(flux_rows, row_signs, HB)
    groups = column_sections(mixed.reshape(N_WIDE, N_BLK * ROWS_DEV, D))
    transformed = groups.reshape(ROWS, D)
    per_device = transformed.reshape(N_WIDE, N_BLK, ROWS_DEV, D)
    row_lists = sample_rows.reshape(N_WIDE, N_BLK, SEL_DEV)
    owner_lists = sample_owner.reshape(N_WIDE, N_BLK, SEL_DEV, 1)

    def group_factors(operands):
        blocks, indices, owner_column = operands
        buckets = jax.vmap(lambda rows_in, picks, owned: make_bucket(rows_in, picks, owned, N_BLK, CAP))(blocks, indices, owner_column)
        buckets = buckets.reshape(N_BLK, N_BLK, CAP, D)

        def owner_factor(owner_index):
            stacked = buckets[:, owner_index].reshape(N_BLK * CAP, D).astype(jnp.float32)
            gram_block = jnp.einsum('rp,rd->pd', stacked[:, :PANEL], stacked, precision=lax.Precision.HIGHEST)
            return factor_panel(gram_block / SEL_DEV)
        return lax.map(owner_factor, jnp.arange(N_BLK, dtype=jnp.int32))
    factors = lax.map(group_factors, (per_device, row_lists, owner_lists))
    return (transformed, factors.reshape(OWNER_ROWS, D))
```

```python
import functools

import jax
import jax.numpy as jnp
import numpy as np
from jax import lax
from jax.experimental import pallas as pl
from jax.experimental.pallas import tpu as pltpu
from jax.sharding import PartitionSpec as P

PANEL = 256
HB = 128
NZ = 4
CHUNKS = ((0, 256), (256, 256), (512, 256), (768, 256))
SQRT_HALF = 0.7071067811865476
HIGHEST = lax.Precision.HIGHEST
F32 = jnp.float32
BF16 = jnp.bfloat16


def hadamard_pair():
    idx = np.arange(HB)
    common = idx[:, None] & idx[None, :]
    parity = np.zeros_like(common)
    for bit in range(HB.bit_length() - 1):
        parity ^= (common >> bit) & 1
    one = 1.0 - 2.0 * parity
    return jnp.asarray(np.kron(np.eye(2), one), BF16)


def mix_kernel(signs_ref, had_ref, x_ref, out_ref):
    rows, cols = x_ref.shape
    size = had_ref.shape[0]
    for b in range(rows // size):
        part = pl.ds(b * size, size)
        signed = (had_ref[...].astype(F32) * signs_ref[b : b + 1, :].astype(F32)).astype(BF16)
        x = x_ref[part, :]
        hi = x.astype(BF16)
        rest = x - hi.astype(F32)
        mid = rest.astype(BF16)
        low = (rest - mid.astype(F32)).astype(BF16)
        total = jnp.dot(signed, low, preferred_element_type=F32)
        total = total + jnp.dot(signed, mid, preferred_element_type=F32)
        total = total + jnp.dot(signed, hi, preferred_element_type=F32)
        out_ref[part, :] = (total * (HB**-0.5)).astype(BF16)


def mix_chunk(signs, had, flux, start, width):
    rows = flux.shape[0]
    block = start // width
    return pl.pallas_call(
        mix_kernel,
        grid=(1,),
        in_specs=[
            pl.BlockSpec(signs.shape, lambda i: (0, 0)),
            pl.BlockSpec(had.shape, lambda i: (0, 0)),
            pl.BlockSpec((rows, width), lambda i: (0, block)),
        ],
        out_specs=pl.BlockSpec((rows, width), lambda i: (0, 0)),
        out_shape=jax.ShapeDtypeStruct((rows, width), BF16),
        cost_estimate=pl.CostEstimate(flops=2 * rows * width * 256 * 3, bytes_accessed=rows * width * 6, transcendentals=0),
        name="mix",
    )(signs, had, flux)


def count_kernel(rows_ref, owner_ref, out_ref):
    owners, rows = out_ref.shape
    listed = rows_ref.shape[1]
    by_row = (lax.broadcasted_iota(jnp.int32, (rows, listed), 0) == rows_ref[...]).astype(F32).astype(BF16)
    by_owner = (lax.broadcasted_iota(jnp.int32, (owners, listed), 0) == owner_ref[...]).astype(F32).astype(BF16)
    out_ref[...] = lax.dot_general(by_owner, by_row, (((1,), (1,)), ((), ())), preferred_element_type=F32)


def count_samples(sample_rows, sample_owner, owners, rows):
    listed = sample_rows.shape[0]
    return pl.pallas_call(
        count_kernel,
        out_shape=jax.ShapeDtypeStruct((owners, rows), F32),
        cost_estimate=pl.CostEstimate(flops=2 * rows * listed * owners, bytes_accessed=rows * owners * 4, transcendentals=0),
        name="counts",
    )(sample_rows.reshape(1, listed), sample_owner.reshape(1, listed))


def weigh_kernel(counts_ref, lead_ref, hi_ref, lo_ref):
    lead = lead_ref[...].astype(F32).T
    for q in range(NZ):
        weighed = lead * counts_ref[q : q + 1, :]
        hi = weighed.astype(BF16)
        hi_ref[q] = hi
        lo_ref[q] = (weighed - hi.astype(F32)).astype(BF16)


def weigh(counts, lead):
    rows = lead.shape[0]
    tile = 256
    out = pl.BlockSpec((NZ, PANEL, tile), lambda i: (0, 0, i))
    shape = jax.ShapeDtypeStruct((NZ, PANEL, rows), BF16)
    return pl.pallas_call(
        weigh_kernel,
        grid=(rows // tile,),
        in_specs=[pl.BlockSpec((NZ, tile), lambda i: (0, i)), pl.BlockSpec((tile, PANEL), lambda i: (i, 0))],
        out_specs=(out, out),
        out_shape=(shape, shape),
        cost_estimate=pl.CostEstimate(flops=rows * PANEL * 16, bytes_accessed=rows * PANEL * 18, transcendentals=0),
        name="weigh",
    )(counts, lead)


def gram_kernel(parts, packed, *refs):
    out_ref = refs[-1]
    total = None
    for p in range(parts):
        hi_ref, lo_ref, rows_ref = refs[3 * p : 3 * p + 3]
        rows = rows_ref[...]
        for ref in (lo_ref, hi_ref):
            term = jnp.dot(ref[0], rows, preferred_element_type=F32)
            total = term if total is None else total + term
    if packed:
        half = PANEL // 2
        out_ref[0, :PANEL, :] = total[:, :half]
        out_ref[0, PANEL:, :] = total[half:, half:]
    else:
        out_ref[0] = total


def partial_grams(weights, chunk_rows, packed):
    parts = len(chunk_rows)
    rows, width = chunk_rows[0].shape
    shape = (NZ, PANEL + PANEL // 2, PANEL // 2) if packed else (NZ, PANEL, width)
    operands, specs = [], []
    for (hi, lo), block in zip(weights, chunk_rows):
        operands += [hi, lo, block]
        weight_spec = pl.BlockSpec((1, PANEL, rows), lambda q: (q, 0, 0))
        specs += [weight_spec, weight_spec, pl.BlockSpec((rows, width), lambda q: (0, 0))]
    return pl.pallas_call(
        functools.partial(gram_kernel, parts, packed),
        grid=(NZ,),
        in_specs=specs,
        out_specs=pl.BlockSpec((1,) + shape[1:], lambda q: (q, 0, 0)),
        out_shape=jax.ShapeDtypeStruct(shape, F32),
        cost_estimate=pl.CostEstimate(
            flops=4 * parts * NZ * PANEL * rows * width,
            bytes_accessed=4 * parts * NZ * PANEL * rows + 2 * parts * rows * width,
            transcendentals=0,
        ),
        name="grams",
    )(*operands)


BAND = 32


def factor_kernel(scale, lead_ref, upper_ref, inverse_ref, work):
    half = PANEL // 2
    ri = lax.broadcasted_iota(jnp.int32, (PANEL, PANEL), 0)
    ci = lax.broadcasted_iota(jnp.int32, (PANEL, PANEL), 1)
    eye = (ri == ci).astype(F32)
    work[:, PANEL:] = eye
    work[:half, :half] = lead_ref[:half, :] * scale + 0.5 * eye[:half, :half]
    work[:half, half:PANEL] = (lead_ref[half:PANEL, :] * scale).T
    work[half:, :half] = lead_ref[half:PANEL, :] * scale
    work[half:, half:PANEL] = lead_ref[PANEL:, :] * scale + 0.5 * eye[:half, :half]
    rb = lax.broadcasted_iota(jnp.int32, (BAND, BAND), 0)
    cb = lax.broadcasted_iota(jnp.int32, (BAND, BAND), 1)
    eye_b = (rb == cb).astype(F32)
    row_id = lax.broadcasted_iota(jnp.int32, (BAND, 1), 0)
    for k in range(PANEL // BAND):
        lo, hi = k * BAND, (k + 1) * BAND
        diag = work[lo:hi, lo:hi]
        tile = jnp.concatenate([diag, eye_b], axis=1)
        for j in range(BAND):
            pivot = tile[j : j + 1, j : j + 1]
            r = lax.rsqrt(pivot)
            r = r * (1.5 - 0.5 * pivot * r * r)
            row = tile[j : j + 1, :] * r
            column = tile[:, j : j + 1] * r
            tile = jnp.where(row_id == j, row, jnp.where(row_id > j, tile - column * row, tile))
        inv = tile[:, BAND:]
        inv = jnp.where(rb >= cb, inv, 0.0)
        full = jnp.dot(inv, work[lo:hi, lo:], precision=HIGHEST, preferred_element_type=F32)
        if hi < PANEL:
            panel = full[:, BAND : PANEL - lo]
            work[hi:, hi:] = work[hi:, hi:] - lax.dot_general(
                panel, full[:, BAND:], (((0,), (0,)), ((), ())), precision=HIGHEST, preferred_element_type=F32
            )
        work[lo:hi, lo:] = full
    upper_ref[...] = jnp.where(ci >= ri, work[:, :PANEL], 0.0)
    inverse_ref[...] = jnp.where(ri >= ci, work[:, PANEL:], 0.0)


def factor(lead, scale):
    shape = jax.ShapeDtypeStruct((PANEL, PANEL), F32)
    return pl.pallas_call(
        functools.partial(factor_kernel, scale),
        out_shape=(shape, shape),
        scratch_shapes=[pltpu.VMEM((PANEL, 2 * PANEL), F32)],
        cost_estimate=pl.CostEstimate(flops=200_000_000, bytes_accessed=1 << 20, transcendentals=0),
        name="factor",
    )(lead)


def swap_pairs(count, bit):
    return [(i, i ^ bit) for i in range(count)]


def butterfly(own, other, sign):
    total = (other.astype(F32) + own.astype(F32) * sign) * SQRT_HALF
    return total.astype(BF16)


def per_device(flux_rows, row_signs, sample_rows, sample_owner):
    wide, blk = lax.axis_size("wide"), lax.axis_size("blk")
    nx = blk // NZ
    rows = flux_rows.shape[0]
    scale = 1.0 / sample_rows.shape[0]
    me_w, me_b = lax.axis_index("wide"), lax.axis_index("blk")
    me_x, me_z = me_b % nx, me_b // nx
    near = me_z < NZ // 2
    outer = jnp.logical_or(me_z == 0, me_z == NZ - 1)
    had = hadamard_pair()
    signs = row_signs.reshape(rows // (2 * HB), 2 * HB)

    def at(z, x):
        return z * nx + x

    def z_route(pairs):
        return [(at(a, x), at(b, x)) for a, b in pairs for x in range(nx)]

    def x_shift(s):
        return [(at(z, x), at(z, (x + s) % nx)) for z in range(NZ) for x in range(nx)]

    counts = count_samples(sample_rows, sample_owner, blk, rows).reshape(NZ, nx, rows)

    def counts_for(x):
        return lax.dynamic_index_in_dim(counts, x, axis=1, keepdims=False)

    owner_counts = [counts_for(me_x)]
    for s in range(1, nx):
        owner_counts.append(lax.ppermute(counts_for((me_x + s) % nx), "blk", x_shift(s)))
    owner_counts = [jnp.where(near, c, c[::-1]) for c in owner_counts]

    weights = None
    pieces, grams = [], []
    for index, (start, width) in enumerate(CHUNKS):
        current = mix_chunk(signs, had, flux_rows, start, width)
        for level in range(wide.bit_length() - 1):
            partner = lax.ppermute(current, "wide", swap_pairs(wide, 1 << level))
            sign = jnp.where((me_w >> level) & 1 == 1, -1.0, 1.0).astype(F32)
            current = butterfly(current, partner, sign)
        pieces.append(current)
        sources = [current] + [lax.ppermute(current, "blk", x_shift(s)) for s in range(1, nx)]
        packed = index == 0
        if packed:
            weights = [weigh(c, lead) for c, lead in zip(owner_counts, sources)]
        part = partial_grams(weights, sources, packed)
        from_outer = lax.ppermute(part[1:], "blk", z_route(((0, 1), (3, 2))))
        to_outer = lax.ppermute(part[0], "blk", z_route(((1, 0), (2, 3))))
        to_inner = lax.ppermute(part[2] + from_outer[1], "blk", z_route(((1, 2), (2, 1))))
        to_far = lax.ppermute(part[3] + from_outer[2], "blk", z_route(((1, 3), (2, 0))))
        kept = jnp.where(outer, part[0], part[1] + from_outer[0])
        grams.append(kept + to_outer + to_inner + to_far)

    upper, inverse = factor(grams[0], scale)
    coupled = [
        jnp.dot(inverse, g * scale, precision=HIGHEST, preferred_element_type=F32) for g in grams[1:]
    ]
    return jnp.concatenate(pieces, axis=1), jnp.concatenate([upper] + coupled, axis=1)


def solution(mesh):
    placed = (
        P(("wide", "blk"), None),
        P(("wide", "blk")),
        P(("wide", "blk")),
        P(("wide", "blk"), None),
    )
    return jax.shard_map(
        per_device,
        mesh=mesh,
        in_specs=placed,
        out_specs=(P(("wide", "blk"), None), P(("wide", "blk"), None)),
        check_vma=False,
    )
```

```python
import functools

import jax
import jax.numpy as jnp
import numpy as np
from jax import lax
from jax.experimental import pallas as pl
from jax.experimental.pallas import tpu as pltpu
from jax.sharding import PartitionSpec as P

PANEL = 256
HB = 128
NZ = 4
CHUNKS = ((0, 256), (256, 256), (512, 256), (768, 256))
SQRT_HALF = 0.7071067811865476
HIGHEST = lax.Precision.HIGHEST
F32 = jnp.float32
BF16 = jnp.bfloat16


def hadamard_pair():
    idx = np.arange(HB)
    common = idx[:, None] & idx[None, :]
    parity = np.zeros_like(common)
    for bit in range(HB.bit_length() - 1):
        parity ^= (common >> bit) & 1
    one = 1.0 - 2.0 * parity
    return jnp.asarray(np.kron(np.eye(2), one), BF16)


VMEM_LIMIT = 24 << 20


def params(**kw):
    return pltpu.CompilerParams(vmem_limit_bytes=VMEM_LIMIT, **kw)


def cost(flops, moved):
    return pl.CostEstimate(flops=flops, bytes_accessed=moved, transcendentals=0)


def mix_kernel(signs_ref, had_ref, x_ref, out_ref):
    signed = (had_ref[...].astype(F32) * signs_ref[...].astype(F32)).astype(BF16)
    x = x_ref[...]
    hi = x.astype(BF16)
    rest = x - hi.astype(F32)
    mid = rest.astype(BF16)
    low = (rest - mid.astype(F32)).astype(BF16)
    total = jnp.dot(signed, low, preferred_element_type=F32)
    total = total + jnp.dot(signed, mid, preferred_element_type=F32)
    total = total + jnp.dot(signed, hi, preferred_element_type=F32)
    out_ref[...] = (total * (HB**-0.5)).astype(BF16)


def mix_chunk(signs, had, flux, start, width):
    rows = flux.shape[0]
    size = had.shape[0]
    block = start // width
    return pl.pallas_call(
        mix_kernel,
        grid=(rows // size,),
        in_specs=[
            pl.BlockSpec((1, size), lambda i: (0, i)),
            pl.BlockSpec(had.shape, lambda i: (0, 0)),
            pl.BlockSpec((size, width), lambda i: (i, block)),
        ],
        out_specs=pl.BlockSpec((size, width), lambda i: (i, 0)),
        out_shape=jax.ShapeDtypeStruct((rows, width), BF16),
        cost_estimate=cost(2 * rows * width * size * 3, rows * width * 6),
        name="mix",
    )(signs, had, flux)


def join_kernel(sign_ref, own_ref, other_ref, *refs):
    total = (other_ref[...].astype(F32) + own_ref[...].astype(F32) * sign_ref[0]) * SQRT_HALF
    total = total.astype(BF16)
    for ref in refs[-2:]:
        ref[...] = total


def join_last(own, other, sign, start, columns, whole):
    rows, width = own.shape
    block = start // width
    tile = rows // 2
    chunk = pl.BlockSpec((tile, width), lambda i: (i, 0))
    operands, specs, alias = [sign.reshape(1), own, other], [pl.BlockSpec(memory_space=pltpu.SMEM), chunk, chunk], {}
    if whole is not None:
        operands.append(whole)
        specs.append(pl.BlockSpec(memory_space=pl.ANY))
        alias = {3: 1}
    return pl.pallas_call(
        join_kernel,
        grid=(rows // tile,),
        in_specs=specs,
        out_specs=(chunk, pl.BlockSpec((tile, width), lambda i: (i, block))),
        out_shape=(jax.ShapeDtypeStruct((rows, width), BF16), jax.ShapeDtypeStruct((rows, columns), BF16)),
        input_output_aliases=alias,
        compiler_params=params(),
        cost_estimate=cost(4 * rows * width, 8 * rows * width),
        name="join",
    )(*operands)


def relative_owner(q):
    return ((q & 1) << 1) | (q >> 1)


def count_kernel(nx, me_ref, rows_ref, owner_ref, *out_refs):
    listed = rows_ref.shape[1]
    rows = out_refs[0].shape[1]
    me_z, me_x = me_ref[0], me_ref[1]
    index = lax.broadcasted_iota(jnp.int32, (NZ * nx, listed), 0)
    q, s = index & (NZ - 1), index >> (NZ.bit_length() - 1)
    z = me_z ^ relative_owner(q)
    x = (me_x + s) & (nx - 1)
    by_owner = (z * nx + x == owner_ref[...]).astype(F32).astype(BF16)
    by_row = (lax.broadcasted_iota(jnp.int32, (rows, listed), 0) == rows_ref[...]).astype(F32).astype(BF16)
    total = lax.dot_general(by_owner, by_row, (((1,), (1,)), ((), ())), preferred_element_type=F32)
    for shift, ref in enumerate(out_refs):
        ref[...] = total[shift * NZ : (shift + 1) * NZ, :]


def count_samples(sample_rows, sample_owner, nx, rows, me_z, me_x):
    listed = sample_rows.shape[0]
    shape = jax.ShapeDtypeStruct((NZ, rows), F32)
    vmem = pl.BlockSpec(memory_space=pltpu.VMEM)
    return pl.pallas_call(
        functools.partial(count_kernel, nx),
        in_specs=[pl.BlockSpec(memory_space=pltpu.SMEM), vmem, vmem],
        out_shape=(shape,) * nx,
        compiler_params=params(),
        cost_estimate=cost(2 * rows * listed * NZ * nx, rows * NZ * nx * 4),
        name="counts",
    )(jnp.stack([me_z, me_x]), sample_rows.reshape(1, listed), sample_owner.reshape(1, listed))


def weigh_kernel(counts_ref, lead_ref, hi_ref, lo_ref):
    lead = lead_ref[...].astype(F32).T
    for q in range(NZ):
        part = pl.ds(q * PANEL, PANEL)
        weighed = lead * counts_ref[q : q + 1, :]
        hi = weighed.astype(BF16)
        hi_ref[part, :] = hi
        lo_ref[part, :] = (weighed - hi.astype(F32)).astype(BF16)


def weigh(counts, lead):
    rows = lead.shape[0]
    tile = rows // 2
    out = pl.BlockSpec((NZ * PANEL, tile), lambda i: (0, i))
    shape = jax.ShapeDtypeStruct((NZ * PANEL, rows), BF16)
    return pl.pallas_call(
        weigh_kernel,
        grid=(rows // tile,),
        in_specs=[pl.BlockSpec((NZ, tile), lambda i: (0, i)), pl.BlockSpec((tile, PANEL), lambda i: (i, 0))],
        out_specs=(out, out),
        out_shape=(shape, shape),
        compiler_params=params(),
        cost_estimate=cost(rows * PANEL * 16, rows * PANEL * 18),
        name="weigh",
    )(counts, lead)


GRAM_TILES = 2


def gram_kernel(parts, packed, *refs):
    keep_ref, send_ref, acc = refs[-3:]
    step = pl.program_id(0)

    @pl.when(step == 0)
    def _():
        acc[...] = jnp.zeros_like(acc)

    for p in range(parts):
        hi_ref, lo_ref, rows_ref = refs[3 * p : 3 * p + 3]

        @pl.when(step // GRAM_TILES == p)
        def _(hi_ref=hi_ref, lo_ref=lo_ref, rows_ref=rows_ref):
            rows = rows_ref[...]
            low = jnp.dot(lo_ref[...], rows, preferred_element_type=F32)
            acc[...] += low + jnp.dot(hi_ref[...], rows, preferred_element_type=F32)

    @pl.when(step == parts * GRAM_TILES - 1)
    def _():
        half = PANEL // 2
        for q in range(NZ):
            ref, place = (keep_ref, q) if q < NZ // 2 else (send_ref, q - NZ // 2)
            base = q * PANEL
            if packed:
                to = place * 3 * half
                ref[to : to + PANEL, :] = acc[base : base + PANEL, :half]
                ref[to + PANEL : to + 3 * half, :] = acc[base + half : base + PANEL, half:]
            else:
                ref[place * PANEL : (place + 1) * PANEL, :] = acc[base : base + PANEL, :]


def partial_grams(weights, chunk_rows, packed):
    parts = len(chunk_rows)
    rows, width = chunk_rows[0].shape
    tile = rows // GRAM_TILES
    half = NZ // 2
    shape = (half * (PANEL + PANEL // 2), PANEL // 2) if packed else (half * PANEL, width)
    operands, specs = [], []
    for p, ((hi, lo), block) in enumerate(zip(weights, chunk_rows)):
        operands += [hi, lo, block]

        def place(k, p=p):
            return jnp.clip(k - p * GRAM_TILES, 0, GRAM_TILES - 1)

        weight_spec = pl.BlockSpec((NZ * PANEL, tile), lambda k, place=place: (0, place(k)))
        specs += [weight_spec, weight_spec, pl.BlockSpec((tile, width), lambda k, place=place: (place(k), 0))]
    out = pl.BlockSpec(shape, lambda k: (0, 0))
    out_shape = jax.ShapeDtypeStruct(shape, F32)
    return pl.pallas_call(
        functools.partial(gram_kernel, parts, packed),
        grid=(parts * GRAM_TILES,),
        in_specs=specs,
        out_specs=(out, out),
        out_shape=(out_shape, out_shape),
        scratch_shapes=[pltpu.VMEM((NZ * PANEL, width), F32)],
        compiler_params=params(),
        cost_estimate=cost(4 * parts * NZ * PANEL * rows * width, 4 * parts * NZ * PANEL * rows + 2 * parts * rows * width),
        name="grams",
    )(*operands)


def add_kernel(keep_ref, near_ref, out_ref):
    out_ref[...] = keep_ref[...] + near_ref[...]


def far_sum(keep, near):
    rows, width = keep.shape[0] // 2, keep.shape[1]
    spec = pl.BlockSpec((rows, width), lambda i: (1, 0))
    return pl.pallas_call(
        add_kernel,
        grid=(1,),
        in_specs=[spec, spec],
        out_specs=pl.BlockSpec((rows, width), lambda i: (0, 0)),
        out_shape=jax.ShapeDtypeStruct((rows, width), F32),
        compiler_params=params(),
        cost_estimate=cost(rows * width, 12 * rows * width),
        name="add",
    )(keep, near)


BAND = 32
CUT = 4


def eliminate(work, first, last):
    rb = lax.broadcasted_iota(jnp.int32, (BAND, BAND), 0)
    cb = lax.broadcasted_iota(jnp.int32, (BAND, BAND), 1)
    eye_b = (rb == cb).astype(F32)
    row_id = lax.broadcasted_iota(jnp.int32, (BAND, 1), 0)
    for k in range(first, last):
        lo, hi = k * BAND, (k + 1) * BAND
        tile = jnp.concatenate([work[lo:hi, lo:hi], eye_b], axis=1)
        for j in range(BAND):
            pivot = tile[j : j + 1, j : j + 1]
            r = lax.rsqrt(pivot)
            r = r * (1.5 - 0.5 * pivot * r * r)
            row = tile[j : j + 1, :] * r
            column = tile[:, j : j + 1] * r
            tile = jnp.where(row_id == j, row, jnp.where(row_id > j, tile - column * row, tile))
        inv = jnp.where(rb >= cb, tile[:, BAND:], 0.0)
        full = jnp.dot(inv, work[lo:hi, lo:], precision=HIGHEST, preferred_element_type=F32)
        if hi < PANEL:
            panel = full[:, BAND : PANEL - lo]
            work[hi:, hi:] = work[hi:, hi:] - lax.dot_general(
                panel, full[:, BAND:], (((0,), (0,)), ((), ())), precision=HIGHEST, preferred_element_type=F32
            )
        work[lo:hi, lo:] = full


def factor_first_kernel(scale, keep_ref, near_ref, far_ref, out_ref, work):
    half = PANEL // 2
    lead = (keep_ref[...] + near_ref[...] + far_ref[...]) * scale
    ri = lax.broadcasted_iota(jnp.int32, (PANEL, PANEL), 0)
    ci = lax.broadcasted_iota(jnp.int32, (PANEL, PANEL), 1)
    eye = (ri == ci).astype(F32)
    work[:, PANEL:] = eye
    work[:half, :half] = lead[:half, :] + 0.5 * eye[:half, :half]
    work[:half, half:PANEL] = lead[half:PANEL, :].T
    work[half:, :half] = lead[half:PANEL, :]
    work[half:, half:PANEL] = lead[PANEL:, :] + 0.5 * eye[:half, :half]
    eliminate(work, 0, CUT)
    out_ref[...] = work[...]


def factor_last_kernel(in_ref, out_ref, inverse_ref, work):
    work[...] = in_ref[...]
    eliminate(work, CUT, PANEL // BAND)
    ri = lax.broadcasted_iota(jnp.int32, (PANEL, PANEL), 0)
    ci = lax.broadcasted_iota(jnp.int32, (PANEL, PANEL), 1)
    out_ref[...] = jnp.where(ci >= ri, work[:, :PANEL], 0.0)
    inverse_ref[...] = jnp.where(ri >= ci, work[:, PANEL:], 0.0)


def factor_first(keep, near, far, scale):
    spec = pl.BlockSpec(far.shape, lambda i: (0, 0))
    shape = (PANEL, 2 * PANEL)
    return pl.pallas_call(
        functools.partial(factor_first_kernel, scale),
        grid=(1,),
        in_specs=[spec, spec, spec],
        out_specs=pl.BlockSpec(shape, lambda i: (0, 0)),
        out_shape=jax.ShapeDtypeStruct(shape, F32),
        scratch_shapes=[pltpu.VMEM(shape, F32)],
        compiler_params=params(),
        cost_estimate=cost(10_000_000_000, 1 << 20),
        name="factor_first",
    )(keep, near, far)


def factor_last(state, columns):
    square = pl.BlockSpec((PANEL, PANEL), lambda i: (0, 0))
    return pl.pallas_call(
        factor_last_kernel,
        grid=(1,),
        in_specs=[pl.BlockSpec(state.shape, lambda i: (0, 0))],
        out_specs=(square, square),
        out_shape=(jax.ShapeDtypeStruct((PANEL, columns), F32), jax.ShapeDtypeStruct((PANEL, PANEL), F32)),
        scratch_shapes=[pltpu.VMEM(state.shape, F32)],
        compiler_params=params(),
        cost_estimate=cost(10_000_000_000, 1 << 20),
        name="factor_last",
    )(state)


def couple_kernel(scale, inverse_ref, keep_ref, near_ref, far_ref, whole_ref, out_ref):
    gram = (keep_ref[...] + near_ref[...] + far_ref[...]) * scale
    out_ref[...] = jnp.dot(inverse_ref[...], gram, precision=HIGHEST, preferred_element_type=F32)


def couple(inverse, keep, near, far, whole, start, scale):
    rows, width = far.shape
    block = start // width
    spec = pl.BlockSpec((rows, width), lambda i: (0, 0))
    return pl.pallas_call(
        functools.partial(couple_kernel, scale),
        grid=(1,),
        in_specs=[pl.BlockSpec(inverse.shape, lambda i: (0, 0)), spec, spec, spec, pl.BlockSpec(memory_space=pl.ANY)],
        out_specs=pl.BlockSpec((rows, width), lambda i: (0, block)),
        out_shape=jax.ShapeDtypeStruct(whole.shape, F32),
        input_output_aliases={4: 0},
        compiler_params=params(),
        cost_estimate=cost(12 * PANEL * rows * width, 20 * rows * width),
        name="couple",
    )(inverse, keep, near, far, whole)


def per_device(flux_rows, row_signs, sample_rows, sample_owner):
    wide, blk = lax.axis_size("wide"), lax.axis_size("blk")
    nx = blk // NZ
    rows, columns = flux_rows.shape
    scale = 1.0 / sample_rows.shape[0]
    me_w, me_b = lax.axis_index("wide"), lax.axis_index("blk")
    me_x, me_z = me_b & (nx - 1), me_b >> (nx.bit_length() - 1)
    had = hadamard_pair()
    signs = row_signs.reshape(1, rows)
    levels = wide.bit_length() - 1

    def at(z, x):
        return z * nx + x

    def z_route(mask):
        return [(at(z, x), at(z ^ mask, x)) for z in range(NZ) for x in range(nx)]

    def x_shift(s):
        return [(at(z, x), at(z, (x + s) % nx)) for z in range(NZ) for x in range(nx)]

    def level_sign(level):
        return jnp.where((me_w >> level) & 1 == 1, -1.0, 1.0).astype(F32)

    chunks = range(len(CHUNKS))
    current = []
    for i in chunks:
        start, width = CHUNKS[i]
        current.append(mix_chunk(signs, had, flux_rows, start, width))
    for level in range(levels - 1):
        for i in chunks:
            partner = lax.ppermute(current[i], "wide", [(w, w ^ (1 << level)) for w in range(wide)])
            own = current[i].astype(F32)
            current[i] = ((partner.astype(F32) + own * level_sign(level)) * SQRT_HALF).astype(BF16)

    counts = count_samples(sample_rows, sample_owner, nx, rows, me_z, me_x)
    owner_counts = [counts[0]]
    for s in range(1, nx):
        owner_counts.append(lax.ppermute(counts[s], "blk", x_shift(s)))

    whole, sources = None, []
    for i in chunks:
        start, width = CHUNKS[i]
        partner = lax.ppermute(current[i], "wide", [(w, w ^ (wide // 2)) for w in range(wide)])
        current[i], whole = join_last(current[i], partner, level_sign(levels - 1), start, columns, whole)
        sources.append([current[i]])
        for s in range(1, nx):
            sources[i].append(lax.ppermute(current[i], "blk", x_shift(s)))

    weights, grams = [], []
    for p in range(nx):
        weights.append(weigh(owner_counts[p], sources[0][p]))
    for i in chunks:
        keep, send = partial_grams(weights, sources[i], i == 0)
        near = lax.ppermute(send, "blk", z_route(1))
        onward = far_sum(keep, near)
        far = lax.ppermute(onward, "blk", z_route(2))
        grams.append((keep, near, far))
    state = factor_first(*grams[0], scale)
    sketch, inverse = factor_last(state, columns)
    for i in chunks[1:]:
        sketch = couple(inverse, *grams[i], sketch, CHUNKS[i][0], scale)
    return whole, sketch


def solution(mesh):
    placed = (
        P(("wide", "blk"), None),
        P(("wide", "blk")),
        P(("wide", "blk")),
        P(("wide", "blk"), None),
    )

    return jax.shard_map(
        per_device,
        mesh=mesh,
        in_specs=placed,
        out_specs=(P(("wide", "blk"), None), P(("wide", "blk"), None)),
        check_vma=False,
    )
```

```python
import functools

import jax
import jax.numpy as jnp
import numpy as np
from jax import lax
from jax.experimental import pallas as pl
from jax.experimental.pallas import tpu as pltpu
from jax.sharding import PartitionSpec as P

PANEL = 256
HB = 128
NZ = 4
CHUNKS = ((0, 256), (256, 256), (512, 256), (768, 256))
SQRT_HALF = 0.7071067811865476
HIGHEST = lax.Precision.HIGHEST
F32 = jnp.float32
BF16 = jnp.bfloat16


def hadamard_pair():
    idx = np.arange(HB)
    common = idx[:, None] & idx[None, :]
    parity = np.zeros_like(common)
    for bit in range(HB.bit_length() - 1):
        parity ^= (common >> bit) & 1
    one = 1.0 - 2.0 * parity
    return jnp.asarray(np.kron(np.eye(2), one), BF16)


VMEM_LIMIT = 24 << 20


def params(**kw):
    return pltpu.CompilerParams(vmem_limit_bytes=VMEM_LIMIT, **kw)


def cost(flops, moved):
    return pl.CostEstimate(flops=flops, bytes_accessed=moved, transcendentals=0)


def mix_kernel(signs_ref, had_ref, x_ref, out_ref):
    rows = x_ref.shape[0]
    size = had_ref.shape[0]
    for b in range(rows // size):
        part = pl.ds(b * size, size)
        signed = (had_ref[...].astype(F32) * signs_ref[:, b * size : (b + 1) * size].astype(F32)).astype(BF16)
        x = x_ref[part, :]
        hi = x.astype(BF16)
        rest = x - hi.astype(F32)
        mid = rest.astype(BF16)
        low = (rest - mid.astype(F32)).astype(BF16)
        total = jnp.dot(signed, low, preferred_element_type=F32)
        total = total + jnp.dot(signed, mid, preferred_element_type=F32)
        total = total + jnp.dot(signed, hi, preferred_element_type=F32)
        out_ref[part, :] = (total * (HB**-0.5)).astype(BF16)


def mix_chunk(signs, had, flux, start, width):
    rows = flux.shape[0]
    size = had.shape[0]
    block = start // width
    return pl.pallas_call(
        mix_kernel,
        grid=(1,),
        in_specs=[
            pl.BlockSpec((1, rows), lambda i: (0, 0)),
            pl.BlockSpec(had.shape, lambda i: (0, 0)),
            pl.BlockSpec((rows, width), lambda i: (0, block)),
        ],
        out_specs=pl.BlockSpec((rows, width), lambda i: (0, 0)),
        out_shape=jax.ShapeDtypeStruct((rows, width), BF16),
        cost_estimate=cost(2 * rows * width * size * 3, rows * width * 6),
        name="mix",
    )(signs, had, flux)


def join_kernel(sign_ref, own_ref, other_ref, *refs):
    total = (other_ref[...].astype(F32) + own_ref[...].astype(F32) * sign_ref[0]) * SQRT_HALF
    total = total.astype(BF16)
    for ref in refs[-2:]:
        ref[...] = total


def join_last(own, other, sign, start, columns, whole):
    rows, width = own.shape
    block = start // width
    tile = rows // 2
    chunk = pl.BlockSpec((tile, width), lambda i: (i, 0))
    operands, specs, alias = [sign.reshape(1), own, other], [pl.BlockSpec(memory_space=pltpu.SMEM), chunk, chunk], {}
    if whole is not None:
        operands.append(whole)
        specs.append(pl.BlockSpec(memory_space=pl.ANY))
        alias = {3: 1}
    return pl.pallas_call(
        join_kernel,
        grid=(rows // tile,),
        in_specs=specs,
        out_specs=(chunk, pl.BlockSpec((tile, width), lambda i: (i, block))),
        out_shape=(jax.ShapeDtypeStruct((rows, width), BF16), jax.ShapeDtypeStruct((rows, columns), BF16)),
        input_output_aliases=alias,
        compiler_params=params(),
        cost_estimate=cost(4 * rows * width, 8 * rows * width),
        name="join",
    )(*operands)


def relative_owner(q):
    return ((q & 1) << 1) | (q >> 1)


def count_kernel(nx, me_ref, rows_ref, owner_ref, *out_refs):
    listed = rows_ref.shape[1]
    rows = out_refs[0].shape[1]
    me_z, me_x = me_ref[0], me_ref[1]
    index = lax.broadcasted_iota(jnp.int32, (NZ * nx, listed), 0)
    q, s = index & (NZ - 1), index >> (NZ.bit_length() - 1)
    z = me_z ^ relative_owner(q)
    x = (me_x + s) & (nx - 1)
    by_owner = (z * nx + x == owner_ref[...]).astype(F32).astype(BF16)
    by_row = (lax.broadcasted_iota(jnp.int32, (rows, listed), 0) == rows_ref[...]).astype(F32).astype(BF16)
    total = lax.dot_general(by_owner, by_row, (((1,), (1,)), ((), ())), preferred_element_type=F32)
    for shift, ref in enumerate(out_refs):
        ref[...] = total[shift * NZ : (shift + 1) * NZ, :]


def count_samples(sample_rows, sample_owner, nx, rows, me_z, me_x):
    listed = sample_rows.shape[0]
    shape = jax.ShapeDtypeStruct((NZ, rows), F32)
    vmem = pl.BlockSpec(memory_space=pltpu.VMEM)
    return pl.pallas_call(
        functools.partial(count_kernel, nx),
        in_specs=[pl.BlockSpec(memory_space=pltpu.SMEM), vmem, vmem],
        out_shape=(shape,) * nx,
        compiler_params=params(),
        cost_estimate=cost(2 * rows * listed * NZ * nx, rows * NZ * nx * 4),
        name="counts",
    )(jnp.stack([me_z, me_x]), sample_rows.reshape(1, listed), sample_owner.reshape(1, listed))


def weigh_kernel(counts_ref, lead_ref, hi_ref, lo_ref):
    lead = lead_ref[...].astype(F32).T
    for q in range(NZ):
        part = pl.ds(q * PANEL, PANEL)
        weighed = lead * counts_ref[q : q + 1, :]
        hi = weighed.astype(BF16)
        hi_ref[part, :] = hi
        lo_ref[part, :] = (weighed - hi.astype(F32)).astype(BF16)


def weigh(counts, lead):
    rows = lead.shape[0]
    tile = rows // 2
    out = pl.BlockSpec((NZ * PANEL, tile), lambda i: (0, i))
    shape = jax.ShapeDtypeStruct((NZ * PANEL, rows), BF16)
    return pl.pallas_call(
        weigh_kernel,
        grid=(rows // tile,),
        in_specs=[pl.BlockSpec((NZ, tile), lambda i: (0, i)), pl.BlockSpec((tile, PANEL), lambda i: (i, 0))],
        out_specs=(out, out),
        out_shape=(shape, shape),
        compiler_params=params(),
        cost_estimate=cost(rows * PANEL * 16, rows * PANEL * 18),
        name="weigh",
    )(counts, lead)


GRAM_TILES = 2


def gram_kernel(parts, packed, *refs):
    keep_ref, send_ref, acc = refs[-3:]
    step = pl.program_id(0)

    @pl.when(step == 0)
    def _():
        acc[...] = jnp.zeros_like(acc)

    for p in range(parts):
        hi_ref, lo_ref, rows_ref = refs[3 * p : 3 * p + 3]

        @pl.when(step // GRAM_TILES == p)
        def _(hi_ref=hi_ref, lo_ref=lo_ref, rows_ref=rows_ref):
            rows = rows_ref[...]
            low = jnp.dot(lo_ref[...], rows, preferred_element_type=F32)
            acc[...] += low + jnp.dot(hi_ref[...], rows, preferred_element_type=F32)

    @pl.when(step == parts * GRAM_TILES - 1)
    def _():
        half = PANEL // 2
        for q in range(NZ):
            ref, place = (keep_ref, q) if q < NZ // 2 else (send_ref, q - NZ // 2)
            base = q * PANEL
            if packed:
                to = place * 3 * half
                ref[to : to + PANEL, :] = acc[base : base + PANEL, :half]
                ref[to + PANEL : to + 3 * half, :] = acc[base + half : base + PANEL, half:]
            else:
                ref[place * PANEL : (place + 1) * PANEL, :] = acc[base : base + PANEL, :]


def partial_grams(weights, chunk_rows, packed):
    parts = len(chunk_rows)
    rows, width = chunk_rows[0].shape
    tile = rows // GRAM_TILES
    half = NZ // 2
    shape = (half * (PANEL + PANEL // 2), PANEL // 2) if packed else (half * PANEL, width)
    operands, specs = [], []
    for p, ((hi, lo), block) in enumerate(zip(weights, chunk_rows)):
        operands += [hi, lo, block]

        def place(k, p=p):
            return jnp.clip(k - p * GRAM_TILES, 0, GRAM_TILES - 1)

        weight_spec = pl.BlockSpec((NZ * PANEL, tile), lambda k, place=place: (0, place(k)))
        specs += [weight_spec, weight_spec, pl.BlockSpec((tile, width), lambda k, place=place: (place(k), 0))]
    out = pl.BlockSpec(shape, lambda k: (0, 0))
    out_shape = jax.ShapeDtypeStruct(shape, F32)
    return pl.pallas_call(
        functools.partial(gram_kernel, parts, packed),
        grid=(parts * GRAM_TILES,),
        in_specs=specs,
        out_specs=(out, out),
        out_shape=(out_shape, out_shape),
        scratch_shapes=[pltpu.VMEM((NZ * PANEL, width), F32)],
        compiler_params=params(),
        cost_estimate=cost(4 * parts * NZ * PANEL * rows * width, 4 * parts * NZ * PANEL * rows + 2 * parts * rows * width),
        name="grams",
    )(*operands)


def add_kernel(keep_ref, near_ref, out_ref):
    out_ref[...] = keep_ref[...] + near_ref[...]


def far_sum(keep, near):
    rows, width = keep.shape[0] // 2, keep.shape[1]
    spec = pl.BlockSpec((rows, width), lambda i: (1, 0))
    return pl.pallas_call(
        add_kernel,
        grid=(1,),
        in_specs=[spec, spec],
        out_specs=pl.BlockSpec((rows, width), lambda i: (0, 0)),
        out_shape=jax.ShapeDtypeStruct((rows, width), F32),
        compiler_params=params(),
        cost_estimate=cost(rows * width, 12 * rows * width),
        name="add",
    )(keep, near)


BAND = 64
CUT = 2
MICRO = 8


def factor_band(tile):
    row_id = lax.broadcasted_iota(jnp.int32, (BAND, 1), 0)
    for first in range(0, BAND, MICRO):
        spread = [jnp.broadcast_to(tile[:, first + t : first + t + 1], tile.shape) for t in range(MICRO)]
        for t in range(MICRO):
            j = first + t
            r = lax.rsqrt(spread[t][j : j + 1, :])
            row = tile[j : j + 1, :] * r
            below = jnp.where(row_id > j, spread[t], 0.0)
            for u in range(t + 1, MICRO):
                spread[u] = spread[u] - below * (spread[u][j : j + 1, :] * (r * r))
            tile = jnp.where(row_id == j, row, tile - below * (row * r))
    return tile


def eliminate(work, first, last):
    rb = lax.broadcasted_iota(jnp.int32, (BAND, BAND), 0)
    cb = lax.broadcasted_iota(jnp.int32, (BAND, BAND), 1)
    eye_b = (rb == cb).astype(F32)
    for k in range(first, last):
        lo, hi = k * BAND, (k + 1) * BAND
        tile = factor_band(jnp.concatenate([work[lo:hi, lo:hi], eye_b], axis=1))
        inv = jnp.where(rb >= cb, tile[:, BAND:], 0.0)
        full = jnp.dot(inv, work[lo:hi, lo:], precision=HIGHEST, preferred_element_type=F32)
        if hi < PANEL:
            panel = full[:, BAND : PANEL - lo]
            work[hi:, hi:] = work[hi:, hi:] - lax.dot_general(
                panel, full[:, BAND:], (((0,), (0,)), ((), ())), precision=HIGHEST, preferred_element_type=F32
            )
        work[lo:hi, lo:] = full


def factor_first_kernel(scale, keep_ref, near_ref, far_ref, out_ref, work):
    half = PANEL // 2
    lead = (keep_ref[...] + near_ref[...] + far_ref[...]) * scale
    ri = lax.broadcasted_iota(jnp.int32, (PANEL, PANEL), 0)
    ci = lax.broadcasted_iota(jnp.int32, (PANEL, PANEL), 1)
    eye = (ri == ci).astype(F32)
    work[:, PANEL:] = eye
    work[:half, :half] = lead[:half, :] + 0.5 * eye[:half, :half]
    work[:half, half:PANEL] = lead[half:PANEL, :].T
    work[half:, :half] = lead[half:PANEL, :]
    work[half:, half:PANEL] = lead[PANEL:, :] + 0.5 * eye[:half, :half]
    eliminate(work, 0, CUT)
    out_ref[...] = work[...]


def factor_last_kernel(in_ref, out_ref, inverse_ref, work):
    work[...] = in_ref[...]
    eliminate(work, CUT, PANEL // BAND)
    ri = lax.broadcasted_iota(jnp.int32, (PANEL, PANEL), 0)
    ci = lax.broadcasted_iota(jnp.int32, (PANEL, PANEL), 1)
    out_ref[...] = jnp.where(ci >= ri, work[:, :PANEL], 0.0)
    inverse_ref[...] = jnp.where(ri >= ci, work[:, PANEL:], 0.0)


def factor_first(keep, near, far, scale):
    spec = pl.BlockSpec(far.shape, lambda i: (0, 0))
    shape = (PANEL, 2 * PANEL)
    return pl.pallas_call(
        functools.partial(factor_first_kernel, scale),
        grid=(1,),
        in_specs=[spec, spec, spec],
        out_specs=pl.BlockSpec(shape, lambda i: (0, 0)),
        out_shape=jax.ShapeDtypeStruct(shape, F32),
        scratch_shapes=[pltpu.VMEM(shape, F32)],
        compiler_params=params(),
        cost_estimate=cost(10_000_000_000, 1 << 20),
        name="factor_first",
    )(keep, near, far)


def factor_last(state, columns):
    square = pl.BlockSpec((PANEL, PANEL), lambda i: (0, 0))
    return pl.pallas_call(
        factor_last_kernel,
        grid=(1,),
        in_specs=[pl.BlockSpec(state.shape, lambda i: (0, 0))],
        out_specs=(square, square),
        out_shape=(jax.ShapeDtypeStruct((PANEL, columns), F32), jax.ShapeDtypeStruct((PANEL, PANEL), F32)),
        scratch_shapes=[pltpu.VMEM(state.shape, F32)],
        compiler_params=params(),
        cost_estimate=cost(10_000_000_000, 1 << 20),
        name="factor_last",
    )(state)


def couple_kernel(scale, inverse_ref, keep_ref, near_ref, far_ref, whole_ref, out_ref):
    gram = (keep_ref[...] + near_ref[...] + far_ref[...]) * scale
    out_ref[...] = jnp.dot(inverse_ref[...], gram, precision=HIGHEST, preferred_element_type=F32)


def couple(inverse, keep, near, far, whole, start, scale):
    rows, width = far.shape
    block = start // width
    spec = pl.BlockSpec((rows, width), lambda i: (0, 0))
    return pl.pallas_call(
        functools.partial(couple_kernel, scale),
        grid=(1,),
        in_specs=[pl.BlockSpec(inverse.shape, lambda i: (0, 0)), spec, spec, spec, pl.BlockSpec(memory_space=pl.ANY)],
        out_specs=pl.BlockSpec((rows, width), lambda i: (0, block)),
        out_shape=jax.ShapeDtypeStruct(whole.shape, F32),
        input_output_aliases={4: 0},
        compiler_params=params(),
        cost_estimate=cost(12 * PANEL * rows * width, 20 * rows * width),
        name="couple",
    )(inverse, keep, near, far, whole)


def per_device(flux_rows, row_signs, sample_rows, sample_owner):
    wide, blk = lax.axis_size("wide"), lax.axis_size("blk")
    nx = blk // NZ
    rows, columns = flux_rows.shape
    scale = 1.0 / sample_rows.shape[0]
    me_w, me_b = lax.axis_index("wide"), lax.axis_index("blk")
    me_x, me_z = me_b & (nx - 1), me_b >> (nx.bit_length() - 1)
    had = hadamard_pair()
    signs = row_signs.reshape(1, rows)
    levels = wide.bit_length() - 1

    def at(z, x):
        return z * nx + x

    def z_route(mask):
        return [(at(z, x), at(z ^ mask, x)) for z in range(NZ) for x in range(nx)]

    def x_shift(s):
        return [(at(z, x), at(z, (x + s) % nx)) for z in range(NZ) for x in range(nx)]

    def level_sign(level):
        return jnp.where((me_w >> level) & 1 == 1, -1.0, 1.0).astype(F32)

    chunks = range(len(CHUNKS))
    current = []
    for i in chunks:
        start, width = CHUNKS[i]
        current.append(mix_chunk(signs, had, flux_rows, start, width))
    counts = count_samples(sample_rows, sample_owner, nx, rows, me_z, me_x)
    owner_counts = [counts[0]]
    for s in range(1, nx):
        owner_counts.append(lax.ppermute(counts[s], "blk", x_shift(s)))

    for level in range(levels - 1):
        for i in chunks:
            partner = lax.ppermute(current[i], "wide", [(w, w ^ (1 << level)) for w in range(wide)])
            own = current[i].astype(F32)
            current[i] = ((partner.astype(F32) + own * level_sign(level)) * SQRT_HALF).astype(BF16)

    whole, sources = None, []
    for i in chunks:
        start, width = CHUNKS[i]
        partner = lax.ppermute(current[i], "wide", [(w, w ^ (wide // 2)) for w in range(wide)])
        current[i], whole = join_last(current[i], partner, level_sign(levels - 1), start, columns, whole)
        sources.append([current[i]])
        for s in range(1, nx):
            sources[i].append(lax.ppermute(current[i], "blk", x_shift(s)))

    weights, grams = [], []
    for p in range(nx):
        weights.append(weigh(owner_counts[p], sources[0][p]))
    for i in chunks:
        keep, send = partial_grams(weights, sources[i], i == 0)
        near = lax.ppermute(send, "blk", z_route(1))
        onward = far_sum(keep, near)
        far = lax.ppermute(onward, "blk", z_route(2))
        grams.append((keep, near, far))
    state = factor_first(*grams[0], scale)
    sketch, inverse = factor_last(state, columns)
    for i in chunks[1:]:
        sketch = couple(inverse, *grams[i], sketch, CHUNKS[i][0], scale)
    return whole, sketch


def solution(mesh):
    placed = (
        P(("wide", "blk"), None),
        P(("wide", "blk")),
        P(("wide", "blk")),
        P(("wide", "blk"), None),
    )

    return jax.shard_map(
        per_device,
        mesh=mesh,
        in_specs=placed,
        out_specs=(P(("wide", "blk"), None), P(("wide", "blk"), None)),
        check_vma=False,
    )
```

```python
import functools

import jax
import jax.numpy as jnp
import numpy as np
from jax import lax
from jax.experimental import pallas as pl
from jax.experimental.pallas import tpu as pltpu
from jax.sharding import PartitionSpec as P

PANEL = 256
HB = 128
NZ = 4
LEAD = ((0, 128), (128, 128))
CHUNKS = ((256, 256), (512, 256), (768, 128), (896, 128))
SQRT_HALF = 0.7071067811865476
HIGHEST = lax.Precision.HIGHEST
F32 = jnp.float32
BF16 = jnp.bfloat16


def hadamard_pair():
    idx = np.arange(HB)
    common = idx[:, None] & idx[None, :]
    parity = np.zeros_like(common)
    for bit in range(HB.bit_length() - 1):
        parity ^= (common >> bit) & 1
    one = 1.0 - 2.0 * parity
    return jnp.asarray(np.kron(np.eye(2), one), BF16)


VMEM_LIMIT = 24 << 20


def params(**kw):
    return pltpu.CompilerParams(vmem_limit_bytes=VMEM_LIMIT, **kw)


def cost(flops, moved):
    return pl.CostEstimate(flops=flops, bytes_accessed=moved, transcendentals=0)


def mix_kernel(signs_ref, had_ref, x_ref, out_ref):
    rows = x_ref.shape[0]
    size = had_ref.shape[0]
    for b in range(rows // size):
        part = pl.ds(b * size, size)
        signed = (had_ref[...].astype(F32) * signs_ref[:, b * size : (b + 1) * size].astype(F32)).astype(BF16)
        x = x_ref[part, :]
        hi = x.astype(BF16)
        rest = x - hi.astype(F32)
        mid = rest.astype(BF16)
        low = (rest - mid.astype(F32)).astype(BF16)
        total = jnp.dot(signed, low, preferred_element_type=F32)
        total = total + jnp.dot(signed, mid, preferred_element_type=F32)
        total = total + jnp.dot(signed, hi, preferred_element_type=F32)
        out_ref[part, :] = (total * (HB**-0.5)).astype(BF16)


def mix_columns(signs, had, flux, first, blocks):
    rows = flux.shape[0]
    return pl.pallas_call(
        mix_kernel,
        grid=(blocks,),
        in_specs=[
            pl.BlockSpec((1, rows), lambda i: (0, 0)),
            pl.BlockSpec(had.shape, lambda i: (0, 0)),
            pl.BlockSpec((rows, PANEL), lambda i: (0, i + first)),
        ],
        out_specs=pl.BlockSpec((None, rows, PANEL), lambda i: (i, 0, 0)),
        out_shape=jax.ShapeDtypeStruct((blocks, rows, PANEL), BF16),
        cost_estimate=cost(2 * blocks * rows * PANEL * had.shape[0] * 3, blocks * rows * PANEL * 6),
        name="mix",
    )(signs, had, flux)


def join_split_kernel(places, sign_ref, own_ref, other_ref, *out_refs):
    total = (other_ref[...].astype(F32) + own_ref[...].astype(F32) * sign_ref[0]) * SQRT_HALF
    total = total.astype(BF16)
    for (block, offset, width), ref in zip(places, out_refs):
        ref[...] = total[block, :, offset : offset + width]


def join_split(own, other, sign, chunks):
    blocks, rows, wide = own.shape
    tile = rows // 4
    base = chunks[0][0]
    places = tuple(((start - base) // wide, (start - base) % wide, width) for start, width in chunks)
    spec = pl.BlockSpec((blocks, tile, wide), lambda i: (0, i, 0))
    return pl.pallas_call(
        functools.partial(join_split_kernel, places),
        grid=(rows // tile,),
        in_specs=[pl.BlockSpec(memory_space=pltpu.SMEM), spec, spec],
        out_specs=tuple(pl.BlockSpec((tile, width), lambda i: (i, 0)) for _, width in chunks),
        out_shape=tuple(jax.ShapeDtypeStruct((rows, width), BF16) for _, width in chunks),
        cost_estimate=cost(4 * blocks * rows * wide, 6 * blocks * rows * wide),
        name="join",
    )(sign.reshape(1), own, other)


def join_kernel(sign_ref, own_ref, other_ref, *refs):
    total = (other_ref[...].astype(F32) + own_ref[...].astype(F32) * sign_ref[0]) * SQRT_HALF
    total = total.astype(BF16)
    for ref in refs[-2:]:
        ref[...] = total


def join_last(own, other, sign, start, columns, whole):
    rows, width = own.shape
    block = start // width
    tile = rows // 2
    chunk = pl.BlockSpec((tile, width), lambda i: (i, 0))
    operands, specs, alias = [sign.reshape(1), own, other], [pl.BlockSpec(memory_space=pltpu.SMEM), chunk, chunk], {}
    if whole is not None:
        operands.append(whole)
        specs.append(pl.BlockSpec(memory_space=pl.ANY))
        alias = {3: 1}
    return pl.pallas_call(
        join_kernel,
        grid=(rows // tile,),
        in_specs=specs,
        out_specs=(chunk, pl.BlockSpec((tile, width), lambda i: (i, block))),
        out_shape=(jax.ShapeDtypeStruct((rows, width), BF16), jax.ShapeDtypeStruct((rows, columns), BF16)),
        input_output_aliases=alias,
        compiler_params=params(),
        cost_estimate=cost(4 * rows * width, 8 * rows * width),
        name="join",
    )(*operands)


def relative_owner(q):
    return ((q & 1) << 1) | (q >> 1)


def count_kernel(nx, me_ref, rows_ref, owner_ref, *out_refs):
    listed = rows_ref.shape[1]
    rows = out_refs[0].shape[1]
    me_z, me_x = me_ref[0], me_ref[1]
    index = lax.broadcasted_iota(jnp.int32, (NZ * nx, listed), 0)
    q, s = index & (NZ - 1), index >> (NZ.bit_length() - 1)
    z = me_z ^ relative_owner(q)
    x = (me_x + s) & (nx - 1)
    by_owner = (z * nx + x == owner_ref[...]).astype(F32).astype(BF16)
    by_row = (lax.broadcasted_iota(jnp.int32, (rows, listed), 0) == rows_ref[...]).astype(F32).astype(BF16)
    total = lax.dot_general(by_owner, by_row, (((1,), (1,)), ((), ())), preferred_element_type=F32)
    for shift, ref in enumerate(out_refs):
        ref[...] = total[shift * NZ : (shift + 1) * NZ, :]


def count_samples(sample_rows, sample_owner, nx, rows, me_z, me_x):
    listed = sample_rows.shape[0]
    shape = jax.ShapeDtypeStruct((NZ, rows), F32)
    vmem = pl.BlockSpec(memory_space=pltpu.VMEM)
    return pl.pallas_call(
        functools.partial(count_kernel, nx),
        in_specs=[pl.BlockSpec(memory_space=pltpu.SMEM), vmem, vmem],
        out_shape=(shape,) * nx,
        compiler_params=params(),
        cost_estimate=cost(2 * rows * listed * NZ * nx, rows * NZ * nx * 4),
        name="counts",
    )(jnp.stack([me_z, me_x]), sample_rows.reshape(1, listed), sample_owner.reshape(1, listed))


def weigh_kernel(counts_ref, left_ref, right_ref, hi_ref, lo_ref):
    lead = jnp.concatenate([left_ref[...].astype(F32).T, right_ref[...].astype(F32).T], axis=0)
    for q in range(NZ):
        part = pl.ds(q * PANEL, PANEL)
        weighed = lead * counts_ref[q : q + 1, :]
        hi = weighed.astype(BF16)
        hi_ref[part, :] = hi
        lo_ref[part, :] = (weighed - hi.astype(F32)).astype(BF16)


def weigh(counts, left, right):
    rows = left.shape[0]
    tile = rows // 2
    out = pl.BlockSpec((NZ * PANEL, tile), lambda i: (0, i))
    shape = jax.ShapeDtypeStruct((NZ * PANEL, rows), BF16)
    return pl.pallas_call(
        weigh_kernel,
        grid=(rows // tile,),
        in_specs=[pl.BlockSpec((NZ, tile), lambda i: (0, i))] + [pl.BlockSpec((tile, PANEL // 2), lambda i: (i, 0))] * 2,
        out_specs=(out, out),
        out_shape=(shape, shape),
        compiler_params=params(),
        cost_estimate=cost(rows * PANEL * 16, rows * PANEL * 18),
        name="weigh",
    )(counts, left, right)


GRAM_TILES = 2


def gram_kernel(parts, packed, *refs):
    keep_ref, send_ref, acc = refs[-3:]
    step = pl.program_id(0)

    @pl.when(step == 0)
    def _():
        acc[...] = jnp.zeros_like(acc)

    each = (len(refs) - 3) // parts
    for p in range(parts):
        hi_ref, lo_ref, *rows_refs = refs[each * p : each * (p + 1)]

        @pl.when(step // GRAM_TILES == p)
        def _(hi_ref=hi_ref, lo_ref=lo_ref, rows_refs=rows_refs):
            rows = jnp.concatenate([ref[...] for ref in rows_refs], axis=1)
            low = jnp.dot(lo_ref[...], rows, preferred_element_type=F32)
            acc[...] += low + jnp.dot(hi_ref[...], rows, preferred_element_type=F32)

    @pl.when(step == parts * GRAM_TILES - 1)
    def _():
        half = PANEL // 2
        for q in range(NZ):
            ref, place = (keep_ref, q) if q < NZ // 2 else (send_ref, q - NZ // 2)
            base = q * PANEL
            if packed:
                to = place * 3 * half
                ref[to : to + PANEL, :] = acc[base : base + PANEL, :half]
                ref[to + PANEL : to + 3 * half, :] = acc[base + half : base + PANEL, half:]
            else:
                ref[place * PANEL : (place + 1) * PANEL, :] = acc[base : base + PANEL, :]


def partial_grams(weights, chunk_rows, packed):
    parts = len(chunk_rows)
    rows = chunk_rows[0][0].shape[0]
    width = sum(piece.shape[1] for piece in chunk_rows[0])
    tile = rows // GRAM_TILES
    half = NZ // 2
    shape = (half * (PANEL + PANEL // 2), PANEL // 2) if packed else (half * PANEL, width)
    operands, specs = [], []
    for p, ((hi, lo), pieces) in enumerate(zip(weights, chunk_rows)):
        operands += [hi, lo, *pieces]

        def place(k, p=p):
            return jnp.clip(k - p * GRAM_TILES, 0, GRAM_TILES - 1)

        weight_spec = pl.BlockSpec((NZ * PANEL, tile), lambda k, place=place: (0, place(k)))
        specs += [weight_spec, weight_spec]
        specs += [pl.BlockSpec((tile, piece.shape[1]), lambda k, place=place: (place(k), 0)) for piece in pieces]
    out = pl.BlockSpec(shape, lambda k: (0, 0))
    out_shape = jax.ShapeDtypeStruct(shape, F32)
    return pl.pallas_call(
        functools.partial(gram_kernel, parts, packed),
        grid=(parts * GRAM_TILES,),
        in_specs=specs,
        out_specs=(out, out),
        out_shape=(out_shape, out_shape),
        scratch_shapes=[pltpu.VMEM((NZ * PANEL, width), F32)],
        compiler_params=params(),
        cost_estimate=cost(4 * parts * NZ * PANEL * rows * width, 4 * parts * NZ * PANEL * rows + 2 * parts * rows * width),
        name="grams",
    )(*operands)


def add_kernel(keep_ref, near_ref, out_ref):
    out_ref[...] = keep_ref[...] + near_ref[...]


def far_sum(keep, near):
    rows, width = keep.shape[0] // 2, keep.shape[1]
    spec = pl.BlockSpec((rows, width), lambda i: (1, 0))
    return pl.pallas_call(
        add_kernel,
        grid=(1,),
        in_specs=[spec, spec],
        out_specs=pl.BlockSpec((rows, width), lambda i: (0, 0)),
        out_shape=jax.ShapeDtypeStruct((rows, width), F32),
        compiler_params=params(),
        cost_estimate=cost(rows * width, 12 * rows * width),
        name="add",
    )(keep, near)


BAND = 64
CUT = 2
MICRO = 8


def factor_band(tile):
    row_id = lax.broadcasted_iota(jnp.int32, (BAND, 1), 0)
    for first in range(0, BAND, MICRO):
        spread = [jnp.broadcast_to(tile[:, first + t : first + t + 1], tile.shape) for t in range(MICRO)]
        for t in range(MICRO):
            j = first + t
            r = lax.rsqrt(spread[t][j : j + 1, :])
            row = tile[j : j + 1, :] * r
            below = jnp.where(row_id > j, spread[t], 0.0)
            for u in range(t + 1, MICRO):
                spread[u] = spread[u] - below * (spread[u][j : j + 1, :] * (r * r))
            tile = jnp.where(row_id == j, row, tile - below * (row * r))
    return tile


def eliminate(work, first, last):
    rb = lax.broadcasted_iota(jnp.int32, (BAND, BAND), 0)
    cb = lax.broadcasted_iota(jnp.int32, (BAND, BAND), 1)
    eye_b = (rb == cb).astype(F32)
    for k in range(first, last):
        lo, hi = k * BAND, (k + 1) * BAND
        tile = factor_band(jnp.concatenate([work[lo:hi, lo:hi], eye_b], axis=1))
        inv = jnp.where(rb >= cb, tile[:, BAND:], 0.0)
        full = jnp.dot(inv, work[lo:hi, lo:], precision=HIGHEST, preferred_element_type=F32)
        if hi < PANEL:
            panel = full[:, BAND : PANEL - lo]
            work[hi:, hi:] = work[hi:, hi:] - lax.dot_general(
                panel, full[:, BAND:], (((0,), (0,)), ((), ())), precision=HIGHEST, preferred_element_type=F32
            )
        work[lo:hi, lo:] = full


def factor_first_kernel(scale, keep_ref, near_ref, far_ref, out_ref, work):
    half = PANEL // 2
    lead = (keep_ref[...] + near_ref[...] + far_ref[...]) * scale
    ri = lax.broadcasted_iota(jnp.int32, (PANEL, PANEL), 0)
    ci = lax.broadcasted_iota(jnp.int32, (PANEL, PANEL), 1)
    eye = (ri == ci).astype(F32)
    work[:, PANEL:] = eye
    work[:half, :half] = lead[:half, :] + 0.5 * eye[:half, :half]
    work[:half, half:PANEL] = lead[half:PANEL, :].T
    work[half:, :half] = lead[half:PANEL, :]
    work[half:, half:PANEL] = lead[PANEL:, :] + 0.5 * eye[:half, :half]
    eliminate(work, 0, CUT)
    out_ref[...] = work[...]


def factor_last_kernel(in_ref, out_ref, inverse_ref, work):
    work[...] = in_ref[...]
    eliminate(work, CUT, PANEL // BAND)
    ri = lax.broadcasted_iota(jnp.int32, (PANEL, PANEL), 0)
    ci = lax.broadcasted_iota(jnp.int32, (PANEL, PANEL), 1)
    out_ref[...] = jnp.where(ci >= ri, work[:, :PANEL], 0.0)
    inverse_ref[...] = jnp.where(ri >= ci, work[:, PANEL:], 0.0)


def factor_first(keep, near, far, scale):
    spec = pl.BlockSpec(far.shape, lambda i: (0, 0))
    shape = (PANEL, 2 * PANEL)
    return pl.pallas_call(
        functools.partial(factor_first_kernel, scale),
        grid=(1,),
        in_specs=[spec, spec, spec],
        out_specs=pl.BlockSpec(shape, lambda i: (0, 0)),
        out_shape=jax.ShapeDtypeStruct(shape, F32),
        scratch_shapes=[pltpu.VMEM(shape, F32)],
        compiler_params=params(),
        cost_estimate=cost(10_000_000_000, 1 << 20),
        name="factor_first",
    )(keep, near, far)


def factor_last(state, columns):
    square = pl.BlockSpec((PANEL, PANEL), lambda i: (0, 0))
    return pl.pallas_call(
        factor_last_kernel,
        grid=(1,),
        in_specs=[pl.BlockSpec(state.shape, lambda i: (0, 0))],
        out_specs=(square, square),
        out_shape=(jax.ShapeDtypeStruct((PANEL, columns), F32), jax.ShapeDtypeStruct((PANEL, PANEL), F32)),
        scratch_shapes=[pltpu.VMEM(state.shape, F32)],
        compiler_params=params(),
        cost_estimate=cost(10_000_000_000, 1 << 20),
        name="factor_last",
    )(state)


def couple_kernel(scale, inverse_ref, keep_ref, near_ref, far_ref, whole_ref, out_ref):
    gram = (keep_ref[...] + near_ref[...] + far_ref[...]) * scale
    out_ref[...] = jnp.dot(inverse_ref[...], gram, precision=HIGHEST, preferred_element_type=F32)


def couple(inverse, keep, near, far, whole, start, scale):
    rows, width = far.shape
    block = start // width
    spec = pl.BlockSpec((rows, width), lambda i: (0, 0))
    return pl.pallas_call(
        functools.partial(couple_kernel, scale),
        grid=(1,),
        in_specs=[pl.BlockSpec(inverse.shape, lambda i: (0, 0)), spec, spec, spec, pl.BlockSpec(memory_space=pl.ANY)],
        out_specs=pl.BlockSpec((rows, width), lambda i: (0, block)),
        out_shape=jax.ShapeDtypeStruct(whole.shape, F32),
        input_output_aliases={4: 0},
        compiler_params=params(),
        cost_estimate=cost(12 * PANEL * rows * width, 20 * rows * width),
        name="couple",
    )(inverse, keep, near, far, whole)


def per_device(flux_rows, row_signs, sample_rows, sample_owner):
    wide, blk = lax.axis_size("wide"), lax.axis_size("blk")
    nx = blk // NZ
    rows, columns = flux_rows.shape
    scale = 1.0 / sample_rows.shape[0]
    me_w, me_b = lax.axis_index("wide"), lax.axis_index("blk")
    me_x, me_z = me_b & (nx - 1), me_b >> (nx.bit_length() - 1)
    had = hadamard_pair()
    signs = row_signs.reshape(1, rows)
    levels = wide.bit_length() - 1

    def at(z, x):
        return z * nx + x

    def z_route(mask):
        return [(at(z, x), at(z ^ mask, x)) for z in range(NZ) for x in range(nx)]

    def x_shift(s):
        return [(at(z, x), at(z, (x + s) % nx)) for z in range(NZ) for x in range(nx)]

    def level_sign(level):
        return jnp.where((me_w >> level) & 1 == 1, -1.0, 1.0).astype(F32)

    def last_level(own, start, whole):
        partner = lax.ppermute(own, "wide", [(w, w ^ (wide // 2)) for w in range(wide)])
        own, whole = join_last(own, partner, level_sign(levels - 1), start, columns, whole)
        pieces = [own]
        for s in range(1, nx):
            pieces.append(lax.ppermute(own, "blk", x_shift(s)))
        return pieces, whole

    def first_levels(current, chunks):
        for level in range(levels - 1):
            partner = lax.ppermute(current, "wide", [(w, w ^ (1 << level)) for w in range(wide)])
            if level == levels - 2:
                return join_split(current, partner, level_sign(level), chunks)
            own = current.astype(F32)
            current = ((partner.astype(F32) + own * level_sign(level)) * SQRT_HALF).astype(BF16)

    mixed = mix_columns(signs, had, flux_rows, 0, 1)
    lead = first_levels(mixed, LEAD)
    counts = count_samples(sample_rows, sample_owner, nx, rows, me_z, me_x)
    owner_counts = [counts[0]]
    for s in range(1, nx):
        owner_counts.append(lax.ppermute(counts[s], "blk", x_shift(s)))
    mixed = mix_columns(signs, had, flux_rows, 1, columns // PANEL - 1)
    rest = first_levels(mixed, CHUNKS)

    lead_pieces, whole = [], None
    for i, (start, _) in enumerate(LEAD):
        pieces, whole = last_level(lead[i], start, whole)
        lead_pieces.append(pieces)
    sources = [[[pieces[p] for pieces in lead_pieces] for p in range(nx)]]
    for i, (start, _) in enumerate(CHUNKS):
        pieces, whole = last_level(rest[i], start, whole)
        sources.append([[piece] for piece in pieces])

    weights, grams = [], []
    for p in range(nx):
        weights.append(weigh(owner_counts[p], *sources[0][p]))
    for i in range(len(CHUNKS) + 1):
        keep, send = partial_grams(weights, sources[i], i == 0)
        near = lax.ppermute(send, "blk", z_route(1))
        onward = far_sum(keep, near)
        far = lax.ppermute(onward, "blk", z_route(2))
        grams.append((keep, near, far))
    state = factor_first(*grams[0], scale)
    sketch, inverse = factor_last(state, columns)
    for i, (start, _) in enumerate(CHUNKS):
        sketch = couple(inverse, *grams[i + 1], sketch, start, scale)
    return whole, sketch


def solution(mesh):
    placed = (
        P(("wide", "blk"), None),
        P(("wide", "blk")),
        P(("wide", "blk")),
        P(("wide", "blk"), None),
    )

    return jax.shard_map(
        per_device,
        mesh=mesh,
        in_specs=placed,
        out_specs=(P(("wide", "blk"), None), P(("wide", "blk"), None)),
        check_vma=False,
    )
```

```python
import functools

import jax
import jax.numpy as jnp
import numpy as np
from jax import lax
from jax.experimental import pallas as pl
from jax.experimental.pallas import tpu as pltpu
from jax.sharding import PartitionSpec as P

PANEL = 256
HB = 128
NZ = 4
PIECE = 128
GROUPS = (2, 3, 2, 1)
SQRT_HALF = 0.7071067811865476
HIGHEST = lax.Precision.HIGHEST
F32 = jnp.float32
BF16 = jnp.bfloat16


def hadamard_pair():
    idx = np.arange(HB)
    common = idx[:, None] & idx[None, :]
    parity = np.zeros_like(common)
    for bit in range(HB.bit_length() - 1):
        parity ^= (common >> bit) & 1
    one = 1.0 - 2.0 * parity
    return jnp.asarray(np.kron(np.eye(2), one), BF16)


VMEM_LIMIT = 24 << 20


def params(**kw):
    return pltpu.CompilerParams(vmem_limit_bytes=VMEM_LIMIT, **kw)


def cost(flops, moved):
    return pl.CostEstimate(flops=flops, bytes_accessed=moved, transcendentals=0)


def mix_kernel(signs_ref, had_ref, x_ref, *out_refs):
    rows = x_ref.shape[0]
    size = had_ref.shape[0]
    for which, out_ref in enumerate(out_refs):

        @pl.when(pl.program_id(0) == which)
        def _(out_ref=out_ref):
            for b in range(rows // size):
                part = pl.ds(b * size, size)
                signed = (had_ref[...].astype(F32) * signs_ref[:, b * size : (b + 1) * size].astype(F32)).astype(BF16)
                x = x_ref[part, :]
                hi = x.astype(BF16)
                rest = x - hi.astype(F32)
                mid = rest.astype(BF16)
                low = (rest - mid.astype(F32)).astype(BF16)
                total = jnp.dot(signed, low, preferred_element_type=F32)
                total = total + jnp.dot(signed, mid, preferred_element_type=F32)
                total = total + jnp.dot(signed, hi, preferred_element_type=F32)
                out_ref[part, :] = (total * (HB**-0.5)).astype(BF16)


def mix_columns(signs, had, flux, chunks):
    rows = flux.shape[0]
    start, width = chunks[0]
    first, count = start // width, len(chunks)
    return pl.pallas_call(
        mix_kernel,
        grid=(count,),
        in_specs=[
            pl.BlockSpec((1, rows), lambda i: (0, 0)),
            pl.BlockSpec(had.shape, lambda i: (0, 0)),
            pl.BlockSpec((rows, width), lambda i: (0, i + first)),
        ],
        out_specs=(pl.BlockSpec((rows, width), lambda i: (0, 0)),) * count,
        out_shape=(jax.ShapeDtypeStruct((rows, width), BF16),) * count,
        cost_estimate=cost(2 * count * rows * width * had.shape[0] * 3, count * rows * width * 6),
        name="mix",
    )(signs, had, flux)


def join_kernel(sign_ref, own_ref, other_ref, *refs):
    total = (other_ref[...].astype(F32) + own_ref[...].astype(F32) * sign_ref[0]) * SQRT_HALF
    total = total.astype(BF16)
    for ref in refs[-2:]:
        ref[...] = total


def join_last(own, other, sign, start, columns, whole):
    rows, width = own.shape
    block = start // width
    tile = rows // 2
    chunk = pl.BlockSpec((tile, width), lambda i: (i, 0))
    operands, specs, alias = [sign.reshape(1), own, other], [pl.BlockSpec(memory_space=pltpu.SMEM), chunk, chunk], {}
    if whole is not None:
        operands.append(whole)
        specs.append(pl.BlockSpec(memory_space=pltpu.HBM))
        alias = {3: 1}
    return pl.pallas_call(
        join_kernel,
        grid=(rows // tile,),
        in_specs=specs,
        out_specs=(chunk, pl.BlockSpec((tile, width), lambda i: (i, block))),
        out_shape=(jax.ShapeDtypeStruct((rows, width), BF16), jax.ShapeDtypeStruct((rows, columns), BF16)),
        input_output_aliases=alias,
        compiler_params=params(),
        cost_estimate=cost(4 * rows * width, 8 * rows * width),
        name="join",
    )(*operands)


def relative_owner(q):
    return ((q & 1) << 1) | (q >> 1)


def count_kernel(nx, me_ref, rows_ref, owner_ref, *out_refs):
    listed = rows_ref.shape[1]
    rows = out_refs[0].shape[1]
    me_z, me_x = me_ref[0], me_ref[1]
    index = lax.broadcasted_iota(jnp.int32, (NZ * nx, listed), 0)
    q, s = index & (NZ - 1), index >> (NZ.bit_length() - 1)
    z = me_z ^ relative_owner(q)
    x = (me_x + s) & (nx - 1)
    by_owner = (z * nx + x == owner_ref[...]).astype(F32).astype(BF16)
    by_row = (lax.broadcasted_iota(jnp.int32, (rows, listed), 0) == rows_ref[...]).astype(F32).astype(BF16)
    total = lax.dot_general(by_owner, by_row, (((1,), (1,)), ((), ())), preferred_element_type=F32)
    for shift, ref in enumerate(out_refs):
        ref[...] = total[shift * NZ : (shift + 1) * NZ, :]


def count_samples(sample_rows, sample_owner, nx, rows, me_z, me_x):
    listed = sample_rows.shape[0]
    shape = jax.ShapeDtypeStruct((NZ, rows), F32)
    vmem = pl.BlockSpec(memory_space=pltpu.VMEM)
    return pl.pallas_call(
        functools.partial(count_kernel, nx),
        in_specs=[pl.BlockSpec(memory_space=pltpu.SMEM), vmem, vmem],
        out_shape=(shape,) * nx,
        compiler_params=params(),
        cost_estimate=cost(2 * rows * listed * NZ * nx, rows * NZ * nx * 4),
        name="counts",
    )(jnp.stack([me_z, me_x]), sample_rows.reshape(1, listed), sample_owner.reshape(1, listed))


def weigh_kernel(counts_ref, left_ref, right_ref, hi_ref, lo_ref):
    lead = jnp.concatenate([left_ref[...].astype(F32).T, right_ref[...].astype(F32).T], axis=0)
    for q in range(NZ):
        part = pl.ds(q * PANEL, PANEL)
        weighed = lead * counts_ref[q : q + 1, :]
        hi = weighed.astype(BF16)
        hi_ref[part, :] = hi
        lo_ref[part, :] = (weighed - hi.astype(F32)).astype(BF16)


def weigh(counts, left, right):
    rows = left.shape[0]
    tile = rows // 2
    out = pl.BlockSpec((NZ * PANEL, tile), lambda i: (0, i))
    shape = jax.ShapeDtypeStruct((NZ * PANEL, rows), BF16)
    return pl.pallas_call(
        weigh_kernel,
        grid=(rows // tile,),
        in_specs=[pl.BlockSpec((NZ, tile), lambda i: (0, i))] + [pl.BlockSpec((tile, PANEL // 2), lambda i: (i, 0))] * 2,
        out_specs=(out, out),
        out_shape=(shape, shape),
        compiler_params=params(),
        cost_estimate=cost(rows * PANEL * 16, rows * PANEL * 18),
        name="weigh",
    )(counts, left, right)


GRAM_TILES = 2


def gram_kernel(parts, packed, each, *refs):
    refs, (acc,) = refs[:-1], refs[-1:]
    outs = refs[parts * each :]
    keep_ref, send_ref = (outs[0], outs[1]) if packed else (outs[1], outs[2])
    step = pl.program_id(0)

    @pl.when(step == 0)
    def _():
        acc[...] = jnp.zeros_like(acc)

    for p in range(parts):
        hi_ref, lo_ref, *rows_refs = refs[each * p : each * (p + 1)]

        @pl.when(step // GRAM_TILES == p)
        def _(hi_ref=hi_ref, lo_ref=lo_ref, rows_refs=rows_refs):
            rows = jnp.concatenate([ref[...] for ref in rows_refs], axis=1)
            low = jnp.dot(lo_ref[...], rows, preferred_element_type=F32)
            acc[...] += low + jnp.dot(hi_ref[...], rows, preferred_element_type=F32)

    @pl.when(step == parts * GRAM_TILES - 1)
    def _():
        half = PANEL // 2
        middle = NZ // 2 * PANEL
        if packed:
            for q in range(NZ):
                ref, place = (keep_ref, q) if q < NZ // 2 else (send_ref, q - NZ // 2)
                base, to = q * PANEL, place * 3 * half
                ref[to : to + PANEL, :] = acc[base : base + PANEL, :half]
                ref[to + PANEL : to + 3 * half, :] = acc[base + half : base + PANEL, half:]
        else:
            before_ref, rounded_ref, squares_ref = outs[0], outs[3], outs[4]
            keep_ref[...] = acc[:middle, :]
            send_ref[...] = acc[middle:, :]
            rounded_ref[...] = acc[middle:, :].astype(BF16)
            squares = (acc[...] * acc[...]).astype(BF16)
            ones = jnp.ones((8, squares.shape[1]), BF16)
            squares_ref[...] = before_ref[...] + lax.dot_general(
                ones, squares, (((1,), (1,)), ((), ())), preferred_element_type=F32
            )


def partial_grams(weights, chunk_rows, before):
    packed = before is None
    parts = len(chunk_rows)
    rows = chunk_rows[0][0].shape[0]
    width = sum(piece.shape[1] for piece in chunk_rows[0])
    tile = rows // GRAM_TILES
    half = NZ // 2
    shape = (half * (PANEL + PANEL // 2), PANEL // 2) if packed else (half * PANEL, width)
    operands, specs = [], []
    for p, ((hi, lo), pieces) in enumerate(zip(weights, chunk_rows)):
        operands += [hi, lo, *pieces]

        def place(k, p=p):
            return jnp.clip(k - p * GRAM_TILES, 0, GRAM_TILES - 1)

        weight_spec = pl.BlockSpec((NZ * PANEL, tile), lambda k, place=place: (0, place(k)))
        specs += [weight_spec, weight_spec]
        specs += [pl.BlockSpec((tile, piece.shape[1]), lambda k, place=place: (place(k), 0)) for piece in pieces]
    each = len(operands) // parts
    out = pl.BlockSpec(shape, lambda k: (0, 0))
    out_specs = [out, out]
    out_shape = [jax.ShapeDtypeStruct(shape, F32)] * 2
    if not packed:
        squares = pl.BlockSpec(before.shape, lambda k: (0, 0))
        operands.append(before)
        specs.append(squares)
        out_specs += [out, squares]
        out_shape += [jax.ShapeDtypeStruct(shape, BF16), jax.ShapeDtypeStruct(before.shape, F32)]
    return pl.pallas_call(
        functools.partial(gram_kernel, parts, packed, each),
        grid=(parts * GRAM_TILES,),
        in_specs=specs,
        out_specs=tuple(out_specs),
        out_shape=tuple(out_shape),
        scratch_shapes=[pltpu.VMEM((NZ * PANEL, width), F32)],
        compiler_params=params(),
        cost_estimate=cost(4 * parts * NZ * PANEL * rows * width, 4 * parts * NZ * PANEL * rows + 2 * parts * rows * width),
        name="grams",
    )(*operands)


def add_kernel(keep_ref, near_ref, out_ref):
    out_ref[...] = (keep_ref[...] + near_ref[...].astype(F32)).astype(out_ref.dtype)


def far_sum(keep, near):
    rows, width = keep.shape[0] // 2, keep.shape[1]
    spec = pl.BlockSpec((rows, width), lambda i: (1, 0))
    return pl.pallas_call(
        add_kernel,
        grid=(1,),
        in_specs=[spec, spec],
        out_specs=pl.BlockSpec((rows, width), lambda i: (0, 0)),
        out_shape=jax.ShapeDtypeStruct((rows, width), near.dtype),
        compiler_params=params(),
        cost_estimate=cost(rows * width, 12 * rows * width),
        name="add",
    )(keep, near)


BAND = 64
CUT = 2
MICRO = 8


def factor_band(tile):
    row_id = lax.broadcasted_iota(jnp.int32, (BAND, 1), 0)
    for first in range(0, BAND, MICRO):
        spread = [jnp.broadcast_to(tile[:, first + t : first + t + 1], tile.shape) for t in range(MICRO)]
        for t in range(MICRO):
            j = first + t
            r = lax.rsqrt(spread[t][j : j + 1, :])
            row = tile[j : j + 1, :] * r
            below = jnp.where(row_id > j, spread[t], 0.0)
            for u in range(t + 1, MICRO):
                spread[u] = spread[u] - below * (spread[u][j : j + 1, :] * (r * r))
            tile = jnp.where(row_id == j, row, tile - below * (row * r))
    return tile


def eliminate(work, first, last):
    rb = lax.broadcasted_iota(jnp.int32, (BAND, BAND), 0)
    cb = lax.broadcasted_iota(jnp.int32, (BAND, BAND), 1)
    eye_b = (rb == cb).astype(F32)
    for k in range(first, last):
        lo, hi = k * BAND, (k + 1) * BAND
        tile = factor_band(jnp.concatenate([work[lo:hi, lo:hi], eye_b], axis=1))
        inv = jnp.where(rb >= cb, tile[:, BAND:], 0.0)
        full = jnp.dot(inv, work[lo:hi, lo:], precision=HIGHEST, preferred_element_type=F32)
        if hi < PANEL:
            panel = full[:, BAND : PANEL - lo]
            work[hi:, hi:] = work[hi:, hi:] - lax.dot_general(
                panel, full[:, BAND:], (((0,), (0,)), ((), ())), precision=HIGHEST, preferred_element_type=F32
            )
        work[lo:hi, lo:] = full


def factor_first_kernel(scale, keep_ref, near_ref, far_ref, out_ref, work):
    half = PANEL // 2
    lead = (keep_ref[...] + near_ref[...] + far_ref[...]) * scale
    ri = lax.broadcasted_iota(jnp.int32, (PANEL, PANEL), 0)
    ci = lax.broadcasted_iota(jnp.int32, (PANEL, PANEL), 1)
    eye = (ri == ci).astype(F32)
    work[:, PANEL:] = eye
    work[:half, :half] = lead[:half, :] + 0.5 * eye[:half, :half]
    work[:half, half:PANEL] = lead[half:PANEL, :].T
    work[half:, :half] = lead[half:PANEL, :]
    work[half:, half:PANEL] = lead[PANEL:, :] + 0.5 * eye[:half, :half]
    eliminate(work, 0, CUT)
    out_ref[...] = work[...]


def factor_last_kernel(in_ref, out_ref, inverse_ref, norms_ref, work):
    work[...] = in_ref[...]
    eliminate(work, CUT, PANEL // BAND)
    ri = lax.broadcasted_iota(jnp.int32, (PANEL, PANEL), 0)
    ci = lax.broadcasted_iota(jnp.int32, (PANEL, PANEL), 1)
    upper = jnp.where(ci >= ri, work[:, :PANEL], 0.0)
    inverse = jnp.where(ri >= ci, work[:, PANEL:], 0.0)
    out_ref[...] = upper
    inverse_ref[...] = inverse
    norms_ref[:8, :] = jnp.broadcast_to(jnp.sum(inverse * inverse, axis=0, keepdims=True), (8, PANEL))
    norms_ref[8:, :] = jnp.broadcast_to(jnp.sum(upper * upper, axis=0, keepdims=True), (8, PANEL))


def factor_first(keep, near, far, scale):
    spec = pl.BlockSpec(far.shape, lambda i: (0, 0))
    shape = (PANEL, 2 * PANEL)
    return pl.pallas_call(
        functools.partial(factor_first_kernel, scale),
        grid=(1,),
        in_specs=[spec, spec, spec],
        out_specs=pl.BlockSpec(shape, lambda i: (0, 0)),
        out_shape=jax.ShapeDtypeStruct(shape, F32),
        scratch_shapes=[pltpu.VMEM(shape, F32)],
        compiler_params=params(),
        cost_estimate=cost(10_000_000_000, 1 << 20),
        name="factor_first",
    )(keep, near, far)


def factor_last(state, columns):
    square = pl.BlockSpec((PANEL, PANEL), lambda i: (0, 0))
    return pl.pallas_call(
        factor_last_kernel,
        grid=(1,),
        in_specs=[pl.BlockSpec(state.shape, lambda i: (0, 0))],
        out_specs=(square, square, pl.BlockSpec((16, PANEL), lambda i: (0, 0))),
        out_shape=(
            jax.ShapeDtypeStruct((PANEL, columns), F32),
            jax.ShapeDtypeStruct((PANEL, PANEL), F32),
            jax.ShapeDtypeStruct((16, PANEL), F32),
        ),
        scratch_shapes=[pltpu.VMEM(state.shape, F32)],
        cost_estimate=cost(10_000_000_000, 1 << 20),
        name="factor_last",
    )(state)


def couple_kernel(scale, inverse_ref, keep_ref, near_ref, far_ref, whole_ref, out_ref):
    gram = (keep_ref[...] + near_ref[...].astype(F32) + far_ref[...].astype(F32)) * scale
    out_ref[...] = jnp.dot(inverse_ref[...], gram, precision=HIGHEST, preferred_element_type=F32)


def couple(inverse, keep, near, far, whole, start, scale):
    rows, width = far.shape
    block = start // PIECE
    spec = pl.BlockSpec((rows, PIECE), lambda i: (0, i))
    return pl.pallas_call(
        functools.partial(couple_kernel, scale),
        grid=(width // PIECE,),
        in_specs=[pl.BlockSpec(inverse.shape, lambda i: (0, 0)), spec, spec, spec, pl.BlockSpec(memory_space=pltpu.HBM)],
        out_specs=pl.BlockSpec((rows, PIECE), lambda i: (0, block + i)),
        out_shape=jax.ShapeDtypeStruct(whole.shape, F32),
        input_output_aliases={4: 0},
        cost_estimate=cost(12 * PANEL * rows * width, 20 * rows * width),
        name="couple",
    )(inverse, keep, near, far, whole)


ROUNDING = 0.6 * 2.0**-8
LIMIT = 0.004


def judge_kernel(scale, *refs):
    norms_refs, squares_refs, out_ref = refs[:NZ], refs[NZ : 2 * NZ], refs[-1]
    worst = jnp.zeros((8, 1), F32)
    for owner in range(NZ):
        terms = []
        for sender in range(NZ):
            apart = owner ^ sender
            place = relative_owner(apart) * PANEL
            terms.append(squares_refs[sender][:, place : place + PANEL] * float(apart))
        total = (terms[0] + terms[1]) + (terms[2] + terms[3])
        error = jnp.sum(norms_refs[owner][:8, :] * total, axis=1, keepdims=True) * (ROUNDING * scale) ** 2
        size = jnp.sum(norms_refs[owner][8:, :], axis=1, keepdims=True) * LIMIT**2
        worst = jnp.maximum(worst, jnp.where(error <= size, 0.0, 1.0))
    out_ref[0] = jnp.max(worst).astype(jnp.int32)


def judge(norms, squares, scale):
    vmem = pl.BlockSpec(memory_space=pltpu.VMEM)
    return pl.pallas_call(
        functools.partial(judge_kernel, scale),
        in_specs=[vmem] * (2 * NZ),
        out_specs=pl.BlockSpec(memory_space=pltpu.SMEM),
        out_shape=jax.ShapeDtypeStruct((1,), jnp.int32),
        name="judge",
    )(*norms, *squares)


def per_device(flux_rows, row_signs, sample_rows, sample_owner):
    wide, blk = lax.axis_size("wide"), lax.axis_size("blk")
    nx = blk // NZ
    rows, columns = flux_rows.shape
    scale = 1.0 / sample_rows.shape[0]
    me_w, me_b = lax.axis_index("wide"), lax.axis_index("blk")
    me_x, me_z = me_b & (nx - 1), me_b >> (nx.bit_length() - 1)
    had = hadamard_pair()
    signs = row_signs.reshape(1, rows)
    levels = wide.bit_length() - 1

    def at(z, x):
        return z * nx + x

    def z_route(mask):
        return [(at(z, x), at(z ^ mask, x)) for z in range(NZ) for x in range(nx)]

    def x_shift(s):
        return [(at(z, x), at(z, (x + s) % nx)) for z in range(NZ) for x in range(nx)]

    def level_sign(level):
        return jnp.where((me_w >> level) & 1 == 1, -1.0, 1.0).astype(F32)

    def last_level(own, start, whole):
        partner = lax.ppermute(own, "wide", [(w, w ^ (wide // 2)) for w in range(wide)])
        own, whole = join_last(own, partner, level_sign(levels - 1), start, columns, whole)
        pieces = [own]
        for s in range(1, nx):
            pieces.append(lax.ppermute(own, "blk", x_shift(s)))
        return pieces, whole

    def cut(mixed):
        for level in range(levels - 1):
            partner = lax.ppermute(mixed, "wide", [(w, w ^ (1 << level)) for w in range(wide)])
            halves = []
            for half in range(PANEL // PIECE if level == levels - 2 else 1):
                part = slice(half * PIECE, (half + 1) * PIECE) if level == levels - 2 else slice(None)
                own = mixed[:, part].astype(F32)
                other = partner[:, part].astype(F32)
                halves.append(((other + own * level_sign(level)) * SQRT_HALF).astype(BF16))
            mixed = halves[0]
        return halves

    blocks = [(start, PANEL) for start in range(0, columns, PANEL)]
    mixed = [*mix_columns(signs, had, flux_rows, blocks[:1])]
    counts = count_samples(sample_rows, sample_owner, nx, rows, me_z, me_x)
    owner_counts = [counts[0]]
    for s in range(1, nx):
        owner_counts.append(lax.ppermute(counts[s], "blk", x_shift(s)))
    mixed += mix_columns(signs, had, flux_rows, blocks[1:])
    moved = [half for block in mixed for half in cut(block)]
    pieces, whole = [], None
    for tag, piece in enumerate(moved):
        piece, whole = last_level(piece, tag * PIECE, whole)
        pieces.append(piece)

    weights, grams, precise, starts = [], [], [], []
    squares = jnp.zeros((8, NZ * PANEL), F32)
    done = 0
    for i, count in enumerate(GROUPS):
        sources = [[piece[p] for piece in pieces[done : done + count]] for p in range(nx)]
        if i == 0:
            for p in range(nx):
                weights.append(weigh(owner_counts[p], *sources[p]))
        if i == 0:
            keep, send = partial_grams(weights, sources, None)
        else:
            keep, exact, send, squares = partial_grams(weights, sources, squares)
            precise.append((keep, exact))
            starts.append(done * PIECE)
        near = lax.ppermute(send, "blk", z_route(1))
        onward = far_sum(keep, near)
        far = lax.ppermute(onward, "blk", z_route(2))
        grams.append((keep, near, far))
        done += count
    state = factor_first(*grams[0], scale)
    sketch, inverse, norms = factor_last(state, columns)
    line_norms, line_squares = [norms], [squares]
    for mask in range(1, NZ):
        line_norms.append(lax.ppermute(norms, "blk", z_route(mask)))
        line_squares.append(lax.ppermute(squares, "blk", z_route(mask)))
    redo = judge(line_norms, line_squares, scale)[0] != 0
    for i, start in enumerate(starts[:-1]):
        sketch = couple(inverse, *grams[i + 1], sketch, start, scale)

    def rounded(sketch, inverse, last, precise):
        return couple(inverse, *last, sketch, starts[-1], scale)

    def exact(sketch, inverse, last, precise):
        for (keep, send), start in zip(precise, starts):
            near = lax.ppermute(send, "blk", z_route(1))
            far = lax.ppermute(far_sum(keep, near), "blk", z_route(2))
            sketch = couple(inverse, keep, near, far, sketch, start, scale)
        return sketch

    sketch = lax.cond(redo, exact, rounded, sketch, inverse, grams[-1], precise)
    return whole, sketch


def solution(mesh):
    placed = (
        P(("wide", "blk"), None),
        P(("wide", "blk")),
        P(("wide", "blk")),
        P(("wide", "blk"), None),
    )

    return jax.shard_map(
        per_device,
        mesh=mesh,
        in_specs=placed,
        out_specs=(P(("wide", "blk"), None), P(("wide", "blk"), None)),
        check_vma=False,
    )
```

```python
import functools

import jax
import jax.numpy as jnp
import numpy as np
from jax import lax
from jax.experimental import pallas as pl
from jax.experimental.pallas import tpu as pltpu
from jax.sharding import PartitionSpec as P

PANEL = 256
HB = 128
NZ = 4
PIECE = 128
SQRT_HALF = 0.7071067811865476
HIGHEST = lax.Precision.HIGHEST
F32 = jnp.float32
BF16 = jnp.bfloat16


def hadamard_pair():
    idx = np.arange(HB)
    common = idx[:, None] & idx[None, :]
    parity = np.zeros_like(common)
    for bit in range(HB.bit_length() - 1):
        parity ^= (common >> bit) & 1
    one = 1.0 - 2.0 * parity
    return jnp.asarray(np.kron(np.eye(2), one), BF16)


VMEM_LIMIT = 24 << 20


def params(**kw):
    return pltpu.CompilerParams(vmem_limit_bytes=VMEM_LIMIT, **kw)


def cost(flops, moved):
    return pl.CostEstimate(flops=flops, bytes_accessed=moved, transcendentals=0)


def mix_kernel(signs_ref, had_ref, x_ref, *out_refs):
    rows = x_ref.shape[0]
    size = had_ref.shape[0]
    for which, out_ref in enumerate(out_refs):

        @pl.when(pl.program_id(0) == which)
        def _(out_ref=out_ref):
            for b in range(rows // size):
                part = pl.ds(b * size, size)
                signed = (had_ref[...].astype(F32) * signs_ref[:, b * size : (b + 1) * size].astype(F32)).astype(BF16)
                x = x_ref[part, :]
                hi = x.astype(BF16)
                rest = x - hi.astype(F32)
                mid = rest.astype(BF16)
                low = (rest - mid.astype(F32)).astype(BF16)
                total = jnp.dot(signed, low, preferred_element_type=F32)
                total = total + jnp.dot(signed, mid, preferred_element_type=F32)
                total = total + jnp.dot(signed, hi, preferred_element_type=F32)
                out_ref[part, :] = (total * (HB**-0.5)).astype(BF16)


def mix_columns(signs, had, flux, chunks):
    rows = flux.shape[0]
    start, width = chunks[0]
    first, count = start // width, len(chunks)
    return pl.pallas_call(
        mix_kernel,
        grid=(count,),
        in_specs=[
            pl.BlockSpec((1, rows), lambda i: (0, 0)),
            pl.BlockSpec(had.shape, lambda i: (0, 0)),
            pl.BlockSpec((rows, width), lambda i: (0, i + first)),
        ],
        out_specs=(pl.BlockSpec((rows, width), lambda i: (0, 0)),) * count,
        out_shape=(jax.ShapeDtypeStruct((rows, width), BF16),) * count,
        cost_estimate=cost(2 * count * rows * width * had.shape[0] * 3, count * rows * width * 6),
        name="mix",
    )(signs, had, flux)


def join_kernel(sign_ref, own_ref, other_ref, *refs):
    total = (other_ref[...].astype(F32) + own_ref[...].astype(F32) * sign_ref[0]) * SQRT_HALF
    total = total.astype(BF16)
    for ref in refs[-2:]:
        ref[...] = total


def join_last(own, other, sign, start, columns, whole):
    rows, width = own.shape
    block = start // width
    tile = rows // 2
    chunk = pl.BlockSpec((tile, width), lambda i: (i, 0))
    operands, specs, alias = [sign.reshape(1), own, other], [pl.BlockSpec(memory_space=pltpu.SMEM), chunk, chunk], {}
    if whole is not None:
        operands.append(whole)
        specs.append(pl.BlockSpec(memory_space=pl.ANY))
        alias = {3: 1}
    return pl.pallas_call(
        join_kernel,
        grid=(rows // tile,),
        in_specs=specs,
        out_specs=(chunk, pl.BlockSpec((tile, width), lambda i: (i, block))),
        out_shape=(jax.ShapeDtypeStruct((rows, width), BF16), jax.ShapeDtypeStruct((rows, columns), BF16)),
        input_output_aliases=alias,
        compiler_params=params(),
        cost_estimate=cost(4 * rows * width, 8 * rows * width),
        name="join",
    )(*operands)


def relative_owner(q):
    return ((q & 1) << 1) | (q >> 1)


def count_kernel(nx, me_ref, rows_ref, owner_ref, *out_refs):
    listed = rows_ref.shape[1]
    rows = out_refs[0].shape[1]
    me_z, me_x = me_ref[0], me_ref[1]
    index = lax.broadcasted_iota(jnp.int32, (NZ * nx, listed), 0)
    q, s = index & (NZ - 1), index >> (NZ.bit_length() - 1)
    z = me_z ^ relative_owner(q)
    x = (me_x + s) & (nx - 1)
    by_owner = (z * nx + x == owner_ref[...]).astype(F32).astype(BF16)
    by_row = (lax.broadcasted_iota(jnp.int32, (rows, listed), 0) == rows_ref[...]).astype(F32).astype(BF16)
    total = lax.dot_general(by_owner, by_row, (((1,), (1,)), ((), ())), preferred_element_type=F32)
    for shift, ref in enumerate(out_refs):
        ref[...] = total[shift * NZ : (shift + 1) * NZ, :]


def count_samples(sample_rows, sample_owner, nx, rows, me_z, me_x):
    listed = sample_rows.shape[0]
    shape = jax.ShapeDtypeStruct((NZ, rows), F32)
    vmem = pl.BlockSpec(memory_space=pltpu.VMEM)
    return pl.pallas_call(
        functools.partial(count_kernel, nx),
        in_specs=[pl.BlockSpec(memory_space=pltpu.SMEM), vmem, vmem],
        out_shape=(shape,) * nx,
        compiler_params=params(),
        cost_estimate=cost(2 * rows * listed * NZ * nx, rows * NZ * nx * 4),
        name="counts",
    )(jnp.stack([me_z, me_x]), sample_rows.reshape(1, listed), sample_owner.reshape(1, listed))


def weigh_kernel(counts_ref, left_ref, right_ref, hi_ref, lo_ref):
    lead = jnp.concatenate([left_ref[...].astype(F32).T, right_ref[...].astype(F32).T], axis=0)
    for q in range(NZ):
        part = pl.ds(q * PANEL, PANEL)
        weighed = lead * counts_ref[q : q + 1, :]
        hi = weighed.astype(BF16)
        hi_ref[part, :] = hi
        lo_ref[part, :] = (weighed - hi.astype(F32)).astype(BF16)


def weigh(counts, left, right):
    rows = left.shape[0]
    tile = rows // 2
    out = pl.BlockSpec((NZ * PANEL, tile), lambda i: (0, i))
    shape = jax.ShapeDtypeStruct((NZ * PANEL, rows), BF16)
    return pl.pallas_call(
        weigh_kernel,
        grid=(rows // tile,),
        in_specs=[pl.BlockSpec((NZ, tile), lambda i: (0, i))] + [pl.BlockSpec((tile, PANEL // 2), lambda i: (i, 0))] * 2,
        out_specs=(out, out),
        out_shape=(shape, shape),
        compiler_params=params(),
        cost_estimate=cost(rows * PANEL * 16, rows * PANEL * 18),
        name="weigh",
    )(counts, left, right)


GRAM_TILES = 2


def gram_kernel(parts, packed, each, *refs):
    refs, (acc,) = refs[:-1], refs[-1:]
    outs = refs[parts * each :]
    keep_ref, send_ref = (outs[0], outs[1]) if packed else (outs[1], outs[2])
    step = pl.program_id(0)

    @pl.when(step == 0)
    def _():
        acc[...] = jnp.zeros_like(acc)

    for p in range(parts):
        hi_ref, lo_ref, *rows_refs = refs[each * p : each * (p + 1)]

        @pl.when(step // GRAM_TILES == p)
        def _(hi_ref=hi_ref, lo_ref=lo_ref, rows_refs=rows_refs):
            rows = jnp.concatenate([ref[...] for ref in rows_refs], axis=1)
            low = jnp.dot(lo_ref[...], rows, preferred_element_type=F32)
            acc[...] += low + jnp.dot(hi_ref[...], rows, preferred_element_type=F32)

    @pl.when(step == parts * GRAM_TILES - 1)
    def _():
        half = PANEL // 2
        middle = NZ // 2 * PANEL
        if packed:
            for q in range(NZ):
                ref, place = (keep_ref, q) if q < NZ // 2 else (send_ref, q - NZ // 2)
                base, to = q * PANEL, place * 3 * half
                ref[to : to + PANEL, :] = acc[base : base + PANEL, :half]
                ref[to + PANEL : to + 3 * half, :] = acc[base + half : base + PANEL, half:]
        else:
            before_ref, rounded_ref, squares_ref = outs[0], outs[3], outs[4]
            keep_ref[...] = acc[:middle, :]
            send_ref[...] = acc[middle:, :]
            rounded_ref[...] = acc[middle:, :].astype(BF16)
            squares = (acc[...] * acc[...]).astype(BF16)
            ones = jnp.ones((8, squares.shape[1]), BF16)
            squares_ref[...] = before_ref[...] + lax.dot_general(
                ones, squares, (((1,), (1,)), ((), ())), preferred_element_type=F32
            )


def partial_grams(weights, chunk_rows, before):
    packed = before is None
    parts = len(chunk_rows)
    rows = chunk_rows[0][0].shape[0]
    width = sum(piece.shape[1] for piece in chunk_rows[0])
    tile = rows // GRAM_TILES
    half = NZ // 2
    shape = (half * (PANEL + PANEL // 2), PANEL // 2) if packed else (half * PANEL, width)
    operands, specs = [], []
    for p, ((hi, lo), pieces) in enumerate(zip(weights, chunk_rows)):
        operands += [hi, lo, *pieces]

        def place(k, p=p):
            return jnp.clip(k - p * GRAM_TILES, 0, GRAM_TILES - 1)

        weight_spec = pl.BlockSpec((NZ * PANEL, tile), lambda k, place=place: (0, place(k)))
        specs += [weight_spec, weight_spec]
        specs += [pl.BlockSpec((tile, piece.shape[1]), lambda k, place=place: (place(k), 0)) for piece in pieces]
    each = len(operands) // parts
    out = pl.BlockSpec(shape, lambda k: (0, 0))
    out_specs = [out, out]
    out_shape = [jax.ShapeDtypeStruct(shape, F32)] * 2
    if not packed:
        squares = pl.BlockSpec(before.shape, lambda k: (0, 0))
        operands.append(before)
        specs.append(squares)
        out_specs += [out, squares]
        out_shape += [jax.ShapeDtypeStruct(shape, BF16), jax.ShapeDtypeStruct(before.shape, F32)]
    return pl.pallas_call(
        functools.partial(gram_kernel, parts, packed, each),
        grid=(parts * GRAM_TILES,),
        in_specs=specs,
        out_specs=tuple(out_specs),
        out_shape=tuple(out_shape),
        scratch_shapes=[pltpu.VMEM((NZ * PANEL, width), F32)],
        compiler_params=params(),
        cost_estimate=cost(4 * parts * NZ * PANEL * rows * width, 4 * parts * NZ * PANEL * rows + 2 * parts * rows * width),
        name="grams",
    )(*operands)


def add_kernel(keep_ref, near_ref, out_ref):
    out_ref[...] = (keep_ref[...] + near_ref[...].astype(F32)).astype(out_ref.dtype)


def far_sum(keep, near):
    rows, width = keep.shape[0] // 2, keep.shape[1]
    spec = pl.BlockSpec((rows, width), lambda i: (1, 0))
    return pl.pallas_call(
        add_kernel,
        grid=(1,),
        in_specs=[spec, spec],
        out_specs=pl.BlockSpec((rows, width), lambda i: (0, 0)),
        out_shape=jax.ShapeDtypeStruct((rows, width), near.dtype),
        compiler_params=params(),
        cost_estimate=cost(rows * width, 12 * rows * width),
        name="add",
    )(keep, near)


BAND = 64
CUT = 2
MICRO = 8


def factor_band(tile):
    row_id = lax.broadcasted_iota(jnp.int32, (BAND, 1), 0)
    for first in range(0, BAND, MICRO):
        spread = [jnp.broadcast_to(tile[:, first + t : first + t + 1], tile.shape) for t in range(MICRO)]
        for t in range(MICRO):
            j = first + t
            r = lax.rsqrt(spread[t][j : j + 1, :])
            row = tile[j : j + 1, :] * r
            below = jnp.where(row_id > j, spread[t], 0.0)
            for u in range(t + 1, MICRO):
                spread[u] = spread[u] - below * (spread[u][j : j + 1, :] * (r * r))
            tile = jnp.where(row_id == j, row, tile - below * (row * r))
    return tile


def eliminate(work, first, last):
    rb = lax.broadcasted_iota(jnp.int32, (BAND, BAND), 0)
    cb = lax.broadcasted_iota(jnp.int32, (BAND, BAND), 1)
    eye_b = (rb == cb).astype(F32)
    for k in range(first, last):
        lo, hi = k * BAND, (k + 1) * BAND
        tile = factor_band(jnp.concatenate([work[lo:hi, lo:hi], eye_b], axis=1))
        inv = jnp.where(rb >= cb, tile[:, BAND:], 0.0)
        full = jnp.dot(inv, work[lo:hi, lo:], precision=HIGHEST, preferred_element_type=F32)
        if hi < PANEL:
            panel = full[:, BAND : PANEL - lo]
            work[hi:, hi:] = work[hi:, hi:] - lax.dot_general(
                panel, full[:, BAND:], (((0,), (0,)), ((), ())), precision=HIGHEST, preferred_element_type=F32
            )
        work[lo:hi, lo:] = full


def factor_first_kernel(scale, keep_ref, near_ref, far_ref, out_ref, work):
    half = PANEL // 2
    lead = (keep_ref[...] + near_ref[...] + far_ref[...]) * scale
    ri = lax.broadcasted_iota(jnp.int32, (PANEL, PANEL), 0)
    ci = lax.broadcasted_iota(jnp.int32, (PANEL, PANEL), 1)
    eye = (ri == ci).astype(F32)
    work[:, PANEL:] = eye
    work[:half, :half] = lead[:half, :] + 0.5 * eye[:half, :half]
    work[:half, half:PANEL] = lead[half:PANEL, :].T
    work[half:, :half] = lead[half:PANEL, :]
    work[half:, half:PANEL] = lead[PANEL:, :] + 0.5 * eye[:half, :half]
    eliminate(work, 0, CUT)
    out_ref[...] = work[...]


def factor_last_kernel(in_ref, squares_ref, out_ref, inverse_ref, guard_ref, work):
    work[...] = in_ref[...]
    eliminate(work, CUT, PANEL // BAND)
    ri = lax.broadcasted_iota(jnp.int32, (PANEL, PANEL), 0)
    ci = lax.broadcasted_iota(jnp.int32, (PANEL, PANEL), 1)
    upper = jnp.where(ci >= ri, work[:, :PANEL], 0.0)
    inverse = jnp.where(ri >= ci, work[:, PANEL:], 0.0)
    out_ref[...] = upper
    inverse_ref[...] = inverse
    guard_ref[:, : NZ * PANEL] = squares_ref[...]
    for place, part in enumerate((inverse, upper)):
        start = (NZ + place) * PANEL
        norms = jnp.sum(part * part, axis=0, keepdims=True)
        guard_ref[:, start : start + PANEL] = jnp.broadcast_to(norms, (8, PANEL))


def factor_first(keep, near, far, scale):
    spec = pl.BlockSpec(far.shape, lambda i: (0, 0))
    shape = (PANEL, 2 * PANEL)
    return pl.pallas_call(
        functools.partial(factor_first_kernel, scale),
        grid=(1,),
        in_specs=[spec, spec, spec],
        out_specs=pl.BlockSpec(shape, lambda i: (0, 0)),
        out_shape=jax.ShapeDtypeStruct(shape, F32),
        scratch_shapes=[pltpu.VMEM(shape, F32)],
        compiler_params=params(),
        cost_estimate=cost(10_000_000_000, 1 << 20),
        name="factor_first",
    )(keep, near, far)


def factor_last(state, squares, columns):
    def resident(shape):
        return pl.BlockSpec(shape, lambda i: (0, 0))

    square, guard = (PANEL, PANEL), (8, (NZ + 2) * PANEL)
    return pl.pallas_call(
        factor_last_kernel,
        grid=(1,),
        in_specs=[resident(state.shape), resident(squares.shape)],
        out_specs=(resident(square), resident(square), resident(guard)),
        out_shape=(
            jax.ShapeDtypeStruct((PANEL, columns), F32),
            jax.ShapeDtypeStruct(square, F32),
            jax.ShapeDtypeStruct(guard, F32),
        ),
        scratch_shapes=[pltpu.VMEM(state.shape, F32)],
        compiler_params=params(),
        cost_estimate=cost(10_000_000_000, 1 << 20),
        name="factor_last",
    )(state, squares)


def couple_kernel(scale, inverse_ref, keep_ref, near_ref, far_ref, whole_ref, out_ref):
    gram = (keep_ref[...] + near_ref[...].astype(F32) + far_ref[...].astype(F32)) * scale
    out_ref[...] = jnp.dot(inverse_ref[...], gram, precision=HIGHEST, preferred_element_type=F32)


def couple(inverse, keep, near, far, whole, start, scale):
    rows, width = far.shape
    block = start // width
    spec = pl.BlockSpec((rows, width), lambda i: (0, 0))
    return pl.pallas_call(
        functools.partial(couple_kernel, scale),
        grid=(1,),
        in_specs=[pl.BlockSpec(inverse.shape, lambda i: (0, 0)), spec, spec, spec, pl.BlockSpec(memory_space=pl.ANY)],
        out_specs=pl.BlockSpec((rows, width), lambda i: (0, block)),
        out_shape=jax.ShapeDtypeStruct(whole.shape, F32),
        input_output_aliases={4: 0},
        compiler_params=params(),
        cost_estimate=cost(12 * PANEL * rows * width, 20 * rows * width),
        name="couple",
    )(inverse, keep, near, far, whole)


ROUNDING = 0.6 * 2.0**-8
LIMIT = 0.004


def judge_kernel(scale, *refs):
    *guards, out_ref = refs
    worst = jnp.zeros((8, 1), F32)
    for owner in range(NZ):
        terms = []
        for sender in range(NZ):
            apart = owner ^ sender
            place = relative_owner(apart) * PANEL
            terms.append(guards[sender][:, place : place + PANEL] * float(apart))
        total = (terms[0] + terms[1]) + (terms[2] + terms[3])
        inverse_norms = guards[owner][:, NZ * PANEL : (NZ + 1) * PANEL]
        upper_norms = guards[owner][:, (NZ + 1) * PANEL :]
        error = jnp.sum(inverse_norms * total, axis=1, keepdims=True) * (ROUNDING * scale) ** 2
        size = jnp.sum(upper_norms, axis=1, keepdims=True) * LIMIT**2
        worst = jnp.maximum(worst, jnp.where(error <= size, 0.0, 1.0))
    out_ref[0] = jnp.max(worst).astype(jnp.int32)


def judge(guards, scale):
    spec = pl.BlockSpec(guards[0].shape, lambda i: (0, 0))
    return pl.pallas_call(
        functools.partial(judge_kernel, scale),
        grid=(1,),
        in_specs=[spec] * NZ,
        out_specs=pl.BlockSpec(memory_space=pltpu.SMEM),
        out_shape=jax.ShapeDtypeStruct((1,), jnp.int32),
        name="judge",
    )(*guards)


def per_device(flux_rows, row_signs, sample_rows, sample_owner):
    wide, blk = lax.axis_size("wide"), lax.axis_size("blk")
    nx = blk // NZ
    rows, columns = flux_rows.shape
    scale = 1.0 / sample_rows.shape[0]
    me_w, me_b = lax.axis_index("wide"), lax.axis_index("blk")
    me_x, me_z = me_b & (nx - 1), me_b >> (nx.bit_length() - 1)
    had = hadamard_pair()
    signs = row_signs.reshape(1, rows)
    levels = wide.bit_length() - 1

    def at(z, x):
        return z * nx + x

    def z_route(mask):
        return [(at(z, x), at(z ^ mask, x)) for z in range(NZ) for x in range(nx)]

    def x_shift(s):
        return [(at(z, x), at(z, (x + s) % nx)) for z in range(NZ) for x in range(nx)]

    def level_sign(level):
        return jnp.where((me_w >> level) & 1 == 1, -1.0, 1.0).astype(F32)

    def last_level(own, start, whole):
        partner = lax.ppermute(own, "wide", [(w, w ^ (wide // 2)) for w in range(wide)])
        own, whole = join_last(own, partner, level_sign(levels - 1), start, columns, whole)
        pieces = [own]
        for s in range(1, nx):
            pieces.append(lax.ppermute(own, "blk", x_shift(s)))
        return pieces, whole

    def level_up(level, own, partner):
        total = (partner.astype(F32) + own.astype(F32) * level_sign(level)) * SQRT_HALF
        return total.astype(BF16)

    def first_levels(mixed, last=levels - 1):
        for level in range(last):
            partner = lax.ppermute(mixed, "wide", [(w, w ^ (1 << level)) for w in range(wide)])
            mixed = level_up(level, mixed, partner)
        return mixed

    def cut_lead(mixed):
        mixed = first_levels(mixed, levels - 2)
        partner = lax.ppermute(mixed, "wide", [(w, w ^ (1 << (levels - 2))) for w in range(wide)])
        cuts = [slice(start, start + PIECE) for start in range(0, PANEL, PIECE)]
        return [level_up(levels - 2, mixed[:, cut], partner[:, cut]) for cut in cuts]

    blocks = [(start, PANEL) for start in range(0, columns, PANEL)]
    mixed = [*mix_columns(signs, had, flux_rows, blocks[:1])]
    counts = count_samples(sample_rows, sample_owner, nx, rows, me_z, me_x)
    owner_counts = [counts[0]]
    for s in range(1, nx):
        owner_counts.append(lax.ppermute(counts[s], "blk", x_shift(s)))
    mixed += mix_columns(signs, had, flux_rows, blocks[1:])
    pieces, whole, place = [], None, 0
    for piece in cut_lead(mixed[0]) + [first_levels(block) for block in mixed[1:]]:
        piece, whole = last_level(piece, place, whole)
        place += piece[0].shape[1]
        pieces.append(piece)
    groups = [[[pieces[0][p], pieces[1][p]] for p in range(nx)]] + [[[piece[p]] for p in range(nx)] for piece in pieces[2:]]

    weights, grams, precise = [], [], []
    squares = jnp.zeros((8, NZ * PANEL), F32)
    for i, sources in enumerate(groups):
        if i == 0:
            for p in range(nx):
                weights.append(weigh(owner_counts[p], *sources[p]))
        if i == 0:
            keep, send = partial_grams(weights, sources, None)
        else:
            keep, exact_send, send, squares = partial_grams(weights, sources, squares)
            precise.append((keep, exact_send))
        near = lax.ppermute(send, "blk", z_route(1))
        onward = far_sum(keep, near)
        far = lax.ppermute(onward, "blk", z_route(2))
        grams.append((keep, near, far))
    state = factor_first(*grams[0], scale)
    sketch, inverse, guard = factor_last(state, squares, columns)
    guards = [guard]
    for mask in range(1, NZ):
        guards.append(lax.ppermute(guard, "blk", z_route(mask)))
    redo = judge(guards, scale)[0] != 0
    for i in range(1, len(groups) - 1):
        sketch = couple(inverse, *grams[i], sketch, i * PANEL, scale)

    def rounded(sketch, inverse, last, precise):
        return couple(inverse, *last, sketch, columns - PANEL, scale)

    def exact(sketch, inverse, last, precise):
        for i, (keep, send) in enumerate(precise):
            near = lax.ppermute(send, "blk", z_route(1))
            far = lax.ppermute(far_sum(keep, near), "blk", z_route(2))
            sketch = couple(inverse, keep, near, far, sketch, (i + 1) * PANEL, scale)
        return sketch

    sketch = lax.cond(redo, exact, rounded, sketch, inverse, grams[-1], precise)
    return whole, sketch


def solution(mesh):
    placed = (
        P(("wide", "blk"), None),
        P(("wide", "blk")),
        P(("wide", "blk")),
        P(("wide", "blk"), None),
    )

    return jax.shard_map(
        per_device,
        mesh=mesh,
        in_specs=placed,
        out_specs=(P(("wide", "blk"), None), P(("wide", "blk"), None)),
        check_vma=False,
    )
```

```python
import functools

import jax
import jax.numpy as jnp
import numpy as np
from jax import lax
from jax.experimental import pallas as pl
from jax.experimental.pallas import tpu as pltpu
from jax.sharding import PartitionSpec as P

PANEL = 256
HB = 128
NZ = 4
PIECE = 128
SQRT_HALF = 0.7071067811865476
HIGHEST = lax.Precision.HIGHEST
F32 = jnp.float32
BF16 = jnp.bfloat16


def hadamard_pair():
    idx = np.arange(HB)
    common = idx[:, None] & idx[None, :]
    parity = np.zeros_like(common)
    for bit in range(HB.bit_length() - 1):
        parity ^= (common >> bit) & 1
    one = 1.0 - 2.0 * parity
    return jnp.asarray(np.kron(np.eye(2), one), BF16)


VMEM_LIMIT = 24 << 20


def params(**kw):
    return pltpu.CompilerParams(vmem_limit_bytes=VMEM_LIMIT, **kw)


def cost(flops, moved):
    return pl.CostEstimate(flops=flops, bytes_accessed=moved, transcendentals=0)


def mix_kernel(signs_ref, had_ref, x_ref, *out_refs):
    rows = x_ref.shape[0]
    size = had_ref.shape[0]
    for which, out_ref in enumerate(out_refs):

        @pl.when(pl.program_id(0) == which)
        def _(out_ref=out_ref):
            for b in range(rows // size):
                part = pl.ds(b * size, size)
                signed = (had_ref[...].astype(F32) * signs_ref[:, b * size : (b + 1) * size].astype(F32)).astype(BF16)
                x = x_ref[part, :]
                hi = x.astype(BF16)
                rest = x - hi.astype(F32)
                mid = rest.astype(BF16)
                low = (rest - mid.astype(F32)).astype(BF16)
                total = jnp.dot(signed, low, preferred_element_type=F32)
                total = total + jnp.dot(signed, mid, preferred_element_type=F32)
                total = total + jnp.dot(signed, hi, preferred_element_type=F32)
                out_ref[part, :] = (total * (HB**-0.5)).astype(BF16)


def mix_columns(signs, had, flux, chunks):
    rows = flux.shape[0]
    start, width = chunks[0]
    first, count = start // width, len(chunks)
    return pl.pallas_call(
        mix_kernel,
        grid=(count,),
        in_specs=[
            pl.BlockSpec((1, rows), lambda i: (0, 0)),
            pl.BlockSpec(had.shape, lambda i: (0, 0)),
            pl.BlockSpec((rows, width), lambda i: (0, i + first)),
        ],
        out_specs=(pl.BlockSpec((rows, width), lambda i: (0, 0)),) * count,
        out_shape=(jax.ShapeDtypeStruct((rows, width), BF16),) * count,
        cost_estimate=cost(2 * count * rows * width * had.shape[0] * 3, count * rows * width * 6),
        name="mix",
    )(signs, had, flux)


def join_kernel(sign_ref, own_ref, other_ref, *refs):
    total = (other_ref[...].astype(F32) + own_ref[...].astype(F32) * sign_ref[0]) * SQRT_HALF
    total = total.astype(BF16)
    for ref in refs[-2:]:
        ref[...] = total


def join_last(own, other, sign, start, columns, whole):
    rows, width = own.shape
    block = start // width
    tile = rows // 2
    chunk = pl.BlockSpec((tile, width), lambda i: (i, 0))
    operands, specs, alias = [sign.reshape(1), own, other], [pl.BlockSpec(memory_space=pltpu.SMEM), chunk, chunk], {}
    if whole is not None:
        operands.append(whole)
        specs.append(pl.BlockSpec(memory_space=pl.ANY))
        alias = {3: 1}
    return pl.pallas_call(
        join_kernel,
        grid=(rows // tile,),
        in_specs=specs,
        out_specs=(chunk, pl.BlockSpec((tile, width), lambda i: (i, block))),
        out_shape=(jax.ShapeDtypeStruct((rows, width), BF16), jax.ShapeDtypeStruct((rows, columns), BF16)),
        input_output_aliases=alias,
        compiler_params=params(),
        cost_estimate=cost(4 * rows * width, 8 * rows * width),
        name="join",
    )(*operands)


def relative_owner(q):
    return ((q & 1) << 1) | (q >> 1)


def count_kernel(nx, me_ref, rows_ref, owner_ref, *out_refs):
    listed = rows_ref.shape[1]
    rows = out_refs[0].shape[1]
    me_z, me_x = me_ref[0], me_ref[1]
    index = lax.broadcasted_iota(jnp.int32, (NZ * nx, listed), 0)
    q, s = index & (NZ - 1), index >> (NZ.bit_length() - 1)
    z = me_z ^ relative_owner(q)
    x = (me_x + s) & (nx - 1)
    by_owner = (z * nx + x == owner_ref[...]).astype(F32).astype(BF16)
    by_row = (lax.broadcasted_iota(jnp.int32, (rows, listed), 0) == rows_ref[...]).astype(F32).astype(BF16)
    total = lax.dot_general(by_owner, by_row, (((1,), (1,)), ((), ())), preferred_element_type=F32)
    for shift, ref in enumerate(out_refs):
        ref[...] = total[shift * NZ : (shift + 1) * NZ, :]


def count_samples(sample_rows, sample_owner, nx, rows, me_z, me_x):
    listed = sample_rows.shape[0]
    shape = jax.ShapeDtypeStruct((NZ, rows), F32)
    vmem = pl.BlockSpec(memory_space=pltpu.VMEM)
    return pl.pallas_call(
        functools.partial(count_kernel, nx),
        in_specs=[pl.BlockSpec(memory_space=pltpu.SMEM), vmem, vmem],
        out_shape=(shape,) * nx,
        compiler_params=params(),
        cost_estimate=cost(2 * rows * listed * NZ * nx, rows * NZ * nx * 4),
        name="counts",
    )(jnp.stack([me_z, me_x]), sample_rows.reshape(1, listed), sample_owner.reshape(1, listed))


def weigh_kernel(counts_ref, left_ref, right_ref, hi_ref, lo_ref):
    lead = jnp.concatenate([left_ref[...].astype(F32).T, right_ref[...].astype(F32).T], axis=0)
    for q in range(NZ):
        part = pl.ds(q * PANEL, PANEL)
        weighed = lead * counts_ref[q : q + 1, :]
        hi = weighed.astype(BF16)
        hi_ref[part, :] = hi
        lo_ref[part, :] = (weighed - hi.astype(F32)).astype(BF16)


def weigh(counts, left, right):
    rows = left.shape[0]
    tile = rows // 2
    out = pl.BlockSpec((NZ * PANEL, tile), lambda i: (0, i))
    shape = jax.ShapeDtypeStruct((NZ * PANEL, rows), BF16)
    return pl.pallas_call(
        weigh_kernel,
        grid=(rows // tile,),
        in_specs=[pl.BlockSpec((NZ, tile), lambda i: (0, i))] + [pl.BlockSpec((tile, PANEL // 2), lambda i: (i, 0))] * 2,
        out_specs=(out, out),
        out_shape=(shape, shape),
        compiler_params=params(),
        cost_estimate=cost(rows * PANEL * 16, rows * PANEL * 18),
        name="weigh",
    )(counts, left, right)


GRAM_TILES = 2


def gram_kernel(parts, packed, each, *refs):
    refs, (acc,) = refs[:-1], refs[-1:]
    outs = refs[parts * each :]
    keep_ref, send_ref = (outs[0], outs[1]) if packed else (outs[1], outs[2])
    step = pl.program_id(0)

    @pl.when(step == 0)
    def _():
        acc[...] = jnp.zeros_like(acc)

    for p in range(parts):
        hi_ref, lo_ref, *rows_refs = refs[each * p : each * (p + 1)]

        @pl.when(step // GRAM_TILES == p)
        def _(hi_ref=hi_ref, lo_ref=lo_ref, rows_refs=rows_refs):
            rows = jnp.concatenate([ref[...] for ref in rows_refs], axis=1)
            low = jnp.dot(lo_ref[...], rows, preferred_element_type=F32)
            acc[...] += low + jnp.dot(hi_ref[...], rows, preferred_element_type=F32)

    @pl.when(step == parts * GRAM_TILES - 1)
    def _():
        half = PANEL // 2
        middle = NZ // 2 * PANEL
        if packed:
            for q in range(NZ):
                ref, place = (keep_ref, q) if q < NZ // 2 else (send_ref, q - NZ // 2)
                base, to = q * PANEL, place * 3 * half
                ref[to : to + PANEL, :] = acc[base : base + PANEL, :half]
                ref[to + PANEL : to + 3 * half, :] = acc[base + half : base + PANEL, half:]
        else:
            before_ref, rounded_ref, squares_ref = outs[0], outs[3], outs[4]
            keep_ref[...] = acc[:middle, :]
            send_ref[...] = acc[middle:, :]
            rounded = acc[PANEL:, :].astype(BF16)
            rounded_ref[...] = rounded[middle - PANEL :, :]
            ones = jnp.ones((8, rounded.shape[1]), BF16)
            squares_ref[:, :PANEL] = before_ref[:, :PANEL]
            squares_ref[:, PANEL:] = before_ref[:, PANEL:] + lax.dot_general(
                ones, rounded * rounded, (((1,), (1,)), ((), ())), preferred_element_type=F32
            )


def partial_grams(weights, chunk_rows, before):
    packed = before is None
    parts = len(chunk_rows)
    rows = chunk_rows[0][0].shape[0]
    width = sum(piece.shape[1] for piece in chunk_rows[0])
    tile = rows // GRAM_TILES
    half = NZ // 2
    shape = (half * (PANEL + PANEL // 2), PANEL // 2) if packed else (half * PANEL, width)
    operands, specs = [], []
    for p, ((hi, lo), pieces) in enumerate(zip(weights, chunk_rows)):
        operands += [hi, lo, *pieces]

        def place(k, p=p):
            return jnp.clip(k - p * GRAM_TILES, 0, GRAM_TILES - 1)

        weight_spec = pl.BlockSpec((NZ * PANEL, tile), lambda k, place=place: (0, place(k)))
        specs += [weight_spec, weight_spec]
        specs += [pl.BlockSpec((tile, piece.shape[1]), lambda k, place=place: (place(k), 0)) for piece in pieces]
    each = len(operands) // parts
    out = pl.BlockSpec(shape, lambda k: (0, 0))
    out_specs = [out, out]
    out_shape = [jax.ShapeDtypeStruct(shape, F32)] * 2
    if not packed:
        squares = pl.BlockSpec(before.shape, lambda k: (0, 0))
        operands.append(before)
        specs.append(squares)
        out_specs += [out, squares]
        out_shape += [jax.ShapeDtypeStruct(shape, BF16), jax.ShapeDtypeStruct(before.shape, F32)]
    return pl.pallas_call(
        functools.partial(gram_kernel, parts, packed, each),
        grid=(parts * GRAM_TILES,),
        in_specs=specs,
        out_specs=tuple(out_specs),
        out_shape=tuple(out_shape),
        scratch_shapes=[pltpu.VMEM((NZ * PANEL, width), F32)],
        compiler_params=params(),
        cost_estimate=cost(4 * parts * NZ * PANEL * rows * width, 4 * parts * NZ * PANEL * rows + 2 * parts * rows * width),
        name="grams",
    )(*operands)


def add_kernel(keep_ref, near_ref, out_ref):
    out_ref[...] = (keep_ref[...] + near_ref[...].astype(F32)).astype(out_ref.dtype)


def far_sum(keep, near):
    rows, width = keep.shape[0] // 2, keep.shape[1]
    spec = pl.BlockSpec((rows, width), lambda i: (1, 0))
    return pl.pallas_call(
        add_kernel,
        grid=(1,),
        in_specs=[spec, spec],
        out_specs=pl.BlockSpec((rows, width), lambda i: (0, 0)),
        out_shape=jax.ShapeDtypeStruct((rows, width), near.dtype),
        compiler_params=params(),
        cost_estimate=cost(rows * width, 12 * rows * width),
        name="add",
    )(keep, near)


BAND = 64
CUT = 2
MICRO = 8


def factor_band(tile):
    row_id = lax.broadcasted_iota(jnp.int32, (BAND, 1), 0)
    for first in range(0, BAND, MICRO):
        spread = [jnp.broadcast_to(tile[:, first + t : first + t + 1], tile.shape) for t in range(MICRO)]
        for t in range(MICRO):
            j = first + t
            r = lax.rsqrt(spread[t][j : j + 1, :])
            row = tile[j : j + 1, :] * r
            below = jnp.where(row_id > j, spread[t], 0.0)
            for u in range(t + 1, MICRO):
                spread[u] = spread[u] - below * (spread[u][j : j + 1, :] * (r * r))
            tile = jnp.where(row_id == j, row, tile - below * (row * r))
    return tile


def eliminate(work, first, last):
    rb = lax.broadcasted_iota(jnp.int32, (BAND, BAND), 0)
    cb = lax.broadcasted_iota(jnp.int32, (BAND, BAND), 1)
    eye_b = (rb == cb).astype(F32)
    for k in range(first, last):
        lo, hi = k * BAND, (k + 1) * BAND
        tile = factor_band(jnp.concatenate([work[lo:hi, lo:hi], eye_b], axis=1))
        inv = jnp.where(rb >= cb, tile[:, BAND:], 0.0)
        full = jnp.dot(inv, work[lo:hi, lo:], precision=HIGHEST, preferred_element_type=F32)
        if hi < PANEL:
            panel = full[:, BAND : PANEL - lo]
            work[hi:, hi:] = work[hi:, hi:] - lax.dot_general(
                panel, full[:, BAND:], (((0,), (0,)), ((), ())), precision=HIGHEST, preferred_element_type=F32
            )
        work[lo:hi, lo:] = full


def factor_first_kernel(scale, keep_ref, near_ref, far_ref, out_ref, work):
    half = PANEL // 2
    lead = (keep_ref[...] + near_ref[...] + far_ref[...]) * scale
    ri = lax.broadcasted_iota(jnp.int32, (PANEL, PANEL), 0)
    ci = lax.broadcasted_iota(jnp.int32, (PANEL, PANEL), 1)
    eye = (ri == ci).astype(F32)
    work[:, PANEL:] = eye
    work[:half, :half] = lead[:half, :] + 0.5 * eye[:half, :half]
    work[:half, half:PANEL] = lead[half:PANEL, :].T
    work[half:, :half] = lead[half:PANEL, :]
    work[half:, half:PANEL] = lead[PANEL:, :] + 0.5 * eye[:half, :half]
    eliminate(work, 0, CUT)
    out_ref[...] = work[...]


def factor_last_kernel(in_ref, squares_ref, out_ref, inverse_ref, guard_ref, work):
    work[...] = in_ref[...]
    eliminate(work, CUT, PANEL // BAND)
    ri = lax.broadcasted_iota(jnp.int32, (PANEL, PANEL), 0)
    ci = lax.broadcasted_iota(jnp.int32, (PANEL, PANEL), 1)
    upper = jnp.where(ci >= ri, work[:, :PANEL], 0.0)
    inverse = jnp.where(ri >= ci, work[:, PANEL:], 0.0)
    out_ref[...] = upper
    inverse_ref[...] = inverse
    guard_ref[:, : NZ * PANEL] = squares_ref[...]
    for place, part in enumerate((inverse, upper)):
        start = (NZ + place) * PANEL
        norms = jnp.sum(part * part, axis=0, keepdims=True)
        guard_ref[:, start : start + PANEL] = jnp.broadcast_to(norms, (8, PANEL))


def factor_first(keep, near, far, scale):
    spec = pl.BlockSpec(far.shape, lambda i: (0, 0))
    shape = (PANEL, 2 * PANEL)
    return pl.pallas_call(
        functools.partial(factor_first_kernel, scale),
        grid=(1,),
        in_specs=[spec, spec, spec],
        out_specs=pl.BlockSpec(shape, lambda i: (0, 0)),
        out_shape=jax.ShapeDtypeStruct(shape, F32),
        scratch_shapes=[pltpu.VMEM(shape, F32)],
        compiler_params=params(),
        cost_estimate=cost(10_000_000_000, 1 << 20),
        name="factor_first",
    )(keep, near, far)


def factor_last(state, squares, columns):
    def resident(shape):
        return pl.BlockSpec(shape, lambda i: (0, 0))

    square, guard = (PANEL, PANEL), (8, (NZ + 2) * PANEL)
    return pl.pallas_call(
        factor_last_kernel,
        grid=(1,),
        in_specs=[resident(state.shape), resident(squares.shape)],
        out_specs=(resident(square), resident(square), resident(guard)),
        out_shape=(
            jax.ShapeDtypeStruct((PANEL, columns), F32),
            jax.ShapeDtypeStruct(square, F32),
            jax.ShapeDtypeStruct(guard, F32),
        ),
        scratch_shapes=[pltpu.VMEM(state.shape, F32)],
        compiler_params=params(),
        cost_estimate=cost(10_000_000_000, 1 << 20),
        name="factor_last",
    )(state, squares)


def couple_kernel(scale, inverse_ref, keep_ref, near_ref, far_ref, whole_ref, out_ref):
    gram = (keep_ref[...] + near_ref[...].astype(F32) + far_ref[...].astype(F32)) * scale
    out_ref[...] = jnp.dot(inverse_ref[...], gram, precision=HIGHEST, preferred_element_type=F32)


def couple(inverse, keep, near, far, whole, start, scale):
    rows, width = far.shape
    block = start // width
    spec = pl.BlockSpec((rows, width), lambda i: (0, 0))
    return pl.pallas_call(
        functools.partial(couple_kernel, scale),
        grid=(1,),
        in_specs=[pl.BlockSpec(inverse.shape, lambda i: (0, 0)), spec, spec, spec, pl.BlockSpec(memory_space=pl.ANY)],
        out_specs=pl.BlockSpec((rows, width), lambda i: (0, block)),
        out_shape=jax.ShapeDtypeStruct(whole.shape, F32),
        input_output_aliases={4: 0},
        compiler_params=params(),
        cost_estimate=cost(12 * PANEL * rows * width, 20 * rows * width),
        name="couple",
    )(inverse, keep, near, far, whole)


ROUNDING = 0.6 * 2.0**-8
LIMIT = 0.004


def judge_kernel(scale, *refs):
    *guard_refs, out_ref, guards, sems = refs
    copies = [pltpu.make_async_copy(ref, guards.at[k], sems.at[k]) for k, ref in enumerate(guard_refs)]
    for copy in copies:
        copy.start()
    for copy in copies:
        copy.wait()
    worst = jnp.zeros((8, 1), F32)
    for owner in range(NZ):
        terms = []
        for sender in range(NZ):
            apart = owner ^ sender
            place = relative_owner(apart) * PANEL
            terms.append(guards[sender, :, place : place + PANEL] * float(apart))
        total = (terms[0] + terms[1]) + (terms[2] + terms[3])
        inverse_norms = guards[owner, :, NZ * PANEL : (NZ + 1) * PANEL]
        upper_norms = guards[owner, :, (NZ + 1) * PANEL :]
        error = jnp.sum(inverse_norms * total, axis=1, keepdims=True) * (ROUNDING * scale) ** 2
        size = jnp.sum(upper_norms, axis=1, keepdims=True) * LIMIT**2
        worst = jnp.maximum(worst, jnp.where(error <= size, 0.0, 1.0))
    out_ref[0] = jnp.max(worst).astype(jnp.int32)


def judge(guards, scale):
    return pl.pallas_call(
        functools.partial(judge_kernel, scale),
        in_specs=[pl.BlockSpec(memory_space=pltpu.HBM)] * NZ,
        out_specs=pl.BlockSpec(memory_space=pltpu.SMEM),
        out_shape=jax.ShapeDtypeStruct((1,), jnp.int32),
        scratch_shapes=[pltpu.VMEM((NZ,) + guards[0].shape, F32), pltpu.SemaphoreType.DMA((NZ,))],
        name="judge",
    )(*guards)


def per_device(flux_rows, row_signs, sample_rows, sample_owner):
    wide, blk = lax.axis_size("wide"), lax.axis_size("blk")
    nx = blk // NZ
    rows, columns = flux_rows.shape
    scale = 1.0 / sample_rows.shape[0]
    me_w, me_b = lax.axis_index("wide"), lax.axis_index("blk")
    me_x, me_z = me_b & (nx - 1), me_b >> (nx.bit_length() - 1)
    had = hadamard_pair()
    signs = row_signs.reshape(1, rows)
    levels = wide.bit_length() - 1

    def at(z, x):
        return z * nx + x

    def z_route(mask):
        return [(at(z, x), at(z ^ mask, x)) for z in range(NZ) for x in range(nx)]

    def x_shift(s):
        return [(at(z, x), at(z, (x + s) % nx)) for z in range(NZ) for x in range(nx)]

    def level_sign(level):
        return jnp.where((me_w >> level) & 1 == 1, -1.0, 1.0).astype(F32)

    def last_level(own, start, whole):
        partner = lax.ppermute(own, "wide", [(w, w ^ (wide // 2)) for w in range(wide)])
        own, whole = join_last(own, partner, level_sign(levels - 1), start, columns, whole)
        pieces = [own]
        for s in range(1, nx):
            pieces.append(lax.ppermute(own, "blk", x_shift(s)))
        return pieces, whole

    def level_up(level, own, partner):
        total = (partner.astype(F32) + own.astype(F32) * level_sign(level)) * SQRT_HALF
        return total.astype(BF16)

    def first_levels(mixed, last=levels - 1):
        for level in range(last):
            partner = lax.ppermute(mixed, "wide", [(w, w ^ (1 << level)) for w in range(wide)])
            mixed = level_up(level, mixed, partner)
        return mixed

    def cut_lead(mixed):
        mixed = first_levels(mixed, levels - 2)
        partner = lax.ppermute(mixed, "wide", [(w, w ^ (1 << (levels - 2))) for w in range(wide)])
        cuts = [slice(start, start + PIECE) for start in range(0, PANEL, PIECE)]
        return [level_up(levels - 2, mixed[:, cut], partner[:, cut]) for cut in cuts]

    blocks = [(start, PANEL) for start in range(0, columns, PANEL)]
    mixed = [*mix_columns(signs, had, flux_rows, blocks[:1])]
    counts = count_samples(sample_rows, sample_owner, nx, rows, me_z, me_x)
    owner_counts = [counts[0]]
    for s in range(1, nx):
        owner_counts.append(lax.ppermute(counts[s], "blk", x_shift(s)))
    mixed += mix_columns(signs, had, flux_rows, blocks[1:])
    pieces, whole, place = [], None, 0
    for piece in cut_lead(mixed[0]) + [first_levels(block) for block in mixed[1:]]:
        piece, whole = last_level(piece, place, whole)
        place += piece[0].shape[1]
        pieces.append(piece)
    groups = [[[pieces[0][p], pieces[1][p]] for p in range(nx)]] + [[[piece[p]] for p in range(nx)] for piece in pieces[2:]]

    weights, grams, precise = [], [], []
    squares = jnp.zeros((8, NZ * PANEL), F32)
    for i, sources in enumerate(groups):
        if i == 0:
            for p in range(nx):
                weights.append(weigh(owner_counts[p], *sources[p]))
        if i == 0:
            keep, send = partial_grams(weights, sources, None)
        else:
            keep, exact_send, send, squares = partial_grams(weights, sources, squares)
            precise.append((keep, exact_send))
        near = lax.ppermute(send, "blk", z_route(1))
        onward = far_sum(keep, near)
        far = lax.ppermute(onward, "blk", z_route(2))
        grams.append((keep, near, far))
    state = factor_first(*grams[0], scale)
    sketch, inverse, guard = factor_last(state, squares, columns)
    guards = [guard]
    for mask in range(1, NZ):
        guards.append(lax.ppermute(guard, "blk", z_route(mask)))
    redo = judge(guards, scale)[0] != 0
    for i in range(1, len(groups) - 1):
        sketch = couple(inverse, *grams[i], sketch, i * PANEL, scale)

    def rounded(sketch, inverse, last, precise):
        return couple(inverse, *last, sketch, columns - PANEL, scale)

    def exact(sketch, inverse, last, precise):
        for i, (keep, send) in enumerate(precise):
            near = lax.ppermute(send, "blk", z_route(1))
            far = lax.ppermute(far_sum(keep, near), "blk", z_route(2))
            sketch = couple(inverse, keep, near, far, sketch, (i + 1) * PANEL, scale)
        return sketch

    sketch = lax.cond(redo, exact, rounded, sketch, inverse, grams[-1], precise)
    return whole, sketch


def solution(mesh):
    placed = (
        P(("wide", "blk"), None),
        P(("wide", "blk")),
        P(("wide", "blk")),
        P(("wide", "blk"), None),
    )

    return jax.shard_map(
        per_device,
        mesh=mesh,
        in_specs=placed,
        out_specs=(P(("wide", "blk"), None), P(("wide", "blk"), None)),
        check_vma=False,
    )
```

```python
import functools

import jax
import jax.numpy as jnp
import numpy as np
from jax import lax
from jax.experimental import pallas as pl
from jax.experimental.pallas import tpu as pltpu
from jax.sharding import PartitionSpec as P

PANEL = 256
HB = 128
NZ = 4
PIECE = 128
SQRT_HALF = 0.7071067811865476
HIGHEST = lax.Precision.HIGHEST
F32 = jnp.float32
BF16 = jnp.bfloat16


def hadamard_pair():
    idx = np.arange(HB)
    common = idx[:, None] & idx[None, :]
    parity = np.zeros_like(common)
    for bit in range(HB.bit_length() - 1):
        parity ^= (common >> bit) & 1
    one = 1.0 - 2.0 * parity
    return jnp.asarray(np.kron(np.eye(2), one), BF16)


VMEM_LIMIT = 24 << 20


def params(**kw):
    return pltpu.CompilerParams(vmem_limit_bytes=VMEM_LIMIT, **kw)


def cost(flops, moved):
    return pl.CostEstimate(flops=flops, bytes_accessed=moved, transcendentals=0)


def mix_kernel(signs_ref, had_ref, x_ref, *out_refs):
    rows = x_ref.shape[0]
    size = had_ref.shape[0]
    for which, out_ref in enumerate(out_refs):

        @pl.when(pl.program_id(0) == which)
        def _(out_ref=out_ref):
            for b in range(rows // size):
                part = pl.ds(b * size, size)
                signed = (had_ref[...].astype(F32) * signs_ref[:, b * size : (b + 1) * size].astype(F32)).astype(BF16)
                x = x_ref[part, :]
                hi = x.astype(BF16)
                rest = x - hi.astype(F32)
                mid = rest.astype(BF16)
                low = (rest - mid.astype(F32)).astype(BF16)
                total = jnp.dot(signed, low, preferred_element_type=F32)
                total = total + jnp.dot(signed, mid, preferred_element_type=F32)
                total = total + jnp.dot(signed, hi, preferred_element_type=F32)
                out_ref[part, :] = (total * (HB**-0.5)).astype(BF16)


def mix_columns(signs, had, flux, chunks):
    rows = flux.shape[0]
    start, width = chunks[0]
    first, count = start // width, len(chunks)
    return pl.pallas_call(
        mix_kernel,
        grid=(count,),
        in_specs=[
            pl.BlockSpec((1, rows), lambda i: (0, 0)),
            pl.BlockSpec(had.shape, lambda i: (0, 0)),
            pl.BlockSpec((rows, width), lambda i: (0, i + first)),
        ],
        out_specs=(pl.BlockSpec((rows, width), lambda i: (0, 0)),) * count,
        out_shape=(jax.ShapeDtypeStruct((rows, width), BF16),) * count,
        cost_estimate=cost(2 * count * rows * width * had.shape[0] * 3, count * rows * width * 6),
        name="mix",
    )(signs, had, flux)


def join_kernel(sign_ref, own_ref, other_ref, *refs):
    total = (other_ref[...].astype(F32) + own_ref[...].astype(F32) * sign_ref[0]) * SQRT_HALF
    total = total.astype(BF16)
    for ref in refs[-2:]:
        ref[...] = total


def join_last(own, other, sign, start, columns, whole):
    rows, width = own.shape
    block = start // width
    tile = rows // 2
    chunk = pl.BlockSpec((tile, width), lambda i: (i, 0))
    operands, specs, alias = [sign.reshape(1), own, other], [pl.BlockSpec(memory_space=pltpu.SMEM), chunk, chunk], {}
    if whole is not None:
        operands.append(whole)
        specs.append(pl.BlockSpec(memory_space=pl.ANY))
        alias = {3: 1}
    return pl.pallas_call(
        join_kernel,
        grid=(rows // tile,),
        in_specs=specs,
        out_specs=(chunk, pl.BlockSpec((tile, width), lambda i: (i, block))),
        out_shape=(jax.ShapeDtypeStruct((rows, width), BF16), jax.ShapeDtypeStruct((rows, columns), BF16)),
        input_output_aliases=alias,
        compiler_params=params(),
        cost_estimate=cost(4 * rows * width, 8 * rows * width),
        name="join",
    )(*operands)


def relative_owner(q):
    return ((q & 1) << 1) | (q >> 1)


def count_kernel(nx, me_ref, rows_ref, owner_ref, *out_refs):
    listed = rows_ref.shape[1]
    rows = out_refs[0].shape[1]
    me_z, me_x = me_ref[0], me_ref[1]
    index = lax.broadcasted_iota(jnp.int32, (NZ * nx, listed), 0)
    q, s = index & (NZ - 1), index >> (NZ.bit_length() - 1)
    z = me_z ^ relative_owner(q)
    x = (me_x + s) & (nx - 1)
    by_owner = (z * nx + x == owner_ref[...]).astype(F32).astype(BF16)
    by_row = (lax.broadcasted_iota(jnp.int32, (rows, listed), 0) == rows_ref[...]).astype(F32).astype(BF16)
    total = lax.dot_general(by_owner, by_row, (((1,), (1,)), ((), ())), preferred_element_type=F32)
    for shift, ref in enumerate(out_refs):
        ref[...] = total[shift * NZ : (shift + 1) * NZ, :]


def count_samples(sample_rows, sample_owner, nx, rows, me_z, me_x):
    listed = sample_rows.shape[0]
    shape = jax.ShapeDtypeStruct((NZ, rows), F32)
    vmem = pl.BlockSpec(memory_space=pltpu.VMEM)
    return pl.pallas_call(
        functools.partial(count_kernel, nx),
        in_specs=[pl.BlockSpec(memory_space=pltpu.SMEM), vmem, vmem],
        out_shape=(shape,) * nx,
        compiler_params=params(),
        cost_estimate=cost(2 * rows * listed * NZ * nx, rows * NZ * nx * 4),
        name="counts",
    )(jnp.stack([me_z, me_x]), sample_rows.reshape(1, listed), sample_owner.reshape(1, listed))


def weigh_kernel(counts_ref, left_ref, right_ref, hi_ref, lo_ref):
    lead = jnp.concatenate([left_ref[...].astype(F32).T, right_ref[...].astype(F32).T], axis=0)
    for q in range(NZ):
        part = pl.ds(q * PANEL, PANEL)
        weighed = lead * counts_ref[q : q + 1, :]
        hi = weighed.astype(BF16)
        hi_ref[part, :] = hi
        lo_ref[part, :] = (weighed - hi.astype(F32)).astype(BF16)


def weigh(counts, left, right):
    rows = left.shape[0]
    tile = rows // 2
    out = pl.BlockSpec((NZ * PANEL, tile), lambda i: (0, i))
    shape = jax.ShapeDtypeStruct((NZ * PANEL, rows), BF16)
    return pl.pallas_call(
        weigh_kernel,
        grid=(rows // tile,),
        in_specs=[pl.BlockSpec((NZ, tile), lambda i: (0, i))] + [pl.BlockSpec((tile, PANEL // 2), lambda i: (i, 0))] * 2,
        out_specs=(out, out),
        out_shape=(shape, shape),
        compiler_params=params(),
        cost_estimate=cost(rows * PANEL * 16, rows * PANEL * 18),
        name="weigh",
    )(counts, left, right)


GRAM_TILES = 2


def gram_kernel(parts, packed, each, *refs):
    refs, (acc,) = refs[:-1], refs[-1:]
    outs = refs[parts * each :]
    keep_ref, send_ref = (outs[0], outs[1]) if packed else (outs[1], outs[2])
    step = pl.program_id(0)

    @pl.when(step == 0)
    def _():
        acc[...] = jnp.zeros_like(acc)

    for p in range(parts):
        hi_ref, lo_ref, *rows_refs = refs[each * p : each * (p + 1)]

        @pl.when(step // GRAM_TILES == p)
        def _(hi_ref=hi_ref, lo_ref=lo_ref, rows_refs=rows_refs):
            rows = jnp.concatenate([ref[...] for ref in rows_refs], axis=1)
            low = jnp.dot(lo_ref[...], rows, preferred_element_type=F32)
            acc[...] += low + jnp.dot(hi_ref[...], rows, preferred_element_type=F32)

    @pl.when(step == parts * GRAM_TILES - 1)
    def _():
        half = PANEL // 2
        middle = NZ // 2 * PANEL
        if packed:
            for q in range(NZ):
                ref, place = (keep_ref, q) if q < NZ // 2 else (send_ref, q - NZ // 2)
                base, to = q * PANEL, place * 3 * half
                ref[to : to + PANEL, :] = acc[base : base + PANEL, :half]
                ref[to + PANEL : to + 3 * half, :] = acc[base + half : base + PANEL, half:]
        else:
            before_ref, rounded_ref, squares_ref = outs[0], outs[3], outs[4]
            keep_ref[...] = acc[:middle, :]
            send_ref[...] = acc[middle:, :]
            rounded = acc[PANEL:, :].astype(BF16)
            rounded_ref[...] = rounded[middle - PANEL :, :]
            ones = jnp.ones((8, rounded.shape[1]), BF16)
            squares_ref[:, :PANEL] = before_ref[:, :PANEL]
            squares_ref[:, PANEL:] = before_ref[:, PANEL:] + lax.dot_general(
                ones, rounded * rounded, (((1,), (1,)), ((), ())), preferred_element_type=F32
            )


def partial_grams(weights, chunk_rows, before):
    packed = before is None
    parts = len(chunk_rows)
    rows = chunk_rows[0][0].shape[0]
    width = sum(piece.shape[1] for piece in chunk_rows[0])
    tile = rows // GRAM_TILES
    half = NZ // 2
    shape = (half * (PANEL + PANEL // 2), PANEL // 2) if packed else (half * PANEL, width)
    operands, specs = [], []
    for p, ((hi, lo), pieces) in enumerate(zip(weights, chunk_rows)):
        operands += [hi, lo, *pieces]

        def place(k, p=p):
            return jnp.clip(k - p * GRAM_TILES, 0, GRAM_TILES - 1)

        weight_spec = pl.BlockSpec((NZ * PANEL, tile), lambda k, place=place: (0, place(k)))
        specs += [weight_spec, weight_spec]
        specs += [pl.BlockSpec((tile, piece.shape[1]), lambda k, place=place: (place(k), 0)) for piece in pieces]
    each = len(operands) // parts
    out = pl.BlockSpec(shape, lambda k: (0, 0))
    out_specs = [out, out]
    out_shape = [jax.ShapeDtypeStruct(shape, F32)] * 2
    if not packed:
        squares = pl.BlockSpec(before.shape, lambda k: (0, 0))
        operands.append(before)
        specs.append(squares)
        out_specs += [out, squares]
        out_shape += [jax.ShapeDtypeStruct(shape, BF16), jax.ShapeDtypeStruct(before.shape, F32)]
    return pl.pallas_call(
        functools.partial(gram_kernel, parts, packed, each),
        grid=(parts * GRAM_TILES,),
        in_specs=specs,
        out_specs=tuple(out_specs),
        out_shape=tuple(out_shape),
        scratch_shapes=[pltpu.VMEM((NZ * PANEL, width), F32)],
        compiler_params=params(),
        cost_estimate=cost(4 * parts * NZ * PANEL * rows * width, 4 * parts * NZ * PANEL * rows + 2 * parts * rows * width),
        name="grams",
    )(*operands)


def add_kernel(*refs):
    *in_refs, out_ref = refs
    rows = in_refs[0].shape[0]
    for k in range(len(in_refs) // 2):
        total = in_refs[2 * k][...] + in_refs[2 * k + 1][...].astype(F32)
        out_ref[k * rows : (k + 1) * rows, :] = total.astype(out_ref.dtype)


def far_sums(*pairs):
    keep, near = pairs[0]
    rows, width = keep.shape[0] // 2, keep.shape[1]
    spec = pl.BlockSpec((rows, width), lambda i: (1, 0))
    shape = (len(pairs) * rows, width)
    return pl.pallas_call(
        add_kernel,
        grid=(1,),
        in_specs=[spec] * (2 * len(pairs)),
        out_specs=pl.BlockSpec(shape, lambda i: (0, 0)),
        out_shape=jax.ShapeDtypeStruct(shape, near.dtype),
        compiler_params=params(),
        cost_estimate=cost(len(pairs) * rows * width, 12 * len(pairs) * rows * width),
        name="add",
    )(*[operand for pair in pairs for operand in pair])


BAND = 64
CUT = 2
MICRO = 8


def factor_band(tile):
    row_id = lax.broadcasted_iota(jnp.int32, (BAND, 1), 0)
    for first in range(0, BAND, MICRO):
        spread = [jnp.broadcast_to(tile[:, first + t : first + t + 1], tile.shape) for t in range(MICRO)]
        for t in range(MICRO):
            j = first + t
            r = lax.rsqrt(spread[t][j : j + 1, :])
            row = tile[j : j + 1, :] * r
            below = jnp.where(row_id > j, spread[t], 0.0)
            for u in range(t + 1, MICRO):
                spread[u] = spread[u] - below * (spread[u][j : j + 1, :] * (r * r))
            tile = jnp.where(row_id == j, row, tile - below * (row * r))
    return tile


def eliminate(work, first, last):
    rb = lax.broadcasted_iota(jnp.int32, (BAND, BAND), 0)
    cb = lax.broadcasted_iota(jnp.int32, (BAND, BAND), 1)
    eye_b = (rb == cb).astype(F32)
    for k in range(first, last):
        lo, hi = k * BAND, (k + 1) * BAND
        tile = factor_band(jnp.concatenate([work[lo:hi, lo:hi], eye_b], axis=1))
        inv = jnp.where(rb >= cb, tile[:, BAND:], 0.0)
        full = jnp.dot(inv, work[lo:hi, lo:], precision=HIGHEST, preferred_element_type=F32)
        if hi < PANEL:
            panel = full[:, BAND : PANEL - lo]
            work[hi:, hi:] = work[hi:, hi:] - lax.dot_general(
                panel, full[:, BAND:], (((0,), (0,)), ((), ())), precision=HIGHEST, preferred_element_type=F32
            )
        work[lo:hi, lo:] = full


def factor_first_kernel(scale, keep_ref, near_ref, far_ref, out_ref, work):
    half = PANEL // 2
    lead = (keep_ref[...] + near_ref[...] + far_ref[...]) * scale
    ri = lax.broadcasted_iota(jnp.int32, (PANEL, PANEL), 0)
    ci = lax.broadcasted_iota(jnp.int32, (PANEL, PANEL), 1)
    eye = (ri == ci).astype(F32)
    work[:, PANEL:] = eye
    work[:half, :half] = lead[:half, :] + 0.5 * eye[:half, :half]
    work[:half, half:PANEL] = lead[half:PANEL, :].T
    work[half:, :half] = lead[half:PANEL, :]
    work[half:, half:PANEL] = lead[PANEL:, :] + 0.5 * eye[:half, :half]
    eliminate(work, 0, CUT)
    out_ref[...] = work[...]


def factor_last_kernel(in_ref, squares_ref, out_ref, inverse_ref, guard_ref, work):
    work[...] = in_ref[...]
    eliminate(work, CUT, PANEL // BAND)
    ri = lax.broadcasted_iota(jnp.int32, (PANEL, PANEL), 0)
    ci = lax.broadcasted_iota(jnp.int32, (PANEL, PANEL), 1)
    upper = jnp.where(ci >= ri, work[:, :PANEL], 0.0)
    inverse = jnp.where(ri >= ci, work[:, PANEL:], 0.0)
    out_ref[...] = upper
    inverse_ref[...] = inverse
    guard_ref[:, : NZ * PANEL] = squares_ref[...]
    for place, part in enumerate((inverse, upper)):
        start = (NZ + place) * PANEL
        norms = jnp.sum(part * part, axis=0, keepdims=True)
        guard_ref[:, start : start + PANEL] = jnp.broadcast_to(norms, (8, PANEL))


def factor_first(keep, near, far, scale):
    spec = pl.BlockSpec(far.shape, lambda i: (0, 0))
    shape = (PANEL, 2 * PANEL)
    return pl.pallas_call(
        functools.partial(factor_first_kernel, scale),
        grid=(1,),
        in_specs=[spec, spec, spec],
        out_specs=pl.BlockSpec(shape, lambda i: (0, 0)),
        out_shape=jax.ShapeDtypeStruct(shape, F32),
        scratch_shapes=[pltpu.VMEM(shape, F32)],
        compiler_params=params(),
        cost_estimate=cost(10_000_000_000, 1 << 20),
        name="factor_first",
    )(keep, near, far)


def factor_last(state, squares, columns):
    def resident(shape):
        return pl.BlockSpec(shape, lambda i: (0, 0))

    square, guard = (PANEL, PANEL), (8, (NZ + 2) * PANEL)
    return pl.pallas_call(
        factor_last_kernel,
        grid=(1,),
        in_specs=[resident(state.shape), resident(squares.shape)],
        out_specs=(resident(square), resident(square), resident(guard)),
        out_shape=(
            jax.ShapeDtypeStruct((PANEL, columns), F32),
            jax.ShapeDtypeStruct(square, F32),
            jax.ShapeDtypeStruct(guard, F32),
        ),
        scratch_shapes=[pltpu.VMEM(state.shape, F32)],
        compiler_params=params(),
        cost_estimate=cost(10_000_000_000, 1 << 20),
        name="factor_last",
    )(state, squares)


def couple_kernel(scale, inverse_ref, keep_ref, near_ref, far_ref, whole_ref, out_ref):
    gram = (keep_ref[...] + near_ref[...].astype(F32) + far_ref[...].astype(F32)) * scale
    out_ref[...] = jnp.dot(inverse_ref[...], gram, precision=HIGHEST, preferred_element_type=F32)


def couple(inverse, keep, near, far, place, whole, start, scale):
    width = far.shape[1]
    rows = PANEL
    block = start // width
    spec = pl.BlockSpec((rows, width), lambda i: (0, 0))
    return pl.pallas_call(
        functools.partial(couple_kernel, scale),
        grid=(1,),
        in_specs=[pl.BlockSpec(inverse.shape, lambda i: (0, 0)), spec, spec, pl.BlockSpec((rows, width), lambda i: (place, 0)), pl.BlockSpec(memory_space=pl.ANY)],
        out_specs=pl.BlockSpec((rows, width), lambda i: (0, block)),
        out_shape=jax.ShapeDtypeStruct(whole.shape, F32),
        input_output_aliases={4: 0},
        compiler_params=params(),
        cost_estimate=cost(12 * PANEL * rows * width, 20 * rows * width),
        name="couple",
    )(inverse, keep, near, far, whole)


ROUNDING = 0.6 * 2.0**-8
LIMIT = 0.004


def judge_kernel(scale, *refs):
    *guard_refs, out_ref, guards, sems = refs
    copies = [pltpu.make_async_copy(ref, guards.at[k], sems.at[k]) for k, ref in enumerate(guard_refs)]
    for copy in copies:
        copy.start()
    for copy in copies:
        copy.wait()
    worst = jnp.zeros((8, 1), F32)
    for owner in range(NZ):
        terms = []
        for sender in range(NZ):
            apart = owner ^ sender
            place = relative_owner(apart) * PANEL
            terms.append(guards[sender, :, place : place + PANEL] * float(apart))
        total = (terms[0] + terms[1]) + (terms[2] + terms[3])
        inverse_norms = guards[owner, :, NZ * PANEL : (NZ + 1) * PANEL]
        upper_norms = guards[owner, :, (NZ + 1) * PANEL :]
        error = jnp.sum(inverse_norms * total, axis=1, keepdims=True) * (ROUNDING * scale) ** 2
        size = jnp.sum(upper_norms, axis=1, keepdims=True) * LIMIT**2
        worst = jnp.maximum(worst, jnp.where(error <= size, 0.0, 1.0))
    out_ref[0] = jnp.max(worst).astype(jnp.int32)


def judge(guards, scale):
    return pl.pallas_call(
        functools.partial(judge_kernel, scale),
        in_specs=[pl.BlockSpec(memory_space=pltpu.HBM)] * NZ,
        out_specs=pl.BlockSpec(memory_space=pltpu.SMEM),
        out_shape=jax.ShapeDtypeStruct((1,), jnp.int32),
        scratch_shapes=[pltpu.VMEM((NZ,) + guards[0].shape, F32), pltpu.SemaphoreType.DMA((NZ,))],
        name="judge",
    )(*guards)


def per_device(flux_rows, row_signs, sample_rows, sample_owner):
    wide, blk = lax.axis_size("wide"), lax.axis_size("blk")
    nx = blk // NZ
    rows, columns = flux_rows.shape
    scale = 1.0 / sample_rows.shape[0]
    me_w, me_b = lax.axis_index("wide"), lax.axis_index("blk")
    me_x, me_z = me_b & (nx - 1), me_b >> (nx.bit_length() - 1)
    had = hadamard_pair()
    signs = row_signs.reshape(1, rows)
    levels = wide.bit_length() - 1

    def at(z, x):
        return z * nx + x

    def z_route(mask):
        return [(at(z, x), at(z ^ mask, x)) for z in range(NZ) for x in range(nx)]

    def x_shift(s):
        return [(at(z, x), at(z, (x + s) % nx)) for z in range(NZ) for x in range(nx)]

    def level_sign(level):
        return jnp.where((me_w >> level) & 1 == 1, -1.0, 1.0).astype(F32)

    def last_level(own, start, whole):
        partner = lax.ppermute(own, "wide", [(w, w ^ (wide // 2)) for w in range(wide)])
        own, whole = join_last(own, partner, level_sign(levels - 1), start, columns, whole)
        pieces = [own]
        for s in range(1, nx):
            pieces.append(lax.ppermute(own, "blk", x_shift(s)))
        return pieces, whole

    def level_up(level, own, partner):
        total = (partner.astype(F32) + own.astype(F32) * level_sign(level)) * SQRT_HALF
        return total.astype(BF16)

    def first_levels(mixed, last=levels - 1):
        for level in range(last):
            partner = lax.ppermute(mixed, "wide", [(w, w ^ (1 << level)) for w in range(wide)])
            mixed = level_up(level, mixed, partner)
        return mixed

    def cut_lead(mixed):
        mixed = first_levels(mixed, levels - 2)
        partner = lax.ppermute(mixed, "wide", [(w, w ^ (1 << (levels - 2))) for w in range(wide)])
        cuts = [slice(start, start + PIECE) for start in range(0, PANEL, PIECE)]
        return [level_up(levels - 2, mixed[:, cut], partner[:, cut]) for cut in cuts]

    blocks = [(start, PANEL) for start in range(0, columns, PANEL)]
    mixed = [*mix_columns(signs, had, flux_rows, blocks[:1])]
    counts = count_samples(sample_rows, sample_owner, nx, rows, me_z, me_x)
    owner_counts = [counts[0]]
    for s in range(1, nx):
        owner_counts.append(lax.ppermute(counts[s], "blk", x_shift(s)))
    mixed += mix_columns(signs, had, flux_rows, blocks[1:])
    pieces, whole, place = [], None, 0
    for piece in cut_lead(mixed[0]) + [first_levels(block) for block in mixed[1:]]:
        piece, whole = last_level(piece, place, whole)
        place += piece[0].shape[1]
        pieces.append(piece)
    groups = [[[pieces[0][p], pieces[1][p]] for p in range(nx)]] + [[[piece[p]] for p in range(nx)] for piece in pieces[2:]]

    weights, grams, precise = [], [], []
    squares = jnp.zeros((8, NZ * PANEL), F32)
    for i, sources in enumerate(groups):
        if i == 0:
            for p in range(nx):
                weights.append(weigh(owner_counts[p], *sources[p]))
        if i == 0:
            keep, send = partial_grams(weights, sources, None)
        else:
            keep, exact_send, send, squares = partial_grams(weights, sources, squares)
            precise.append((keep, exact_send))
        near = lax.ppermute(send, "blk", z_route(1))
        grams.append((keep, near))
    last = len(groups) - 1
    far = {}
    for members in ((0,), tuple(range(1, last)), (last,)):
        onward = far_sums(*[grams[i] for i in members])
        onward = lax.ppermute(onward, "blk", z_route(2))
        for place, i in enumerate(members):
            far[i] = (onward, place)
    grams = [pair + far[i] for i, pair in enumerate(grams)]
    state = factor_first(*grams[0][:3], scale)
    sketch, inverse, guard = factor_last(state, squares, columns)
    guards = [guard]
    for mask in range(1, NZ):
        guards.append(lax.ppermute(guard, "blk", z_route(mask)))
    redo = judge(guards, scale)[0] != 0
    for i in range(1, len(groups) - 1):
        sketch = couple(inverse, *grams[i], sketch, i * PANEL, scale)

    def rounded(sketch, inverse, last, precise):
        return couple(inverse, *last, 0, sketch, columns - PANEL, scale)

    def exact(sketch, inverse, last, precise):
        for i, (keep, send) in enumerate(precise):
            near = lax.ppermute(send, "blk", z_route(1))
            far = lax.ppermute(far_sums((keep, near)), "blk", z_route(2))
            sketch = couple(inverse, keep, near, far, 0, sketch, (i + 1) * PANEL, scale)
        return sketch

    sketch = lax.cond(redo, exact, rounded, sketch, inverse, grams[-1][:3], precise)
    return whole, sketch


def solution(mesh):
    placed = (
        P(("wide", "blk"), None),
        P(("wide", "blk")),
        P(("wide", "blk")),
        P(("wide", "blk"), None),
    )

    return jax.shard_map(
        per_device,
        mesh=mesh,
        in_specs=placed,
        out_specs=(P(("wide", "blk"), None), P(("wide", "blk"), None)),
        check_vma=False,
    )
```

```python
import functools

import jax
import jax.numpy as jnp
import numpy as np
from jax import lax
from jax.experimental import pallas as pl
from jax.experimental.pallas import tpu as pltpu
from jax.sharding import PartitionSpec as P

PANEL = 256
HB = 128
NZ = 4
PIECE = 128
SQRT_HALF = 0.7071067811865476
HIGHEST = lax.Precision.HIGHEST
F32 = jnp.float32
BF16 = jnp.bfloat16


def hadamard_pair():
    idx = np.arange(HB)
    common = idx[:, None] & idx[None, :]
    parity = np.zeros_like(common)
    for bit in range(HB.bit_length() - 1):
        parity ^= (common >> bit) & 1
    one = 1.0 - 2.0 * parity
    return jnp.asarray(np.kron(np.eye(2), one), BF16)


VMEM_LIMIT = 24 << 20


def params(**kw):
    return pltpu.CompilerParams(vmem_limit_bytes=VMEM_LIMIT, **kw)


def cost(flops, moved):
    return pl.CostEstimate(flops=flops, bytes_accessed=moved, transcendentals=0)


def mix_kernel(signs_ref, had_ref, x_ref, *out_refs):
    rows = x_ref.shape[0]
    size = had_ref.shape[0]
    for which, out_ref in enumerate(out_refs):

        @pl.when(pl.program_id(0) == which)
        def _(out_ref=out_ref):
            for b in range(rows // size):
                part = pl.ds(b * size, size)
                signed = (had_ref[...].astype(F32) * signs_ref[:, b * size : (b + 1) * size].astype(F32)).astype(BF16)
                x = x_ref[part, :]
                hi = x.astype(BF16)
                rest = x - hi.astype(F32)
                mid = rest.astype(BF16)
                low = (rest - mid.astype(F32)).astype(BF16)
                total = jnp.dot(signed, low, preferred_element_type=F32)
                total = total + jnp.dot(signed, mid, preferred_element_type=F32)
                total = total + jnp.dot(signed, hi, preferred_element_type=F32)
                out_ref[part, :] = (total * (HB**-0.5)).astype(BF16)


def mix_columns(signs, had, flux, chunks):
    rows = flux.shape[0]
    start, width = chunks[0]
    first, count = start // width, len(chunks)
    return pl.pallas_call(
        mix_kernel,
        grid=(count,),
        in_specs=[
            pl.BlockSpec((1, rows), lambda i: (0, 0)),
            pl.BlockSpec(had.shape, lambda i: (0, 0)),
            pl.BlockSpec((rows, width), lambda i: (0, i + first)),
        ],
        out_specs=(pl.BlockSpec((rows, width), lambda i: (0, 0)),) * count,
        out_shape=(jax.ShapeDtypeStruct((rows, width), BF16),) * count,
        cost_estimate=cost(2 * count * rows * width * had.shape[0] * 3, count * rows * width * 6),
        name="mix",
    )(signs, had, flux)


def join_kernel(sign_ref, own_ref, other_ref, *refs):
    total = (other_ref[...].astype(F32) + own_ref[...].astype(F32) * sign_ref[0]) * SQRT_HALF
    total = total.astype(BF16)
    for ref in refs[-2:]:
        ref[...] = total


def join_last(own, other, sign, start, columns, whole):
    rows, width = own.shape
    block = start // width
    tile = rows // 2
    chunk = pl.BlockSpec((tile, width), lambda i: (i, 0))
    operands, specs, alias = [sign.reshape(1), own, other], [pl.BlockSpec(memory_space=pltpu.SMEM), chunk, chunk], {}
    if whole is not None:
        operands.append(whole)
        specs.append(pl.BlockSpec(memory_space=pl.ANY))
        alias = {3: 1}
    return pl.pallas_call(
        join_kernel,
        grid=(rows // tile,),
        in_specs=specs,
        out_specs=(chunk, pl.BlockSpec((tile, width), lambda i: (i, block))),
        out_shape=(jax.ShapeDtypeStruct((rows, width), BF16), jax.ShapeDtypeStruct((rows, columns), BF16)),
        input_output_aliases=alias,
        compiler_params=params(),
        cost_estimate=cost(4 * rows * width, 8 * rows * width),
        name="join",
    )(*operands)


def relative_owner(q):
    return ((q & 1) << 1) | (q >> 1)


def count_kernel(nx, me_ref, rows_ref, owner_ref, *out_refs):
    listed = rows_ref.shape[1]
    rows = out_refs[0].shape[1]
    me_z, me_x = me_ref[0], me_ref[1]
    index = lax.broadcasted_iota(jnp.int32, (NZ * nx, listed), 0)
    q, s = index & (NZ - 1), index >> (NZ.bit_length() - 1)
    z = me_z ^ relative_owner(q)
    x = (me_x + s) & (nx - 1)
    by_owner = (z * nx + x == owner_ref[...]).astype(F32).astype(BF16)
    by_row = (lax.broadcasted_iota(jnp.int32, (rows, listed), 0) == rows_ref[...]).astype(F32).astype(BF16)
    total = lax.dot_general(by_owner, by_row, (((1,), (1,)), ((), ())), preferred_element_type=F32)
    for shift, ref in enumerate(out_refs):
        ref[...] = total[shift * NZ : (shift + 1) * NZ, :]


def count_samples(sample_rows, sample_owner, nx, rows, me_z, me_x):
    listed = sample_rows.shape[0]
    shape = jax.ShapeDtypeStruct((NZ, rows), F32)
    vmem = pl.BlockSpec(memory_space=pltpu.VMEM)
    return pl.pallas_call(
        functools.partial(count_kernel, nx),
        in_specs=[pl.BlockSpec(memory_space=pltpu.SMEM), vmem, vmem],
        out_shape=(shape,) * nx,
        compiler_params=params(),
        cost_estimate=cost(2 * rows * listed * NZ * nx, rows * NZ * nx * 4),
        name="counts",
    )(jnp.stack([me_z, me_x]), sample_rows.reshape(1, listed), sample_owner.reshape(1, listed))


def weigh_kernel(counts_ref, left_ref, right_ref, hi_ref, lo_ref):
    lead = jnp.concatenate([left_ref[...].astype(F32).T, right_ref[...].astype(F32).T], axis=0)
    for q in range(NZ):
        part = pl.ds(q * PANEL, PANEL)
        weighed = lead * counts_ref[q : q + 1, :]
        hi = weighed.astype(BF16)
        hi_ref[part, :] = hi
        lo_ref[part, :] = (weighed - hi.astype(F32)).astype(BF16)


def weigh(counts, left, right):
    rows = left.shape[0]
    tile = rows // 2
    out = pl.BlockSpec((NZ * PANEL, tile), lambda i: (0, i))
    shape = jax.ShapeDtypeStruct((NZ * PANEL, rows), BF16)
    return pl.pallas_call(
        weigh_kernel,
        grid=(rows // tile,),
        in_specs=[pl.BlockSpec((NZ, tile), lambda i: (0, i))] + [pl.BlockSpec((tile, PANEL // 2), lambda i: (i, 0))] * 2,
        out_specs=(out, out),
        out_shape=(shape, shape),
        compiler_params=params(),
        cost_estimate=cost(rows * PANEL * 16, rows * PANEL * 18),
        name="weigh",
    )(counts, left, right)


GRAM_TILES = 2


def gram_kernel(parts, packed, each, begun, *refs):
    refs, (acc,) = refs[:-1], refs[-1:]
    outs = refs[parts * each :]
    if begun:
        begun_ref, *outs = outs
    keep_ref, send_ref = (outs[0], outs[1]) if packed else (outs[1], outs[2])
    step = pl.program_id(0)

    @pl.when(step == 0)
    def _():
        acc[...] = begun_ref[...] if begun else jnp.zeros_like(acc)

    for p in range(parts):
        hi_ref, lo_ref, *rows_refs = refs[each * p : each * (p + 1)]

        @pl.when(step // GRAM_TILES == p)
        def _(hi_ref=hi_ref, lo_ref=lo_ref, rows_refs=rows_refs):
            rows = jnp.concatenate([ref[...] for ref in rows_refs], axis=1)
            low = jnp.dot(lo_ref[...], rows, preferred_element_type=F32)
            acc[...] += low + jnp.dot(hi_ref[...], rows, preferred_element_type=F32)

    @pl.when(step == parts * GRAM_TILES - 1)
    def _():
        half = PANEL // 2
        middle = NZ // 2 * PANEL
        if packed:
            for q in range(NZ):
                ref, place = (keep_ref, q) if q < NZ // 2 else (send_ref, q - NZ // 2)
                base, to = q * PANEL, place * 3 * half
                ref[to : to + PANEL, :] = acc[base : base + PANEL, :half]
                ref[to + PANEL : to + 3 * half, :] = acc[base + half : base + PANEL, half:]
        else:
            before_ref, rounded_ref, squares_ref = outs[0], outs[3], outs[4]
            keep_ref[...] = acc[:middle, :]
            send_ref[...] = acc[middle:, :]
            rounded = acc[PANEL:, :].astype(BF16)
            rounded_ref[...] = rounded[middle - PANEL :, :]
            ones = jnp.ones((8, rounded.shape[1]), BF16)
            squares_ref[:, :PANEL] = before_ref[:, :PANEL]
            squares_ref[:, PANEL:] = before_ref[:, PANEL:] + lax.dot_general(
                ones, rounded * rounded, (((1,), (1,)), ((), ())), preferred_element_type=F32
            )


def own_kernel(hi_ref, lo_ref, rows_ref, out_ref):
    rows = rows_ref[...]
    total = jnp.dot(lo_ref[...], rows, preferred_element_type=F32) + jnp.dot(hi_ref[...], rows, preferred_element_type=F32)

    @pl.when(pl.program_id(0) == 0)
    def _():
        out_ref[...] = total

    @pl.when(pl.program_id(0) > 0)
    def _():
        out_ref[...] += total


def own_share(weight, block):
    rows, width = block.shape
    tile = rows // GRAM_TILES
    weight_spec = pl.BlockSpec((NZ * PANEL, tile), lambda k: (0, k))
    return pl.pallas_call(
        own_kernel,
        grid=(GRAM_TILES,),
        in_specs=[weight_spec, weight_spec, pl.BlockSpec((tile, width), lambda k: (k, 0))],
        out_specs=pl.BlockSpec((NZ * PANEL, width), lambda k: (0, 0)),
        out_shape=jax.ShapeDtypeStruct((NZ * PANEL, width), F32),
        compiler_params=params(),
        cost_estimate=cost(4 * NZ * PANEL * rows * width, 4 * NZ * PANEL * (rows + width)),
        name="share",
    )(*weight, block)


def partial_grams(weights, chunk_rows, before, begun=None):
    packed = before is None
    parts = len(chunk_rows)
    rows = chunk_rows[0][0].shape[0]
    width = sum(piece.shape[1] for piece in chunk_rows[0])
    tile = rows // GRAM_TILES
    half = NZ // 2
    shape = (half * (PANEL + PANEL // 2), PANEL // 2) if packed else (half * PANEL, width)
    operands, specs = [], []
    for p, ((hi, lo), pieces) in enumerate(zip(weights, chunk_rows)):
        operands += [hi, lo, *pieces]

        def place(k, p=p):
            return jnp.clip(k - p * GRAM_TILES, 0, GRAM_TILES - 1)

        weight_spec = pl.BlockSpec((NZ * PANEL, tile), lambda k, place=place: (0, place(k)))
        specs += [weight_spec, weight_spec]
        specs += [pl.BlockSpec((tile, piece.shape[1]), lambda k, place=place: (place(k), 0)) for piece in pieces]
    each = len(operands) // parts
    out = pl.BlockSpec(shape, lambda k: (0, 0))
    out_specs = [out, out]
    out_shape = [jax.ShapeDtypeStruct(shape, F32)] * 2
    if begun is not None:
        operands.append(begun)
        specs.append(pl.BlockSpec(begun.shape, lambda k: (0, 0)))
    if not packed:
        squares = pl.BlockSpec(before.shape, lambda k: (0, 0))
        operands.append(before)
        specs.append(squares)
        out_specs += [out, squares]
        out_shape += [jax.ShapeDtypeStruct(shape, BF16), jax.ShapeDtypeStruct(before.shape, F32)]
    return pl.pallas_call(
        functools.partial(gram_kernel, parts, packed, each, begun is not None),
        grid=(parts * GRAM_TILES,),
        in_specs=specs,
        out_specs=tuple(out_specs),
        out_shape=tuple(out_shape),
        scratch_shapes=[pltpu.VMEM((NZ * PANEL, width), F32)],
        compiler_params=params(),
        cost_estimate=cost(4 * parts * NZ * PANEL * rows * width, 4 * parts * NZ * PANEL * rows + 2 * parts * rows * width),
        name="grams",
    )(*operands)


def add_kernel(keep_ref, near_ref, out_ref):
    out_ref[...] = (keep_ref[...] + near_ref[...].astype(F32)).astype(out_ref.dtype)


def far_sum(keep, near):
    rows, width = keep.shape[0] // 2, keep.shape[1]
    spec = pl.BlockSpec((rows, width), lambda i: (1, 0))
    return pl.pallas_call(
        add_kernel,
        grid=(1,),
        in_specs=[spec, spec],
        out_specs=pl.BlockSpec((rows, width), lambda i: (0, 0)),
        out_shape=jax.ShapeDtypeStruct((rows, width), near.dtype),
        compiler_params=params(),
        cost_estimate=cost(rows * width, 12 * rows * width),
        name="add",
    )(keep, near)


BAND = 64
CUT = 2
MICRO = 8


def factor_band(tile):
    row_id = lax.broadcasted_iota(jnp.int32, (BAND, 1), 0)
    for first in range(0, BAND, MICRO):
        spread = [jnp.broadcast_to(tile[:, first + t : first + t + 1], tile.shape) for t in range(MICRO)]
        for t in range(MICRO):
            j = first + t
            r = lax.rsqrt(spread[t][j : j + 1, :])
            row = tile[j : j + 1, :] * r
            below = jnp.where(row_id > j, spread[t], 0.0)
            for u in range(t + 1, MICRO):
                spread[u] = spread[u] - below * (spread[u][j : j + 1, :] * (r * r))
            tile = jnp.where(row_id == j, row, tile - below * (row * r))
    return tile


def eliminate(work, first, last):
    rb = lax.broadcasted_iota(jnp.int32, (BAND, BAND), 0)
    cb = lax.broadcasted_iota(jnp.int32, (BAND, BAND), 1)
    eye_b = (rb == cb).astype(F32)
    for k in range(first, last):
        lo, hi = k * BAND, (k + 1) * BAND
        tile = factor_band(jnp.concatenate([work[lo:hi, lo:hi], eye_b], axis=1))
        inv = jnp.where(rb >= cb, tile[:, BAND:], 0.0)
        full = jnp.dot(inv, work[lo:hi, lo:], precision=HIGHEST, preferred_element_type=F32)
        if hi < PANEL:
            panel = full[:, BAND : PANEL - lo]
            work[hi:, hi:] = work[hi:, hi:] - lax.dot_general(
                panel, full[:, BAND:], (((0,), (0,)), ((), ())), precision=HIGHEST, preferred_element_type=F32
            )
        work[lo:hi, lo:] = full


def factor_first_kernel(scale, keep_ref, near_ref, far_ref, out_ref, work):
    half = PANEL // 2
    lead = (keep_ref[...] + near_ref[...] + far_ref[...]) * scale
    ri = lax.broadcasted_iota(jnp.int32, (PANEL, PANEL), 0)
    ci = lax.broadcasted_iota(jnp.int32, (PANEL, PANEL), 1)
    eye = (ri == ci).astype(F32)
    work[:, PANEL:] = eye
    work[:half, :half] = lead[:half, :] + 0.5 * eye[:half, :half]
    work[:half, half:PANEL] = lead[half:PANEL, :].T
    work[half:, :half] = lead[half:PANEL, :]
    work[half:, half:PANEL] = lead[PANEL:, :] + 0.5 * eye[:half, :half]
    eliminate(work, 0, CUT)
    out_ref[...] = work[...]


def factor_last_kernel(in_ref, squares_ref, out_ref, inverse_ref, guard_ref, work):
    work[...] = in_ref[...]
    eliminate(work, CUT, PANEL // BAND)
    ri = lax.broadcasted_iota(jnp.int32, (PANEL, PANEL), 0)
    ci = lax.broadcasted_iota(jnp.int32, (PANEL, PANEL), 1)
    upper = jnp.where(ci >= ri, work[:, :PANEL], 0.0)
    inverse = jnp.where(ri >= ci, work[:, PANEL:], 0.0)
    out_ref[...] = upper
    inverse_ref[...] = inverse
    guard_ref[:, : NZ * PANEL] = squares_ref[...]
    for place, part in enumerate((inverse, upper)):
        start = (NZ + place) * PANEL
        norms = jnp.sum(part * part, axis=0, keepdims=True)
        guard_ref[:, start : start + PANEL] = jnp.broadcast_to(norms, (8, PANEL))


def factor_first(keep, near, far, scale):
    spec = pl.BlockSpec(far.shape, lambda i: (0, 0))
    shape = (PANEL, 2 * PANEL)
    return pl.pallas_call(
        functools.partial(factor_first_kernel, scale),
        grid=(1,),
        in_specs=[spec, spec, spec],
        out_specs=pl.BlockSpec(shape, lambda i: (0, 0)),
        out_shape=jax.ShapeDtypeStruct(shape, F32),
        scratch_shapes=[pltpu.VMEM(shape, F32)],
        compiler_params=params(),
        cost_estimate=cost(10_000_000_000, 1 << 20),
        name="factor_first",
    )(keep, near, far)


def factor_last(state, squares, columns):
    def resident(shape):
        return pl.BlockSpec(shape, lambda i: (0, 0))

    square, guard = (PANEL, PANEL), (8, (NZ + 2) * PANEL)
    return pl.pallas_call(
        factor_last_kernel,
        grid=(1,),
        in_specs=[resident(state.shape), resident(squares.shape)],
        out_specs=(resident(square), resident(square), resident(guard)),
        out_shape=(
            jax.ShapeDtypeStruct((PANEL, columns), F32),
            jax.ShapeDtypeStruct(square, F32),
            jax.ShapeDtypeStruct(guard, F32),
        ),
        scratch_shapes=[pltpu.VMEM(state.shape, F32)],
        compiler_params=params(),
        cost_estimate=cost(10_000_000_000, 1 << 20),
        name="factor_last",
    )(state, squares)


def couple_kernel(scale, inverse_ref, keep_ref, near_ref, far_ref, whole_ref, out_ref):
    gram = (keep_ref[...] + near_ref[...].astype(F32) + far_ref[...].astype(F32)) * scale
    out_ref[...] = jnp.dot(inverse_ref[...], gram, precision=HIGHEST, preferred_element_type=F32)


def couple(inverse, keep, near, far, whole, start, scale):
    rows, width = far.shape
    block = start // width
    spec = pl.BlockSpec((rows, width), lambda i: (0, 0))
    return pl.pallas_call(
        functools.partial(couple_kernel, scale),
        grid=(1,),
        in_specs=[pl.BlockSpec(inverse.shape, lambda i: (0, 0)), spec, spec, spec, pl.BlockSpec(memory_space=pl.ANY)],
        out_specs=pl.BlockSpec((rows, width), lambda i: (0, block)),
        out_shape=jax.ShapeDtypeStruct(whole.shape, F32),
        input_output_aliases={4: 0},
        compiler_params=params(),
        cost_estimate=cost(12 * PANEL * rows * width, 20 * rows * width),
        name="couple",
    )(inverse, keep, near, far, whole)


ROUNDING = 0.6 * 2.0**-8
LIMIT = 0.004


def judge_kernel(scale, *refs):
    *guard_refs, out_ref, guards, sems = refs
    copies = [pltpu.make_async_copy(ref, guards.at[k], sems.at[k]) for k, ref in enumerate(guard_refs)]
    for copy in copies:
        copy.start()
    for copy in copies:
        copy.wait()
    worst = jnp.zeros((8, 1), F32)
    for owner in range(NZ):
        terms = []
        for sender in range(NZ):
            apart = owner ^ sender
            place = relative_owner(apart) * PANEL
            terms.append(guards[sender, :, place : place + PANEL] * float(apart))
        total = (terms[0] + terms[1]) + (terms[2] + terms[3])
        inverse_norms = guards[owner, :, NZ * PANEL : (NZ + 1) * PANEL]
        upper_norms = guards[owner, :, (NZ + 1) * PANEL :]
        error = jnp.sum(inverse_norms * total, axis=1, keepdims=True) * (ROUNDING * scale) ** 2
        size = jnp.sum(upper_norms, axis=1, keepdims=True) * LIMIT**2
        worst = jnp.maximum(worst, jnp.where(error <= size, 0.0, 1.0))
    out_ref[0] = jnp.max(worst).astype(jnp.int32)


def judge(guards, scale):
    return pl.pallas_call(
        functools.partial(judge_kernel, scale),
        in_specs=[pl.BlockSpec(memory_space=pltpu.HBM)] * NZ,
        out_specs=pl.BlockSpec(memory_space=pltpu.SMEM),
        out_shape=jax.ShapeDtypeStruct((1,), jnp.int32),
        scratch_shapes=[pltpu.VMEM((NZ,) + guards[0].shape, F32), pltpu.SemaphoreType.DMA((NZ,))],
        name="judge",
    )(*guards)


def per_device(flux_rows, row_signs, sample_rows, sample_owner):
    wide, blk = lax.axis_size("wide"), lax.axis_size("blk")
    nx = blk // NZ
    rows, columns = flux_rows.shape
    scale = 1.0 / sample_rows.shape[0]
    me_w, me_b = lax.axis_index("wide"), lax.axis_index("blk")
    me_x, me_z = me_b & (nx - 1), me_b >> (nx.bit_length() - 1)
    had = hadamard_pair()
    signs = row_signs.reshape(1, rows)
    levels = wide.bit_length() - 1

    def at(z, x):
        return z * nx + x

    def z_route(mask):
        return [(at(z, x), at(z ^ mask, x)) for z in range(NZ) for x in range(nx)]

    def x_shift(s):
        return [(at(z, x), at(z, (x + s) % nx)) for z in range(NZ) for x in range(nx)]

    def level_sign(level):
        return jnp.where((me_w >> level) & 1 == 1, -1.0, 1.0).astype(F32)

    def last_level(own, start, whole):
        partner = lax.ppermute(own, "wide", [(w, w ^ (wide // 2)) for w in range(wide)])
        own, whole = join_last(own, partner, level_sign(levels - 1), start, columns, whole)
        pieces = [own]
        for s in range(1, nx):
            pieces.append(lax.ppermute(own, "blk", x_shift(s)))
        return pieces, whole

    def level_up(level, own, partner):
        total = (partner.astype(F32) + own.astype(F32) * level_sign(level)) * SQRT_HALF
        return total.astype(BF16)

    def first_levels(mixed, last=levels - 1):
        for level in range(last):
            partner = lax.ppermute(mixed, "wide", [(w, w ^ (1 << level)) for w in range(wide)])
            mixed = level_up(level, mixed, partner)
        return mixed

    def cut_lead(mixed):
        mixed = first_levels(mixed, levels - 2)
        partner = lax.ppermute(mixed, "wide", [(w, w ^ (1 << (levels - 2))) for w in range(wide)])
        cuts = [slice(start, start + PIECE) for start in range(0, PANEL, PIECE)]
        return [level_up(levels - 2, mixed[:, cut], partner[:, cut]) for cut in cuts]

    blocks = [(start, PANEL) for start in range(0, columns, PANEL)]
    mixed = [*mix_columns(signs, had, flux_rows, blocks[:1])]
    counts = count_samples(sample_rows, sample_owner, nx, rows, me_z, me_x)
    owner_counts = [counts[0]]
    for s in range(1, nx):
        owner_counts.append(lax.ppermute(counts[s], "blk", x_shift(s)))
    mixed += mix_columns(signs, had, flux_rows, blocks[1:])
    pieces, whole, place = [], None, 0
    for piece in cut_lead(mixed[0]) + [first_levels(block) for block in mixed[1:]]:
        piece, whole = last_level(piece, place, whole)
        place += piece[0].shape[1]
        pieces.append(piece)
    groups = [[[pieces[0][p], pieces[1][p]] for p in range(nx)]] + [[[piece[p]] for p in range(nx)] for piece in pieces[2:]]

    weights, grams, precise = [], [], []
    squares = jnp.zeros((8, NZ * PANEL), F32)
    for i, sources in enumerate(groups):
        if i == 0:
            for p in range(nx):
                weights.append(weigh(owner_counts[p], *sources[p]))
        begun, first = None, 0
        if 0 < i < len(groups) - 1:
            begun, first = own_share(weights[0], sources[0][0]), 1
        if i == 0:
            keep, send = partial_grams(weights, sources, None)
        else:
            keep, exact_send, send, squares = partial_grams(weights[first:], sources[first:], squares, begun)
            precise.append((keep, exact_send))
        near = lax.ppermute(send, "blk", z_route(1))
        onward = far_sum(keep, near)
        far = lax.ppermute(onward, "blk", z_route(2))
        grams.append((keep, near, far))
    state = factor_first(*grams[0], scale)
    sketch, inverse, guard = factor_last(state, squares, columns)
    guards = [guard]
    for mask in range(1, NZ):
        guards.append(lax.ppermute(guard, "blk", z_route(mask)))
    redo = judge(guards, scale)[0] != 0
    for i in range(1, len(groups) - 1):
        sketch = couple(inverse, *grams[i], sketch, i * PANEL, scale)

    def rounded(sketch, inverse, last, precise):
        return couple(inverse, *last, sketch, columns - PANEL, scale)

    def exact(sketch, inverse, last, precise):
        for i, (keep, send) in enumerate(precise):
            near = lax.ppermute(send, "blk", z_route(1))
            far = lax.ppermute(far_sum(keep, near), "blk", z_route(2))
            sketch = couple(inverse, keep, near, far, sketch, (i + 1) * PANEL, scale)
        return sketch

    sketch = lax.cond(redo, exact, rounded, sketch, inverse, grams[-1], precise)
    return whole, sketch


def solution(mesh):
    placed = (
        P(("wide", "blk"), None),
        P(("wide", "blk")),
        P(("wide", "blk")),
        P(("wide", "blk"), None),
    )

    return jax.shard_map(
        per_device,
        mesh=mesh,
        in_specs=placed,
        out_specs=(P(("wide", "blk"), None), P(("wide", "blk"), None)),
        check_vma=False,
    )
```

```python
import functools

import jax
import jax.numpy as jnp
import numpy as np
from jax import lax
from jax.experimental import pallas as pl
from jax.experimental.pallas import tpu as pltpu
from jax.sharding import PartitionSpec as P

PANEL = 256
HB = 128
NZ = 4
PIECE = 128
SQRT_HALF = 0.7071067811865476
HIGHEST = lax.Precision.HIGHEST
F32 = jnp.float32
BF16 = jnp.bfloat16


def hadamard_pair():
    idx = np.arange(HB)
    common = idx[:, None] & idx[None, :]
    parity = np.zeros_like(common)
    for bit in range(HB.bit_length() - 1):
        parity ^= (common >> bit) & 1
    one = 1.0 - 2.0 * parity
    return jnp.asarray(np.kron(np.eye(2), one), BF16)


VMEM_LIMIT = 24 << 20


def params(**kw):
    return pltpu.CompilerParams(vmem_limit_bytes=VMEM_LIMIT, **kw)


def cost(flops, moved):
    return pl.CostEstimate(flops=flops, bytes_accessed=moved, transcendentals=0)


def mix_kernel(signs_ref, had_ref, x_ref, *out_refs):
    rows = x_ref.shape[0]
    size = had_ref.shape[0]
    for which, out_ref in enumerate(out_refs):

        @pl.when(pl.program_id(0) == which)
        def _(out_ref=out_ref):
            for b in range(rows // size):
                part = pl.ds(b * size, size)
                signed = (had_ref[...].astype(F32) * signs_ref[:, b * size : (b + 1) * size].astype(F32)).astype(BF16)
                x = x_ref[part, :]
                hi = x.astype(BF16)
                rest = x - hi.astype(F32)
                mid = rest.astype(BF16)
                low = (rest - mid.astype(F32)).astype(BF16)
                total = jnp.dot(signed, low, preferred_element_type=F32)
                total = total + jnp.dot(signed, mid, preferred_element_type=F32)
                total = total + jnp.dot(signed, hi, preferred_element_type=F32)
                out_ref[part, :] = (total * (HB**-0.5)).astype(BF16)


def mix_columns(signs, had, flux, chunks):
    rows = flux.shape[0]
    start, width = chunks[0]
    first, count = start // width, len(chunks)
    return pl.pallas_call(
        mix_kernel,
        grid=(count,),
        in_specs=[
            pl.BlockSpec((1, rows), lambda i: (0, 0)),
            pl.BlockSpec(had.shape, lambda i: (0, 0)),
            pl.BlockSpec((rows, width), lambda i: (0, i + first)),
        ],
        out_specs=(pl.BlockSpec((rows, width), lambda i: (0, 0)),) * count,
        out_shape=(jax.ShapeDtypeStruct((rows, width), BF16),) * count,
        cost_estimate=cost(2 * count * rows * width * had.shape[0] * 3, count * rows * width * 6),
        name="mix",
    )(signs, had, flux)


def join_kernel(sign_ref, own_ref, other_ref, *refs):
    total = (other_ref[...].astype(F32) + own_ref[...].astype(F32) * sign_ref[0]) * SQRT_HALF
    total = total.astype(BF16)
    for ref in refs[-2:]:
        ref[...] = total


def join_last(own, other, sign, start, columns, whole):
    rows, width = own.shape
    block = start // width
    tile = rows // 2
    chunk = pl.BlockSpec((tile, width), lambda i: (i, 0))
    operands, specs, alias = [sign.reshape(1), own, other], [pl.BlockSpec(memory_space=pltpu.SMEM), chunk, chunk], {}
    if whole is not None:
        operands.append(whole)
        specs.append(pl.BlockSpec(memory_space=pl.ANY))
        alias = {3: 1}
    return pl.pallas_call(
        join_kernel,
        grid=(rows // tile,),
        in_specs=specs,
        out_specs=(chunk, pl.BlockSpec((tile, width), lambda i: (i, block))),
        out_shape=(jax.ShapeDtypeStruct((rows, width), BF16), jax.ShapeDtypeStruct((rows, columns), BF16)),
        input_output_aliases=alias,
        compiler_params=params(),
        cost_estimate=cost(4 * rows * width, 8 * rows * width),
        name="join",
    )(*operands)


def relative_owner(q):
    return ((q & 1) << 1) | (q >> 1)


def count_kernel(nx, me_ref, rows_ref, owner_ref, *out_refs):
    listed = rows_ref.shape[1]
    rows = out_refs[0].shape[1]
    me_z, me_x = me_ref[0], me_ref[1]
    index = lax.broadcasted_iota(jnp.int32, (NZ * nx, listed), 0)
    q, s = index & (NZ - 1), index >> (NZ.bit_length() - 1)
    z = me_z ^ relative_owner(q)
    x = (me_x + s) & (nx - 1)
    by_owner = (z * nx + x == owner_ref[...]).astype(F32).astype(BF16)
    by_row = (lax.broadcasted_iota(jnp.int32, (rows, listed), 0) == rows_ref[...]).astype(F32).astype(BF16)
    total = lax.dot_general(by_owner, by_row, (((1,), (1,)), ((), ())), preferred_element_type=F32)
    for shift, ref in enumerate(out_refs):
        ref[...] = total[shift * NZ : (shift + 1) * NZ, :]


def count_samples(sample_rows, sample_owner, nx, rows, me_z, me_x):
    listed = sample_rows.shape[0]
    shape = jax.ShapeDtypeStruct((NZ, rows), F32)
    vmem = pl.BlockSpec(memory_space=pltpu.VMEM)
    return pl.pallas_call(
        functools.partial(count_kernel, nx),
        in_specs=[pl.BlockSpec(memory_space=pltpu.SMEM), vmem, vmem],
        out_shape=(shape,) * nx,
        compiler_params=params(),
        cost_estimate=cost(2 * rows * listed * NZ * nx, rows * NZ * nx * 4),
        name="counts",
    )(jnp.stack([me_z, me_x]), sample_rows.reshape(1, listed), sample_owner.reshape(1, listed))


def weigh_kernel(counts_ref, left_ref, right_ref, hi_ref, lo_ref):
    lead = jnp.concatenate([left_ref[...].astype(F32).T, right_ref[...].astype(F32).T], axis=0)
    for q in range(NZ):
        part = pl.ds(q * PANEL, PANEL)
        weighed = lead * counts_ref[q : q + 1, :]
        hi = weighed.astype(BF16)
        hi_ref[part, :] = hi
        lo_ref[part, :] = (weighed - hi.astype(F32)).astype(BF16)


def weigh(counts, left, right):
    rows = left.shape[0]
    tile = rows // 2
    out = pl.BlockSpec((NZ * PANEL, tile), lambda i: (0, i))
    shape = jax.ShapeDtypeStruct((NZ * PANEL, rows), BF16)
    return pl.pallas_call(
        weigh_kernel,
        grid=(rows // tile,),
        in_specs=[pl.BlockSpec((NZ, tile), lambda i: (0, i))] + [pl.BlockSpec((tile, PANEL // 2), lambda i: (i, 0))] * 2,
        out_specs=(out, out),
        out_shape=(shape, shape),
        compiler_params=params(),
        cost_estimate=cost(rows * PANEL * 16, rows * PANEL * 18),
        name="weigh",
    )(counts, left, right)


GRAM_TILES = 2


def gram_kernel(parts, packed, each, begun, *refs):
    refs, (acc,) = refs[:-1], refs[-1:]
    outs = refs[parts * each :]
    if begun:
        begun_ref, *outs = outs
    keep_ref, send_ref = (outs[0], outs[1]) if packed else (outs[1], outs[2])
    step = pl.program_id(0)

    @pl.when(step == 0)
    def _():
        acc[...] = begun_ref[...] if begun else jnp.zeros_like(acc)

    for p in range(parts):
        hi_ref, lo_ref, *rows_refs = refs[each * p : each * (p + 1)]

        @pl.when(step // GRAM_TILES == p)
        def _(hi_ref=hi_ref, lo_ref=lo_ref, rows_refs=rows_refs):
            rows = jnp.concatenate([ref[...] for ref in rows_refs], axis=1)
            low = jnp.dot(lo_ref[...], rows, preferred_element_type=F32)
            acc[...] += low + jnp.dot(hi_ref[...], rows, preferred_element_type=F32)

    @pl.when(step == parts * GRAM_TILES - 1)
    def _():
        half = PANEL // 2
        middle = NZ // 2 * PANEL
        if packed:
            for q in range(NZ):
                ref, place = (keep_ref, q) if q < NZ // 2 else (send_ref, q - NZ // 2)
                base, to = q * PANEL, place * 3 * half
                ref[to : to + PANEL, :] = acc[base : base + PANEL, :half]
                ref[to + PANEL : to + 3 * half, :] = acc[base + half : base + PANEL, half:]
        else:
            before_ref, rounded_ref, squares_ref = outs[0], outs[3], outs[4]
            keep_ref[...] = acc[:middle, :]
            send_ref[...] = acc[middle:, :]
            rounded = acc[PANEL:, :].astype(BF16)
            rounded_ref[...] = rounded[middle - PANEL :, :]
            ones = jnp.ones((8, rounded.shape[1]), BF16)
            squares_ref[:, :PANEL] = before_ref[:, :PANEL]
            squares_ref[:, PANEL:] = before_ref[:, PANEL:] + lax.dot_general(
                ones, rounded * rounded, (((1,), (1,)), ((), ())), preferred_element_type=F32
            )


def own_kernel(hi_ref, lo_ref, rows_ref, out_ref):
    rows = rows_ref[...]
    total = jnp.dot(lo_ref[...], rows, preferred_element_type=F32) + jnp.dot(hi_ref[...], rows, preferred_element_type=F32)

    @pl.when(pl.program_id(0) == 0)
    def _():
        out_ref[...] = total

    @pl.when(pl.program_id(0) > 0)
    def _():
        out_ref[...] += total


def own_share(weight, block):
    rows, width = block.shape
    tile = rows // GRAM_TILES
    weight_spec = pl.BlockSpec((NZ * PANEL, tile), lambda k: (0, k))
    return pl.pallas_call(
        own_kernel,
        grid=(GRAM_TILES,),
        in_specs=[weight_spec, weight_spec, pl.BlockSpec((tile, width), lambda k: (k, 0))],
        out_specs=pl.BlockSpec((NZ * PANEL, width), lambda k: (0, 0)),
        out_shape=jax.ShapeDtypeStruct((NZ * PANEL, width), F32),
        compiler_params=params(),
        cost_estimate=cost(4 * NZ * PANEL * rows * width, 4 * NZ * PANEL * (rows + width)),
        name="share",
    )(*weight, block)


def partial_grams(weights, chunk_rows, before, begun=None):
    packed = before is None
    parts = len(chunk_rows)
    rows = chunk_rows[0][0].shape[0]
    width = sum(piece.shape[1] for piece in chunk_rows[0])
    tile = rows // GRAM_TILES
    half = NZ // 2
    shape = (half * (PANEL + PANEL // 2), PANEL // 2) if packed else (half * PANEL, width)
    operands, specs = [], []
    for p, ((hi, lo), pieces) in enumerate(zip(weights, chunk_rows)):
        operands += [hi, lo, *pieces]

        def place(k, p=p):
            return jnp.clip(k - p * GRAM_TILES, 0, GRAM_TILES - 1)

        weight_spec = pl.BlockSpec((NZ * PANEL, tile), lambda k, place=place: (0, place(k)))
        specs += [weight_spec, weight_spec]
        specs += [pl.BlockSpec((tile, piece.shape[1]), lambda k, place=place: (place(k), 0)) for piece in pieces]
    each = len(operands) // parts
    out = pl.BlockSpec(shape, lambda k: (0, 0))
    out_specs = [out, out]
    out_shape = [jax.ShapeDtypeStruct(shape, F32)] * 2
    if begun is not None:
        operands.append(begun)
        specs.append(pl.BlockSpec(begun.shape, lambda k: (0, 0)))
    if not packed:
        squares = pl.BlockSpec(before.shape, lambda k: (0, 0))
        operands.append(before)
        specs.append(squares)
        out_specs += [out, squares]
        out_shape += [jax.ShapeDtypeStruct(shape, BF16), jax.ShapeDtypeStruct(before.shape, F32)]
    return pl.pallas_call(
        functools.partial(gram_kernel, parts, packed, each, begun is not None),
        grid=(parts * GRAM_TILES,),
        in_specs=specs,
        out_specs=tuple(out_specs),
        out_shape=tuple(out_shape),
        scratch_shapes=[pltpu.VMEM((NZ * PANEL, width), F32)],
        compiler_params=params(),
        cost_estimate=cost(4 * parts * NZ * PANEL * rows * width, 4 * parts * NZ * PANEL * rows + 2 * parts * rows * width),
        name="grams",
    )(*operands)


def add_kernel(keep_ref, near_ref, out_ref):
    out_ref[...] = (keep_ref[...] + near_ref[...].astype(F32)).astype(out_ref.dtype)


def far_sum(keep, near):
    rows, width = keep.shape[0] // 2, keep.shape[1]
    spec = pl.BlockSpec((rows, width), lambda i: (1, 0))
    return pl.pallas_call(
        add_kernel,
        grid=(1,),
        in_specs=[spec, spec],
        out_specs=pl.BlockSpec((rows, width), lambda i: (0, 0)),
        out_shape=jax.ShapeDtypeStruct((rows, width), near.dtype),
        compiler_params=params(),
        cost_estimate=cost(rows * width, 12 * rows * width),
        name="add",
    )(keep, near)


BAND = 64
CUT = 2
MICRO = 8


def factor_band(tile):
    row_id = lax.broadcasted_iota(jnp.int32, (BAND, 1), 0)
    for first in range(0, BAND, MICRO):
        spread = [jnp.broadcast_to(tile[:, first + t : first + t + 1], tile.shape) for t in range(MICRO)]
        for t in range(MICRO):
            j = first + t
            r = lax.rsqrt(spread[t][j : j + 1, :])
            row = tile[j : j + 1, :] * r
            below = jnp.where(row_id > j, spread[t], 0.0)
            for u in range(t + 1, MICRO):
                spread[u] = spread[u] - below * (spread[u][j : j + 1, :] * (r * r))
            tile = jnp.where(row_id == j, row, tile - below * (row * r))
    return tile


def eliminate(work, first, last):
    rb = lax.broadcasted_iota(jnp.int32, (BAND, BAND), 0)
    cb = lax.broadcasted_iota(jnp.int32, (BAND, BAND), 1)
    eye_b = (rb == cb).astype(F32)
    for k in range(first, last):
        lo, hi = k * BAND, (k + 1) * BAND
        tile = factor_band(jnp.concatenate([work[lo:hi, lo:hi], eye_b], axis=1))
        inv = jnp.where(rb >= cb, tile[:, BAND:], 0.0)
        full = jnp.dot(inv, work[lo:hi, lo:], precision=HIGHEST, preferred_element_type=F32)
        if hi < PANEL:
            panel = full[:, BAND : PANEL - lo]
            work[hi:, hi:] = work[hi:, hi:] - lax.dot_general(
                panel, full[:, BAND:], (((0,), (0,)), ((), ())), precision=HIGHEST, preferred_element_type=F32
            )
        work[lo:hi, lo:] = full


def factor_first_kernel(scale, keep_ref, near_ref, far_ref, out_ref, work):
    half = PANEL // 2
    lead = (keep_ref[...] + near_ref[...] + far_ref[...]) * scale
    ri = lax.broadcasted_iota(jnp.int32, (PANEL, PANEL), 0)
    ci = lax.broadcasted_iota(jnp.int32, (PANEL, PANEL), 1)
    eye = (ri == ci).astype(F32)
    work[:, PANEL:] = eye
    work[:half, :half] = lead[:half, :] + 0.5 * eye[:half, :half]
    work[:half, half:PANEL] = lead[half:PANEL, :].T
    work[half:, :half] = lead[half:PANEL, :]
    work[half:, half:PANEL] = lead[PANEL:, :] + 0.5 * eye[:half, :half]
    eliminate(work, 0, CUT)
    out_ref[...] = work[...]


def factor_last_kernel(in_ref, squares_ref, out_ref, inverse_ref, guard_ref, work):
    work[...] = in_ref[...]
    eliminate(work, CUT, PANEL // BAND)
    ri = lax.broadcasted_iota(jnp.int32, (PANEL, PANEL), 0)
    ci = lax.broadcasted_iota(jnp.int32, (PANEL, PANEL), 1)
    upper = jnp.where(ci >= ri, work[:, :PANEL], 0.0)
    inverse = jnp.where(ri >= ci, work[:, PANEL:], 0.0)
    out_ref[...] = upper
    inverse_ref[...] = inverse
    guard_ref[:, : NZ * PANEL] = squares_ref[:1, :]
    for place, part in enumerate((inverse, upper)):
        start = (NZ + place) * PANEL
        guard_ref[:, start : start + PANEL] = jnp.sum(part * part, axis=0, keepdims=True)


def factor_first(keep, near, far, scale):
    spec = pl.BlockSpec(far.shape, lambda i: (0, 0))
    shape = (PANEL, 2 * PANEL)
    return pl.pallas_call(
        functools.partial(factor_first_kernel, scale),
        grid=(1,),
        in_specs=[spec, spec, spec],
        out_specs=pl.BlockSpec(shape, lambda i: (0, 0)),
        out_shape=jax.ShapeDtypeStruct(shape, F32),
        scratch_shapes=[pltpu.VMEM(shape, F32)],
        compiler_params=params(),
        cost_estimate=cost(10_000_000_000, 1 << 20),
        name="factor_first",
    )(keep, near, far)


def factor_last(state, squares, columns):
    def resident(shape):
        return pl.BlockSpec(shape, lambda i: (0, 0))

    square, guard = (PANEL, PANEL), (1, (NZ + 2) * PANEL)
    return pl.pallas_call(
        factor_last_kernel,
        grid=(1,),
        in_specs=[resident(state.shape), resident(squares.shape)],
        out_specs=(resident(square), resident(square), resident(guard)),
        out_shape=(
            jax.ShapeDtypeStruct((PANEL, columns), F32),
            jax.ShapeDtypeStruct(square, F32),
            jax.ShapeDtypeStruct(guard, F32),
        ),
        scratch_shapes=[pltpu.VMEM(state.shape, F32)],
        compiler_params=params(),
        cost_estimate=cost(10_000_000_000, 1 << 20),
        name="factor_last",
    )(state, squares)


def couple_kernel(scale, inverse_ref, keep_ref, near_ref, far_ref, whole_ref, out_ref):
    gram = (keep_ref[...] + near_ref[...].astype(F32) + far_ref[...].astype(F32)) * scale
    out_ref[...] = jnp.dot(inverse_ref[...], gram, precision=HIGHEST, preferred_element_type=F32)


def couple(inverse, keep, near, far, whole, start, scale):
    rows, width = far.shape
    block = start // width
    spec = pl.BlockSpec((rows, width), lambda i: (0, 0))
    return pl.pallas_call(
        functools.partial(couple_kernel, scale),
        grid=(1,),
        in_specs=[pl.BlockSpec(inverse.shape, lambda i: (0, 0)), spec, spec, spec, pl.BlockSpec(memory_space=pl.ANY)],
        out_specs=pl.BlockSpec((rows, width), lambda i: (0, block)),
        out_shape=jax.ShapeDtypeStruct(whole.shape, F32),
        input_output_aliases={4: 0},
        compiler_params=params(),
        cost_estimate=cost(12 * PANEL * rows * width, 20 * rows * width),
        name="couple",
    )(inverse, keep, near, far, whole)


ROUNDING = 0.6 * 2.0**-8
LIMIT = 0.004


def judge_kernel(scale, *refs):
    *guard_refs, out_ref, guards, sems = refs
    copies = [pltpu.make_async_copy(ref, guards.at[k], sems.at[k]) for k, ref in enumerate(guard_refs)]
    for copy in copies:
        copy.start()
    for copy in copies:
        copy.wait()
    worst = jnp.zeros((1, 1), F32)
    for owner in range(NZ):
        terms = []
        for sender in range(NZ):
            apart = owner ^ sender
            place = relative_owner(apart) * PANEL
            terms.append(guards[sender, :, place : place + PANEL] * float(apart))
        total = (terms[0] + terms[1]) + (terms[2] + terms[3])
        inverse_norms = guards[owner, :, NZ * PANEL : (NZ + 1) * PANEL]
        upper_norms = guards[owner, :, (NZ + 1) * PANEL :]
        error = jnp.sum(inverse_norms * total, axis=1, keepdims=True) * (ROUNDING * scale) ** 2
        size = jnp.sum(upper_norms, axis=1, keepdims=True) * LIMIT**2
        worst = jnp.maximum(worst, jnp.where(error <= size, 0.0, 1.0))
    out_ref[0] = jnp.max(worst).astype(jnp.int32)


def judge(guards, scale):
    return pl.pallas_call(
        functools.partial(judge_kernel, scale),
        in_specs=[pl.BlockSpec(memory_space=pltpu.HBM)] * NZ,
        out_specs=pl.BlockSpec(memory_space=pltpu.SMEM),
        out_shape=jax.ShapeDtypeStruct((1,), jnp.int32),
        scratch_shapes=[pltpu.VMEM((NZ,) + guards[0].shape, F32), pltpu.SemaphoreType.DMA((NZ,))],
        name="judge",
    )(*guards)


def per_device(flux_rows, row_signs, sample_rows, sample_owner):
    wide, blk = lax.axis_size("wide"), lax.axis_size("blk")
    nx = blk // NZ
    rows, columns = flux_rows.shape
    scale = 1.0 / sample_rows.shape[0]
    me_w, me_b = lax.axis_index("wide"), lax.axis_index("blk")
    me_x, me_z = me_b & (nx - 1), me_b >> (nx.bit_length() - 1)
    had = hadamard_pair()
    signs = row_signs.reshape(1, rows)
    levels = wide.bit_length() - 1

    def at(z, x):
        return z * nx + x

    def z_route(mask):
        return [(at(z, x), at(z ^ mask, x)) for z in range(NZ) for x in range(nx)]

    def x_shift(s):
        return [(at(z, x), at(z, (x + s) % nx)) for z in range(NZ) for x in range(nx)]

    def level_sign(level):
        return jnp.where((me_w >> level) & 1 == 1, -1.0, 1.0).astype(F32)

    def last_level(own, start, whole):
        partner = lax.ppermute(own, "wide", [(w, w ^ (wide // 2)) for w in range(wide)])
        own, whole = join_last(own, partner, level_sign(levels - 1), start, columns, whole)
        pieces = [own]
        for s in range(1, nx):
            pieces.append(lax.ppermute(own, "blk", x_shift(s)))
        return pieces, whole

    def level_up(level, own, partner):
        total = (partner.astype(F32) + own.astype(F32) * level_sign(level)) * SQRT_HALF
        return total.astype(BF16)

    def first_levels(mixed, last=levels - 1):
        for level in range(last):
            partner = lax.ppermute(mixed, "wide", [(w, w ^ (1 << level)) for w in range(wide)])
            mixed = level_up(level, mixed, partner)
        return mixed

    def cut_lead(mixed):
        mixed = first_levels(mixed, levels - 2)
        partner = lax.ppermute(mixed, "wide", [(w, w ^ (1 << (levels - 2))) for w in range(wide)])
        cuts = [slice(start, start + PIECE) for start in range(0, PANEL, PIECE)]
        return [level_up(levels - 2, mixed[:, cut], partner[:, cut]) for cut in cuts]

    blocks = [(start, PANEL) for start in range(0, columns, PANEL)]
    mixed = [*mix_columns(signs, had, flux_rows, blocks[:1])]
    counts = count_samples(sample_rows, sample_owner, nx, rows, me_z, me_x)
    owner_counts = [counts[0]]
    for s in range(1, nx):
        owner_counts.append(lax.ppermute(counts[s], "blk", x_shift(s)))
    mixed += mix_columns(signs, had, flux_rows, blocks[1:])
    pieces, whole, place = [], None, 0
    for piece in cut_lead(mixed[0]) + [first_levels(block) for block in mixed[1:]]:
        piece, whole = last_level(piece, place, whole)
        place += piece[0].shape[1]
        pieces.append(piece)
    groups = [[[pieces[0][p], pieces[1][p]] for p in range(nx)]] + [[[piece[p]] for p in range(nx)] for piece in pieces[2:]]

    weights, grams, precise = [], [], []
    squares = jnp.zeros((8, NZ * PANEL), F32)
    for i, sources in enumerate(groups):
        if i == 0:
            for p in range(nx):
                weights.append(weigh(owner_counts[p], *sources[p]))
        begun, first = None, 0
        if 0 < i < len(groups) - 1:
            begun, first = own_share(weights[0], sources[0][0]), 1
        if i == 0:
            keep, send = partial_grams(weights, sources, None)
        else:
            keep, exact_send, send, squares = partial_grams(weights[first:], sources[first:], squares, begun)
            precise.append((keep, exact_send))
        near = lax.ppermute(send, "blk", z_route(1))
        onward = far_sum(keep, near)
        far = lax.ppermute(onward, "blk", z_route(2))
        grams.append((keep, near, far))
    state = factor_first(*grams[0], scale)
    sketch, inverse, guard = factor_last(state, squares, columns)
    guards = [guard]
    for mask in range(1, NZ):
        guards.append(lax.ppermute(guard, "blk", z_route(mask)))
    redo = judge(guards, scale)[0] != 0
    for i in range(1, len(groups) - 1):
        sketch = couple(inverse, *grams[i], sketch, i * PANEL, scale)

    def rounded(sketch, inverse, last, precise):
        return couple(inverse, *last, sketch, columns - PANEL, scale)

    def exact(sketch, inverse, last, precise):
        for i, (keep, send) in enumerate(precise):
            near = lax.ppermute(send, "blk", z_route(1))
            far = lax.ppermute(far_sum(keep, near), "blk", z_route(2))
            sketch = couple(inverse, keep, near, far, sketch, (i + 1) * PANEL, scale)
        return sketch

    sketch = lax.cond(redo, exact, rounded, sketch, inverse, grams[-1], precise)
    return whole, sketch


def solution(mesh):
    placed = (
        P(("wide", "blk"), None),
        P(("wide", "blk")),
        P(("wide", "blk")),
        P(("wide", "blk"), None),
    )

    return jax.shard_map(
        per_device,
        mesh=mesh,
        in_specs=placed,
        out_specs=(P(("wide", "blk"), None), P(("wide", "blk"), None)),
        check_vma=False,
    )
```
